32 devices in a mesh: dp: 4 (over z), expert: 8 (over y, x, core).
Axes of the slice: x: 2, y: 2, z: 4, core: 2. Of those that a mesh axis runs over, the one named last changes fastest.
Arguments:
- layer_input: bfloat16 [4096, 1024], P(('dp', 'expert')), may hold values from -6 to 6
- segment_ids: int32 [4096], P(('dp', 'expert')), may hold values from 0 to 127, never falling along the last dimension, each value on 1 to 64 neighbouring positions
- expert_routes: int32 [4096, 8], P(('dp', 'expert')), may hold values from 0 to 31, all different within a row; in each aligned block of 128 rows (0 to 127, 128 to 255, ...) at most 40 rows name the same one
- first_gain: float32 [1024], replicated, may hold values from 0.5 to 1.5
- w_query: bfloat16 [1024, 1024], P('dp'), may hold values from -0.1875 to 0.1875
- w_keyvalue: bfloat16 [1024, 1024], P('dp'), may hold values from -0.1875 to 0.1875
- w_output: bfloat16 [1024, 1024], P('dp'), may hold values from -1.5 to 1.5
- second_gain: float32 [1024], replicated, may hold values from 0.5 to 1.5
- w_router: bfloat16 [1024, 32], P('dp'), may hold values from -0.1875 to 0.1875
- w_gate_up: bfloat16 [32, 1024, 1024], P('expert', 'dp'), may hold values from -0.1875 to 0.1875
- w_down: bfloat16 [32, 512, 1024], P('expert', 'dp'), may hold values from -1 to 1
- out_cotangent: bfloat16 [4096, 1024], P(('dp', 'expert')), may hold values from -6 to 6
Outputs:
- layer_output: bfloat16 [4096, 1024], P(('dp', 'expert'))
- input_grad: bfloat16 [4096, 1024], P(('dp', 'expert'))
- first_gain_grad: float32 [1024], replicated
- query_grad: float32 [1024, 1024], P('dp')
- keyvalue_grad: float32 [1024, 1024], P('dp')
- output_grad: float32 [1024, 1024], P('dp')
- second_gain_grad: float32 [1024], replicated
- router_grad: float32 [1024, 32], P('dp')
- gate_up_grad: float32 [32, 1024, 1024], P('expert', 'dp')
- down_grad: float32 [32, 512, 1024], P('expert', 'dp')
The draws below stay inside these ranges and needn't reach their ends.
Inputs may be any that keep to these rules, and one draw needn't show every extreme that they name: `expert_routes`: each row names 8 different experts. Among the rows of one device no expert is named by more than 40 rows, a bound that some block reaches. `segment_ids`: segment numbers never fall along the tokens; each document holds 1 to 64 tokens, and one holds exactly 64.
All inputs are finite; a program needn't handle non-finite values.
Results may differ from the reference program's by a relative error of at most 0.018.
Values may be sent and summed in bfloat16 or wider, within the bound.
No kernel may reach another device: no remote copies, remote signals or barrier semaphores. Data moves between devices by JAX's collectives and lax.ppermute only.
A program may use at most 128 MiB of HBM per device.

```python
import math
import jax
import jax.numpy as jnp
import numpy as np
from jax import lax

D = 1024
HEADS = 16
KV_HEADS = 8
HEAD_DIM = 64
F = 512
EXPERTS = 32
TOPK = 8
TOK_DEV = 128
CAP = 40
TOKENS = 4096
SEGMENTS = 128
DOC_MOST = 64


def raised(array, own_key, source, target, blocks, factor):
    def block_of(axis_at):
        return (jnp.arange(array.shape[axis_at]) // (array.shape[axis_at] // blocks)).reshape((-1,) + (1,) * (array.ndim - 1 - axis_at))

    near = jax.random.permutation(own_key, blocks)[block_of(target)]
    second = (block_of(target) + blocks // 2) % blocks
    return jnp.where((block_of(source) == near) | (block_of(source) == second), factor * array, array)


def level_of(rng, extent, pieces, least, largest):
    factor_of = 1.0
    for dim, blocks in pieces:
        draws = jax.random.uniform(jax.random.fold_in(jax.random.fold_in(rng, 6), dim), (blocks,), jnp.float32, least / len(pieces), largest / len(pieces))
        factor_of = factor_of * jnp.repeat(jnp.exp(draws), extent[dim] // blocks).reshape((-1,) + (1,) * (len(extent) - 1 - dim))
    return factor_of


def length_profile(amount, total, reach, slope):
    loads = [(1 << 20) // math.isqrt(standing ** slope) + 1 for standing in range(2, amount + 1)]
    spare, given = total - reach - (amount - 1), [1] * (amount - 1)
    while spare > 0:
        free = [i for i in range(amount - 1) if given[i] < reach]
        pool, remaining = sum([loads[i] for i in free]), spare
        for i in free:
            addition = min(reach - given[i], max(1, remaining * loads[i] // pool), spare)
            given[i] = given[i] + addition
            spare = spare - addition
    return np.array([reach] + given)


def ragged(rng, count, total, most, lean):
    if count == 2:
        one = jax.random.randint(rng, (), max(1, total - most), min(most, total - 1) + 1)
        return jnp.stack([one, total - one])
    lengths = jnp.asarray(length_profile(count, total, most, lean), jnp.int32)
    twos = (count - 1) // 2
    source_of, receiver = lengths[1:1 + 2 * twos:2], lengths[2:2 + 2 * twos:2]
    room = jnp.minimum(source_of - 1, most - receiver)
    passed = jax.random.randint(jax.random.fold_in(rng, 1), (twos,), 0, 1 << 20) % (room + 1)
    lengths = lengths.at[1:1 + 2 * twos:2].set(source_of - passed).at[2:2 + 2 * twos:2].set(receiver + passed)
    return lengths[jax.random.permutation(jax.random.fold_in(rng, 2), count)]


def shared_out(stream_key, own, number, rows, number_of, top, reach, lean):
    order = jax.random.permutation(stream_key, number_of)
    packed, ordinary = portions_of(number_of, rows * top, reach, lean, True), portions_of(number_of, rows * top, reach, lean, False)
    places = jnp.arange(number_of)

    def named(lengths, turn):
        used = int((lengths > 0).sum())
        fixed = max(1, used // 4)
        moved = fixed + (places - fixed + turn * (used - fixed)) % max(1, number_of - fixed)
        return jnp.zeros((number_of,), jnp.int32).at[order[jnp.where(places < fixed, places, moved)]].set(jnp.asarray(lengths, jnp.int32))

    lengths = jnp.where(number % 4 == 0, named(packed, number // 4), named(ordinary, number - number // 4 - 1))
    mixed = jax.random.permutation(jax.random.fold_in(own, 3), number_of)
    donor, receiver = mixed[0:number_of // 2 * 2:2], mixed[1:number_of // 2 * 2:2]
    slack = jnp.minimum(lengths[donor] - 1, reach - lengths[receiver]) // 2
    slack = jnp.where((donor == order[0]) | (receiver == order[0]) | (lengths[receiver] == 0), 0, jnp.maximum(slack, 0))
    moved = jax.random.randint(jax.random.fold_in(own, 4), (number_of // 2,), 0, 1 << 20) % (slack + 1)
    lengths = lengths.at[donor].add(-moved).at[receiver].add(moved)
    labels = jnp.searchsorted(jnp.cumsum(lengths), jnp.arange(rows * top), side="right").astype(jnp.int32)
    table = labels.reshape(top, rows).T
    table = table[jax.random.permutation(jax.random.fold_in(own, 1), rows)]
    turn = jax.random.randint(jax.random.fold_in(own, 2), (rows, 1), 0, top)
    return jnp.take_along_axis(table, (jnp.arange(top)[None, :] + turn) % top, axis=1)


def portions_of(amount, total, reach, slope, full):
    loads = [(1 << 20) // math.isqrt(rank ** slope) + 1 for rank in range(1, amount + 1)]
    largest = reach if full else min(reach, max(-(-total // amount), total * loads[0] // sum(loads)))
    least = 1 if total - largest >= amount - 1 else 0
    holding, spare = [largest] + [least] * (amount - 1), total - largest - least * (amount - 1)
    while spare > 0:
        movable = [i for i in range(1, amount) if holding[i] < largest] or [i for i in range(1, amount) if holding[i] < reach]
        whole, left = sum([loads[i] for i in movable]), spare
        for i in movable:
            extra = min(reach - holding[i], max(1, left * loads[i] // whole), spare)
            holding[i] = holding[i] + extra
            spare = spare - extra
    return np.array(holding)


def noise(stream_key, shape, width, limit, cuts=(), kind=jnp.bfloat16):
    drawn = width * jax.random.normal(stream_key, shape, jnp.float32)
    if cuts:
        drawn = drawn * level_of(stream_key, shape, cuts, -0.22, 0.18)
    return jnp.clip(drawn, -limit, limit).astype(kind)


def noise_with(key, extent, width, reach, shards, heavy, kind=jnp.bfloat16):
    drawn = width * jax.random.normal(key, extent, jnp.float32)
    if shards:
        drawn = drawn * level_of(key, extent, shards, -0.22, 0.18)
    return jnp.clip(raised(drawn, jax.random.fold_in(key, 3), *heavy), -reach, reach).astype(kind)


def setup_inputs(seed: int = 0) -> dict:
    arg_keys = jax.random.split(jax.random.key(seed), 13)
    layer_input = noise(arg_keys[0], (TOKENS, D), 1.0, 6.0, ((0, 32),))
    segment_ids = jnp.searchsorted(jnp.cumsum(ragged(arg_keys[1], SEGMENTS, TOKENS, DOC_MOST, 2)), jnp.arange(TOKENS), side="right").astype(jnp.int32)
    expert_routes_keys = jax.random.split(jax.random.fold_in(arg_keys[2], 1), TOKENS // TOK_DEV)
    expert_routes_turns = jax.random.permutation(jax.random.fold_in(arg_keys[2], 3), TOKENS // TOK_DEV)
    expert_routes = jax.vmap(lambda own, number: shared_out(jax.random.fold_in(arg_keys[2], 2), own, number, TOK_DEV, EXPERTS, TOPK, CAP, 2))(expert_routes_keys, expert_routes_turns).reshape((TOKENS, TOPK))
    first_gain = jnp.clip(1.0 + 0.1 * jax.random.normal(arg_keys[3], (D,), jnp.float32), 0.5, 1.5)
    w_query = noise(arg_keys[4], (D, HEADS * HEAD_DIM), D ** -0.5, 0.1875, ((0, 4),))
    w_keyvalue = noise(arg_keys[5], (D, 2 * KV_HEADS * HEAD_DIM), D ** -0.5, 0.1875, ((0, 4),))
    w_output = noise(arg_keys[6], (HEADS * HEAD_DIM, D), (D // 64) ** -0.5, 1.5, ((0, 4),))
    second_gain = jnp.clip(1.0 + 0.1 * jax.random.normal(arg_keys[7], (D,), jnp.float32), 0.5, 1.5)
    w_router = noise(arg_keys[8], (D, EXPERTS), D ** -0.5, 0.1875, ((0, 4),))
    w_gate_up = noise(arg_keys[9], (EXPERTS, D, 2 * F), D ** -0.5, 0.1875, ((0, 8), (1, 4)))
    w_down = noise(arg_keys[10], (EXPERTS, F, D), (F // 16) ** -0.5, 1.0, ((0, 8), (1, 4)))
    out_cotangent = noise_with(arg_keys[11], (TOKENS, D), 1.0, 6.0, ((0, 32),), (0, 1, 32, 2.75))
    return {"layer_input": layer_input, "segment_ids": segment_ids, "expert_routes": expert_routes, "first_gain": first_gain, "w_query": w_query, "w_keyvalue": w_keyvalue, "w_output": w_output, "second_gain": second_gain, "w_router": w_router, "w_gate_up": w_gate_up, "w_down": w_down, "out_cotangent": out_cotangent}


epsilon = 1e-06
residual_scale = 0.22
score_scale = 0.015625
rope_base = 10000.0

def rope_tables(length, head_width):
    halfway = head_width // 2
    frequency = jnp.exp(-jnp.log(rope_base) * (2.0 * jnp.arange(halfway, dtype=jnp.float32) / head_width))
    angles = jnp.arange(length, dtype=jnp.float32)[:, None] * frequency[None, :]
    cosine = jnp.concatenate([jnp.cos(angles), jnp.cos(angles)], axis=1)
    sine_table = jnp.concatenate([jnp.sin(angles), jnp.sin(angles)], axis=1)
    return (cosine, sine_table)

def rotate(values, cosine, sine_table, direction):
    halfway = values.shape[-1] // 2
    turned = jnp.concatenate([-values[..., halfway:], values[..., :halfway]], axis=-1)
    return values * cosine[:, None, :] + direction * turned * sine_table[:, None, :]

def norm_forward(inputs_f32, gain_vector):
    inverse = lax.rsqrt(lax.optimization_barrier(jnp.mean(inputs_f32 * inputs_f32, axis=-1, keepdims=True)) + epsilon)
    return (inputs_f32 * inverse * gain_vector, inverse)

def norm_backward(inputs_f32, inverse, gain_vector, upstream):
    weighted = upstream * gain_vector
    gain_part = lax.optimization_barrier(jnp.sum(upstream * inputs_f32 * inverse, axis=0))
    through = inverse * weighted - inputs_f32 * (inverse * inverse * inverse) * lax.optimization_barrier(jnp.mean(weighted * inputs_f32, axis=-1, keepdims=True))
    return (gain_part, through)

def activate(pre_act):
    gate_half = pre_act[..., :F]
    up_half = pre_act[..., F:]
    return gate_half * jax.nn.sigmoid(gate_half) * up_half

def activate_backward(pre_act, d_act):
    gate_half = pre_act[..., :F]
    up_half = pre_act[..., F:]
    sigmoid_gate = jax.nn.sigmoid(gate_half)
    d_gate = d_act * up_half * sigmoid_gate * (1.0 + gate_half * (1.0 - sigmoid_gate))
    d_up = d_act * gate_half * sigmoid_gate
    return jnp.concatenate([d_gate, d_up], axis=-1)

def visible_mask(segment):
    places = jnp.arange(segment.shape[0])
    return (places[:, None] >= places[None, :]) & (segment[:, None] == segment[None, :])

def masked_scores(query, keys, visible):
    raw_scores = jnp.einsum('qkgd,pkd->kgqp', query.astype(jnp.float32), keys.astype(jnp.float32)) * score_scale
    return jnp.where(visible[None, None], raw_scores, -1e+30)

def attend_forward(normed, w_query, w_keyvalue, visible, cosine, sine_table):
    length = normed.shape[0]
    per_group = HEADS // KV_HEADS
    query_raw = jnp.dot(normed, w_query, preferred_element_type=jnp.float32).reshape(length, HEADS, HEAD_DIM)
    keyval = jnp.dot(normed, w_keyvalue, preferred_element_type=jnp.float32).reshape(length, 2, KV_HEADS, HEAD_DIM)
    query = rotate(query_raw, cosine, sine_table, 1.0).astype(jnp.bfloat16).reshape(length, KV_HEADS, per_group, HEAD_DIM)
    keys = rotate(keyval[:, 0], cosine, sine_table, 1.0).astype(jnp.bfloat16)
    values = keyval[:, 1].astype(jnp.bfloat16)
    scores = masked_scores(query, keys, visible)
    highest = lax.optimization_barrier(jnp.max(scores, axis=-1, keepdims=True))
    log_total = highest + jnp.log(lax.optimization_barrier(jnp.sum(jnp.exp(scores - highest), axis=-1, keepdims=True)))
    probabilities = jnp.exp(scores - log_total).astype(jnp.bfloat16)
    attended = jnp.einsum('kgqp,pkd->qkgd', probabilities.astype(jnp.float32), values.astype(jnp.float32))
    attended = attended.reshape(length, HEADS * HEAD_DIM).astype(jnp.bfloat16)
    return (query, keys, values, attended, log_total)

def attend_backward(query, keys, values, attended, log_total, d_attended, visible):
    length = query.shape[0]
    per_group = HEADS // KV_HEADS
    scores = masked_scores(query, keys, visible)
    probs_f32 = jnp.exp(scores - log_total)
    probs_half = probs_f32.astype(jnp.bfloat16)
    d_att4 = d_attended.reshape(length, KV_HEADS, per_group, HEAD_DIM).astype(jnp.float32)
    att_four = attended.reshape(length, KV_HEADS, per_group, HEAD_DIM).astype(jnp.float32)
    d_values = jnp.einsum('kgqp,qkgd->pkd', probs_half.astype(jnp.float32), d_att4)
    d_probs = jnp.einsum('qkgd,pkd->kgqp', d_att4, values.astype(jnp.float32))
    row_delta = jnp.einsum('qkgd,qkgd->kgq', d_att4, att_four)
    d_scores = (probs_f32 * (d_probs - row_delta[..., None]) * score_scale).astype(jnp.bfloat16)
    d_query = jnp.einsum('kgqp,pkd->qkgd', d_scores.astype(jnp.float32), keys.astype(jnp.float32)).reshape(length, HEADS, HEAD_DIM)
    d_keys = jnp.einsum('kgqp,qkgd->pkd', d_scores.astype(jnp.float32), query.astype(jnp.float32))
    return (d_query, d_keys, d_values)

def reference(layer_input, segment_ids, expert_routes, first_gain, w_query, w_keyvalue, w_output, second_gain, w_router, w_gate_up, w_down, out_cotangent):
    length = TOK_DEV
    blocks = TOKENS // TOK_DEV
    cosine, sine_table = rope_tables(length, HEAD_DIM)
    inputs_f32 = layer_input.astype(jnp.float32).reshape(blocks, length, D)
    segments = segment_ids.reshape(blocks, length)

    def forward_step(carry, item):
        block_rows, segment = item
        normed, inverse = norm_forward(block_rows, first_gain)
        normed = normed.astype(jnp.bfloat16)
        visible = visible_mask(segment)
        outputs = attend_forward(normed, w_query, w_keyvalue, visible, cosine, sine_table)
        branch = jnp.dot(outputs[3], w_output, preferred_element_type=jnp.float32)
        return (carry, block_rows + residual_scale * branch)
    zero_carry = jnp.zeros((), jnp.float32)
    _, hidden = lax.scan(forward_step, zero_carry, (inputs_f32, segments))
    hidden = hidden.reshape(TOKENS, D)
    normed2, inverse2 = norm_forward(hidden, second_gain)
    normed2 = normed2.astype(jnp.bfloat16)
    logits = jnp.dot(normed2, w_router, preferred_element_type=jnp.float32)
    chosen = jnp.take_along_axis(logits, expert_routes, axis=1)
    highest = lax.optimization_barrier(jnp.max(chosen, axis=1, keepdims=True))
    exponent = jnp.exp(chosen - highest)
    gates = exponent / lax.optimization_barrier(jnp.sum(exponent, axis=1, keepdims=True))
    onehot = (expert_routes.reshape(blocks, length * TOPK)[:, :, None] == jnp.arange(EXPERTS, dtype=jnp.int32)[None, None, :]).astype(jnp.int32)
    ranking = lax.optimization_barrier(jnp.sum((jnp.cumsum(onehot, axis=1) - 1) * onehot, axis=2))
    columns = (jnp.arange(blocks, dtype=jnp.int32)[:, None] * CAP + ranking).reshape(-1).astype(jnp.int32)
    pair_ids = jnp.arange(TOKENS * TOPK, dtype=jnp.int32)
    table = jnp.full((EXPERTS, blocks * CAP), TOKENS * TOPK, jnp.int32)
    table = table.at[expert_routes.reshape(-1), columns].set(pair_ids)
    padded_normed = jnp.concatenate([normed2, jnp.zeros((1, D), jnp.bfloat16)], axis=0)
    d_out = out_cotangent.astype(jnp.float32)
    padded_cot = jnp.concatenate([d_out, jnp.zeros((1, D), jnp.float32)], axis=0)
    padded_gates = jnp.concatenate([gates.reshape(-1), jnp.zeros((1,), jnp.float32)], axis=0)

    def expert_step(carry, item):
        mixed, back_sum, gate_sum = carry
        pairs, gate_up, down = item
        token_index = pairs // TOPK
        picked_rows = padded_normed[token_index]
        pre_act = jnp.dot(picked_rows, gate_up, preferred_element_type=jnp.float32)
        activated = activate(pre_act).astype(jnp.bfloat16)
        result = jnp.dot(activated, down, preferred_element_type=jnp.float32).astype(jnp.bfloat16)
        gate_rows = padded_gates[pairs]
        cot_rows = padded_cot[token_index]
        mixed = mixed.at[token_index].add(gate_rows[:, None] * result.astype(jnp.float32))
        gate_sum = gate_sum.at[pairs].add(residual_scale * lax.optimization_barrier(jnp.sum(cot_rows * result.astype(jnp.float32), axis=1)))
        d_result = (residual_scale * gate_rows[:, None] * cot_rows).astype(jnp.bfloat16)
        d_act = jnp.dot(d_result, down.T, preferred_element_type=jnp.float32)
        d_down = jnp.dot(activated.T, d_result, preferred_element_type=jnp.float32)
        d_pre = activate_backward(pre_act, d_act).astype(jnp.bfloat16)
        d_gate_up = jnp.dot(picked_rows.T, d_pre, preferred_element_type=jnp.float32)
        d_rows = jnp.dot(d_pre, gate_up.T, preferred_element_type=jnp.float32).astype(jnp.bfloat16)
        back_sum = back_sum.at[token_index].add(d_rows.astype(jnp.float32))
        return ((mixed, back_sum, gate_sum), (d_gate_up, d_down))
    start = (jnp.zeros((TOKENS + 1, D), jnp.float32), jnp.zeros((TOKENS + 1, D), jnp.float32), jnp.zeros((TOKENS * TOPK + 1,), jnp.float32))
    (mixed, back_sum, gate_sum), (gate_up_grad, down_grad) = lax.scan(expert_step, start, (table, w_gate_up, w_down))
    layer_output = (hidden + residual_scale * mixed[:TOKENS]).astype(jnp.bfloat16)
    d_gates = gate_sum[:TOKENS * TOPK].reshape(TOKENS, TOPK)
    d_chosen = gates * (d_gates - lax.optimization_barrier(jnp.sum(gates * d_gates, axis=1, keepdims=True)))
    select = (expert_routes[:, :, None] == jnp.arange(EXPERTS, dtype=jnp.int32)[None, None, :]).astype(jnp.float32)
    d_logits = lax.optimization_barrier(jnp.sum(select * d_chosen[:, :, None], axis=1)).astype(jnp.bfloat16)
    router_grad = jnp.dot(normed2.T, d_logits, preferred_element_type=jnp.float32)
    d_normed2 = back_sum[:TOKENS] + jnp.dot(d_logits, w_router.T, preferred_element_type=jnp.float32)
    second_gain_grad, d_through = norm_backward(hidden, inverse2, second_gain, d_normed2)
    d_hidden = (d_out + d_through).reshape(blocks, length, D)

    def backward_step(carry, item):
        block_rows, segment, d_block = item
        normed, inverse = norm_forward(block_rows, first_gain)
        normed = normed.astype(jnp.bfloat16)
        visible = visible_mask(segment)
        query, keys, values, attended, log_total = attend_forward(normed, w_query, w_keyvalue, visible, cosine, sine_table)
        d_branch = (residual_scale * d_block).astype(jnp.bfloat16)
        d_wout = jnp.dot(attended.T, d_branch, preferred_element_type=jnp.float32)
        d_attended = jnp.dot(d_branch, w_output.T, preferred_element_type=jnp.float32).astype(jnp.bfloat16)
        d_query, d_keys, d_values = attend_backward(query, keys, values, attended, log_total, d_attended, visible)
        d_query = rotate(d_query, cosine, sine_table, -1.0).reshape(length, HEADS * HEAD_DIM).astype(jnp.bfloat16)
        d_keys = rotate(d_keys, cosine, sine_table, -1.0)
        d_keyvalue = jnp.stack([d_keys, d_values], axis=1).reshape(length, 2 * KV_HEADS * HEAD_DIM).astype(jnp.bfloat16)
        d_wquery = jnp.dot(normed.T, d_query, preferred_element_type=jnp.float32)
        d_wkeyvalue = jnp.dot(normed.T, d_keyvalue, preferred_element_type=jnp.float32)
        d_normed = jnp.dot(d_query, w_query.T, preferred_element_type=jnp.float32) + jnp.dot(d_keyvalue, w_keyvalue.T, preferred_element_type=jnp.float32)
        gain_part, d_rows = norm_backward(block_rows, inverse, first_gain, d_normed)
        grad_block = (d_block + d_rows).astype(jnp.bfloat16)
        carry = (carry[0] + d_wquery, carry[1] + d_wkeyvalue, carry[2] + d_wout, carry[3] + gain_part)
        return (carry, grad_block)
    start = (jnp.zeros((D, HEADS * HEAD_DIM), jnp.float32), jnp.zeros((D, 2 * KV_HEADS * HEAD_DIM), jnp.float32), jnp.zeros((HEADS * HEAD_DIM, D), jnp.float32), jnp.zeros((D,), jnp.float32))
    (query_grad, keyvalue_grad, output_grad, first_gain_grad), input_grad = lax.scan(backward_step, start, (inputs_f32, segments, d_hidden))
    input_grad = input_grad.reshape(TOKENS, D)
    return (layer_output, input_grad, first_gain_grad, query_grad, keyvalue_grad, output_grad, second_gain_grad, router_grad, gate_up_grad, down_grad)
```

```python
import jax
import jax.numpy as jnp
from jax import lax
from jax.sharding import PartitionSpec as P

D = 1024
HEADS = 16
KV_HEADS = 8
HEAD_DIM = 64
F = 512
EXPERTS = 32
TOPK = 8
CAP = 40


epsilon = 1e-06
residual_scale = 0.22
score_scale = 0.015625
rope_base = 10000.0


def rope_tables(length, head_width):
    halfway = head_width // 2
    frequency = jnp.exp(
        -jnp.log(rope_base) * (2.0 * jnp.arange(halfway, dtype=jnp.float32) / head_width)
    )
    angles = jnp.arange(length, dtype=jnp.float32)[:, None] * frequency[None, :]
    cosine = jnp.concatenate([jnp.cos(angles), jnp.cos(angles)], axis=1)
    sine_table = jnp.concatenate([jnp.sin(angles), jnp.sin(angles)], axis=1)
    return (cosine, sine_table)


def rotate(values, cosine, sine_table, direction):
    halfway = values.shape[-1] // 2
    turned = jnp.concatenate([-values[..., halfway:], values[..., :halfway]], axis=-1)
    return values * cosine[:, None, :] + direction * turned * sine_table[:, None, :]


def norm_forward(inputs_f32, gain_vector):
    inverse = lax.rsqrt(jnp.mean(inputs_f32 * inputs_f32, axis=-1, keepdims=True) + epsilon)
    return (inputs_f32 * inverse * gain_vector, inverse)


def norm_backward(inputs_f32, inverse, gain_vector, upstream):
    weighted = upstream * gain_vector
    gain_part = jnp.sum(upstream * inputs_f32 * inverse, axis=0)
    through = inverse * weighted - inputs_f32 * (inverse * inverse * inverse) * jnp.mean(
        weighted * inputs_f32, axis=-1, keepdims=True
    )
    return (gain_part, through)


def activate(pre_act):
    gate_half = pre_act[..., :F]
    up_half = pre_act[..., F:]
    return gate_half * jax.nn.sigmoid(gate_half) * up_half


def activate_backward(pre_act, d_act):
    gate_half = pre_act[..., :F]
    up_half = pre_act[..., F:]
    sigmoid_gate = jax.nn.sigmoid(gate_half)
    d_gate = d_act * up_half * sigmoid_gate * (1.0 + gate_half * (1.0 - sigmoid_gate))
    d_up = d_act * gate_half * sigmoid_gate
    return jnp.concatenate([d_gate, d_up], axis=-1)


def masked_scores(query, keys, visible):
    raw_scores = (
        jnp.einsum("qkgd,pkd->kgqp", query, keys, preferred_element_type=jnp.float32) * score_scale
    )
    return jnp.where(visible[None, None], raw_scores, -1e30)


def attend_forward(normed, full_query, full_keyvalue, visible, cosine, sine_table):
    length = normed.shape[0]
    per_group = HEADS // KV_HEADS
    query_raw = jnp.dot(normed, full_query, preferred_element_type=jnp.float32).reshape(
        length, HEADS, HEAD_DIM
    )
    keyval = jnp.dot(normed, full_keyvalue, preferred_element_type=jnp.float32).reshape(
        length, 2, KV_HEADS, HEAD_DIM
    )
    query = (
        rotate(query_raw, cosine, sine_table, 1.0)
        .astype(jnp.bfloat16)
        .reshape(length, KV_HEADS, per_group, HEAD_DIM)
    )
    keys = rotate(keyval[:, 0], cosine, sine_table, 1.0).astype(jnp.bfloat16)
    values = keyval[:, 1].astype(jnp.bfloat16)
    scores = masked_scores(query, keys, visible)
    highest = jnp.max(scores, axis=-1, keepdims=True)
    log_total = highest + jnp.log(jnp.sum(jnp.exp(scores - highest), axis=-1, keepdims=True))
    probabilities = jnp.exp(scores - log_total).astype(jnp.bfloat16)
    attended = jnp.einsum(
        "kgqp,pkd->qkgd", probabilities, values, preferred_element_type=jnp.float32
    )
    attended = attended.reshape(length, HEADS * HEAD_DIM).astype(jnp.bfloat16)
    return (query, keys, values, attended, log_total)


def attend_backward(query, keys, values, attended, log_total, d_attended, visible):
    length = query.shape[0]
    per_group = HEADS // KV_HEADS
    scores = masked_scores(query, keys, visible)
    probs_f32 = jnp.exp(scores - log_total)
    probs_half = probs_f32.astype(jnp.bfloat16)
    d_att4 = d_attended.reshape(length, KV_HEADS, per_group, HEAD_DIM)
    att_four = attended.reshape(length, KV_HEADS, per_group, HEAD_DIM)
    d_values = jnp.einsum("kgqp,qkgd->pkd", probs_half, d_att4, preferred_element_type=jnp.float32)
    d_probs = jnp.einsum("qkgd,pkd->kgqp", d_att4, values, preferred_element_type=jnp.float32)
    row_delta = jnp.einsum("qkgd,qkgd->kgq", d_att4, att_four, preferred_element_type=jnp.float32)
    d_scores = (probs_f32 * (d_probs - row_delta[..., None]) * score_scale).astype(jnp.bfloat16)
    d_query = jnp.einsum(
        "kgqp,pkd->qkgd", d_scores, keys, preferred_element_type=jnp.float32
    ).reshape(length, HEADS, HEAD_DIM)
    d_keys = jnp.einsum("kgqp,qkgd->pkd", d_scores, query, preferred_element_type=jnp.float32)
    return (d_query, d_keys, d_values)


def butterfly_sum(value, axes):
    for axis in axes:
        size = lax.axis_size(axis)
        step = 1
        while step < size:
            value = value + lax.ppermute(value, axis, [(i, i ^ step) for i in range(size)])
            step *= 2
    return value


def spread_over(axes, array):
    for axis in reversed(axes):
        array = lax.all_gather(array, axis, axis=0, tiled=True)
    return array


def sum_to_owner(axes, array):
    for axis in axes:
        array = lax.psum_scatter(array, axis, scatter_dimension=0, tiled=True)
    return array


def expert_pass(tokens, cotangents, gate, hit, w_up, w_dn):
    blocks = tokens.shape[0] // 128
    ranking = jnp.cumsum(hit.reshape(blocks, 128).astype(jnp.int32), axis=1) - 1
    slot = jnp.where(hit.reshape(blocks, 128), ranking, -1)
    select = slot[:, None, :] == jnp.arange(CAP, dtype=jnp.int32)[None, :, None]
    onehot = select.astype(jnp.bfloat16)
    rows = blocks * CAP
    picked = jnp.einsum(
        "bst,btd->bsd", onehot, tokens.reshape(blocks, 128, D), preferred_element_type=jnp.float32
    ).astype(jnp.bfloat16).reshape(rows, D)
    cot = jnp.einsum(
        "bst,btd->bsd",
        onehot,
        cotangents.reshape(blocks, 128, D),
        preferred_element_type=jnp.float32,
    ).reshape(rows, D)
    gate_slot = jnp.sum(
        jnp.where(select, gate.reshape(blocks, 1, 128), 0.0), axis=2
    ).reshape(rows, 1)
    pre_act = jnp.dot(picked, w_up, preferred_element_type=jnp.float32)
    activated = activate(pre_act).astype(jnp.bfloat16)
    result = (
        jnp.dot(activated, w_dn, preferred_element_type=jnp.float32)
        .astype(jnp.bfloat16)
        .astype(jnp.float32)
    )
    d_gate_slot = residual_scale * jnp.sum(cot * result, axis=1)
    d_gate = jnp.sum(jnp.where(select, d_gate_slot.reshape(blocks, CAP, 1), 0.0), axis=1)
    gated = (gate_slot * result).astype(jnp.bfloat16)
    mixed = jnp.einsum(
        "bst,bsd->btd", onehot, gated.reshape(blocks, CAP, D), preferred_element_type=jnp.float32
    ).reshape(blocks * 128, D)
    d_result = (residual_scale * gate_slot * cot).astype(jnp.bfloat16)
    d_act = jnp.dot(d_result, w_dn.T, preferred_element_type=jnp.float32)
    d_down = jnp.dot(activated.T, d_result, preferred_element_type=jnp.float32)
    d_pre = activate_backward(pre_act, d_act).astype(jnp.bfloat16)
    d_up = jnp.dot(picked.T, d_pre, preferred_element_type=jnp.float32)
    d_rows = jnp.dot(d_pre, w_up.T, preferred_element_type=jnp.float32).astype(jnp.bfloat16)
    back = jnp.einsum(
        "bst,bsd->btd", onehot, d_rows.reshape(blocks, CAP, D), preferred_element_type=jnp.float32
    ).reshape(blocks * 128, D)
    return (mixed, back, d_gate.reshape(blocks * 128), d_up, d_down)


def per_device(
    layer_input,
    segment_ids,
    expert_routes,
    first_gain,
    w_query,
    w_keyvalue,
    w_output,
    second_gain,
    w_router,
    w_gate_up,
    w_down,
    out_cotangent,
):
    length = layer_input.shape[0]
    owners = lax.axis_size("expert")
    groups = lax.axis_size("dp")
    group_at = lax.axis_index("dp")
    owner_at = lax.axis_index("expert")
    per_owner = w_gate_up.shape[0]
    shard = w_query.shape[0]
    part = shard // owners
    every = ("dp", "expert")

    def own_part(weight):
        return lax.dynamic_slice_in_dim(weight, owner_at * part, part, 0)

    router_rows = part * EXPERTS // D if part * EXPERTS % D == 0 else 0
    pack = jnp.concatenate([own_part(w_query), own_part(w_keyvalue), own_part(w_output)], axis=0)
    gathered = lax.all_gather(pack, every, axis=0).reshape(groups * owners, 3, part, D)
    full_query = gathered[:, 0].reshape(D, HEADS * HEAD_DIM)
    full_keyvalue = gathered[:, 1].reshape(D, 2 * KV_HEADS * HEAD_DIM)
    full_output = gathered[:, 2].reshape(HEADS * HEAD_DIM, D)
    full_router = lax.all_gather(own_part(w_router), every, axis=0, tiled=True)

    exchange = per_owner % groups == 0
    if exchange:
        local = per_owner // groups
        token_axes = ("expert", "dp")
        first_expert = owner_at * per_owner + group_at * local
        own_up = lax.all_to_all(w_gate_up, "dp", split_axis=0, concat_axis=1, tiled=True)
        own_down = lax.all_to_all(w_down, "dp", split_axis=0, concat_axis=1, tiled=True)
    else:
        local = per_owner
        token_axes = ("expert",)
        first_expert = owner_at * per_owner
        own_up = lax.all_gather(w_gate_up, "dp", axis=1, tiled=True)
        own_down = lax.all_gather(w_down, "dp", axis=1, tiled=True)
    all_routes = spread_over(token_axes, expert_routes)
    all_cotangents = spread_over(token_axes, out_cotangent)

    cosine, sine_table = rope_tables(length, HEAD_DIM)
    places = jnp.arange(length)
    visible = (places[:, None] >= places[None, :]) & (segment_ids[:, None] == segment_ids[None, :])
    inputs_f32 = layer_input.astype(jnp.float32)
    normed, inverse = norm_forward(inputs_f32, first_gain)
    normed = normed.astype(jnp.bfloat16)
    query, keys, values, attended, log_total = attend_forward(
        normed, full_query, full_keyvalue, visible, cosine, sine_table
    )
    hidden = inputs_f32 + residual_scale * jnp.dot(
        attended, full_output, preferred_element_type=jnp.float32
    )
    normed2, inverse2 = norm_forward(hidden, second_gain)
    normed2 = normed2.astype(jnp.bfloat16)
    all_normed2 = spread_over(token_axes, normed2)

    def gates_of(rows, routes):
        named = jnp.any(
            routes[:, :, None] == jnp.arange(EXPERTS, dtype=jnp.int32)[None, None, :], axis=1
        )
        logits = jnp.dot(rows, full_router, preferred_element_type=jnp.float32)
        highest = jnp.max(jnp.where(named, logits, -jnp.inf), axis=1, keepdims=True)
        exponent = jnp.where(named, jnp.exp(jnp.where(named, logits - highest, 0.0)), 0.0)
        return exponent / jnp.sum(exponent, axis=1, keepdims=True)

    all_gates = gates_of(all_normed2, all_routes)
    d_out = out_cotangent.astype(jnp.float32)
    mixed, back = 0.0, 0.0
    d_gate_list, up_list, down_list = [], [], []
    for j in range(local):
        hit = jnp.any(all_routes == first_expert + j, axis=1)
        gate = lax.dynamic_index_in_dim(all_gates, first_expert + j, 1, keepdims=False)
        one_mixed, one_back, d_gate, d_up, d_dn = expert_pass(
            all_normed2, all_cotangents, gate, hit, own_up[j], own_down[j]
        )
        mixed, back = mixed + one_mixed, back + one_back
        d_gate_list.append(d_gate)
        up_list.append(d_up.astype(jnp.bfloat16))
        down_list.append(d_dn.astype(jnp.bfloat16))
    back_own = sum_to_owner(token_axes, back.astype(jnp.bfloat16)).astype(jnp.float32)
    sources = EXPERTS // local
    d_gate_out = jnp.stack(d_gate_list).reshape(local, sources, length).transpose(1, 0, 2)
    d_gates = (
        lax.all_to_all(d_gate_out, token_axes, split_axis=0, concat_axis=0, tiled=True)
        .reshape(EXPERTS, length)
        .T
    )
    d_up_all, d_down_all = jnp.stack(up_list), jnp.stack(down_list)
    if exchange:
        gate_up_grad = lax.all_to_all(d_up_all, "dp", split_axis=1, concat_axis=0, tiled=True)
        down_grad = lax.all_to_all(d_down_all, "dp", split_axis=1, concat_axis=0, tiled=True)
    else:
        gate_up_grad = lax.psum_scatter(d_up_all, "dp", scatter_dimension=1, tiled=True)
        down_grad = lax.psum_scatter(d_down_all, "dp", scatter_dimension=1, tiled=True)
    mixed_own = sum_to_owner(token_axes, mixed.astype(jnp.bfloat16)).astype(jnp.float32)
    layer_output = (hidden + residual_scale * mixed_own).astype(jnp.bfloat16)

    gates = gates_of(normed2, expert_routes)
    d_logits = (gates * (d_gates - jnp.sum(gates * d_gates, axis=1, keepdims=True))).astype(
        jnp.bfloat16
    )
    d_router = jnp.dot(normed2.T, d_logits, preferred_element_type=jnp.float32)
    d_normed2 = back_own + jnp.dot(d_logits, full_router.T, preferred_element_type=jnp.float32)
    d_second_gain, d_through = norm_backward(hidden, inverse2, second_gain, d_normed2)
    second_gain_grad = butterfly_sum(d_second_gain, ("expert", "dp"))
    d_hidden = d_out + d_through
    d_branch = (residual_scale * d_hidden).astype(jnp.bfloat16)
    d_wout = jnp.dot(attended.T, d_branch, preferred_element_type=jnp.float32)
    d_attended = jnp.dot(d_branch, full_output.T, preferred_element_type=jnp.float32).astype(
        jnp.bfloat16
    )
    d_query, d_keys, d_values = attend_backward(
        query, keys, values, attended, log_total, d_attended, visible
    )
    d_query = (
        rotate(d_query, cosine, sine_table, -1.0)
        .reshape(length, HEADS * HEAD_DIM)
        .astype(jnp.bfloat16)
    )
    d_keys = rotate(d_keys, cosine, sine_table, -1.0)
    d_keyvalue = (
        jnp.stack([d_keys, d_values], axis=1)
        .reshape(length, 2 * KV_HEADS * HEAD_DIM)
        .astype(jnp.bfloat16)
    )
    d_wquery = jnp.dot(normed.T, d_query, preferred_element_type=jnp.float32)
    d_wkeyvalue = jnp.dot(normed.T, d_keyvalue, preferred_element_type=jnp.float32)
    d_normed = jnp.dot(d_query, full_query.T, preferred_element_type=jnp.float32) + jnp.dot(
        d_keyvalue, full_keyvalue.T, preferred_element_type=jnp.float32
    )
    d_first_gain, d_inputs = norm_backward(inputs_f32, inverse, first_gain, d_normed)
    first_gain_grad = butterfly_sum(d_first_gain, ("expert", "dp"))
    input_grad = (d_hidden + d_inputs).astype(jnp.bfloat16)

    def reduced(*grads):
        packed = jnp.stack([g.astype(jnp.bfloat16) for g in grads])
        count, width = len(grads), grads[0].shape[1]
        packed = packed.reshape(count, groups, owners, part, width).transpose(2, 1, 0, 3, 4)
        packed = packed.reshape(owners * groups * count * part, width)
        mine = sum_to_owner(("expert", "dp"), packed).reshape(1, count, part, width)
        whole = lax.all_gather(mine, "expert", axis=0, tiled=True)
        whole = whole.transpose(1, 0, 2, 3).reshape(count, owners * part, width)
        return [whole[i].astype(jnp.float32) for i in range(count)]

    output_grad, query_grad, keyvalue_grad = reduced(d_wout, d_wquery, d_wkeyvalue)
    (router_grad,) = reduced(d_router)
    return (
        layer_output,
        input_grad,
        first_gain_grad,
        query_grad,
        keyvalue_grad,
        output_grad,
        second_gain_grad,
        router_grad,
        gate_up_grad.astype(jnp.float32),
        down_grad.astype(jnp.float32),
    )


def solution(mesh):
    return jax.shard_map(
        per_device,
        mesh=mesh,
        in_specs=(
            P(("dp", "expert"), None),
            P(("dp", "expert")),
            P(("dp", "expert"), None),
            P(),
            P("dp", None),
            P("dp", None),
            P("dp", None),
            P(),
            P("dp", None),
            P("expert", "dp", None),
            P("expert", "dp", None),
            P(("dp", "expert"), None),
        ),
        out_specs=(
            P(("dp", "expert"), None),
            P(("dp", "expert"), None),
            P(),
            P("dp", None),
            P("dp", None),
            P("dp", None),
            P(),
            P("dp", None),
            P("expert", "dp", None),
            P("expert", "dp", None),
        ),
        check_vma=False,
    )
```

```python
import jax
import jax.numpy as jnp
import numpy as np
from jax import lax
from jax.experimental import pallas as pl
from jax.experimental.pallas import tpu as pltpu
from jax.sharding import PartitionSpec as P

D = 1024
HEADS = 16
KV_HEADS = 8
HEAD_DIM = 64
F = 512
EXPERTS = 32
TOPK = 8
CAP = 40


epsilon = 1e-06
residual_scale = 0.22
score_scale = 0.015625
rope_base = 10000.0


def rope_tables(length, head_width):
    halfway = head_width // 2
    frequency = jnp.exp(
        -jnp.log(rope_base) * (2.0 * jnp.arange(halfway, dtype=jnp.float32) / head_width)
    )
    angles = jnp.arange(length, dtype=jnp.float32)[:, None] * frequency[None, :]
    cosine = jnp.concatenate([jnp.cos(angles), jnp.cos(angles)], axis=1)
    sine_table = jnp.concatenate([jnp.sin(angles), jnp.sin(angles)], axis=1)
    return (cosine, sine_table)


def rotate(values, cosine, sine_table, direction):
    halfway = values.shape[-1] // 2
    turned = jnp.concatenate([-values[..., halfway:], values[..., :halfway]], axis=-1)
    return values * cosine[:, None, :] + direction * turned * sine_table[:, None, :]


def norm_forward(inputs_f32, gain_vector):
    inverse = lax.rsqrt(jnp.mean(inputs_f32 * inputs_f32, axis=-1, keepdims=True) + epsilon)
    return (inputs_f32 * inverse * gain_vector, inverse)


def norm_backward(inputs_f32, inverse, gain_vector, upstream):
    weighted = upstream * gain_vector
    gain_part = jnp.sum(upstream * inputs_f32 * inverse, axis=0)
    through = inverse * weighted - inputs_f32 * (inverse * inverse * inverse) * jnp.mean(
        weighted * inputs_f32, axis=-1, keepdims=True
    )
    return (gain_part, through)


def activate(pre_act):
    gate_half = pre_act[..., :F]
    up_half = pre_act[..., F:]
    return gate_half * jax.nn.sigmoid(gate_half) * up_half


def activate_backward(pre_act, d_act):
    gate_half = pre_act[..., :F]
    up_half = pre_act[..., F:]
    sigmoid_gate = jax.nn.sigmoid(gate_half)
    d_gate = d_act * up_half * sigmoid_gate * (1.0 + gate_half * (1.0 - sigmoid_gate))
    d_up = d_act * gate_half * sigmoid_gate
    return jnp.concatenate([d_gate, d_up], axis=-1)


def masked_scores(query, keys, visible):
    raw_scores = (
        jnp.einsum("qkgd,pkd->kgqp", query, keys, preferred_element_type=jnp.float32) * score_scale
    )
    return jnp.where(visible[None, None], raw_scores, -1e30)


def attend_forward(normed, full_query, full_keyvalue, visible, cosine, sine_table):
    length = normed.shape[0]
    per_group = HEADS // KV_HEADS
    query_raw = jnp.dot(normed, full_query, preferred_element_type=jnp.float32).reshape(
        length, HEADS, HEAD_DIM
    )
    keyval = jnp.dot(normed, full_keyvalue, preferred_element_type=jnp.float32).reshape(
        length, 2, KV_HEADS, HEAD_DIM
    )
    query = (
        rotate(query_raw, cosine, sine_table, 1.0)
        .astype(jnp.bfloat16)
        .reshape(length, KV_HEADS, per_group, HEAD_DIM)
    )
    keys = rotate(keyval[:, 0], cosine, sine_table, 1.0).astype(jnp.bfloat16)
    values = keyval[:, 1].astype(jnp.bfloat16)
    scores = masked_scores(query, keys, visible)
    highest = jnp.max(scores, axis=-1, keepdims=True)
    log_total = highest + jnp.log(jnp.sum(jnp.exp(scores - highest), axis=-1, keepdims=True))
    probabilities = jnp.exp(scores - log_total).astype(jnp.bfloat16)
    attended = jnp.einsum(
        "kgqp,pkd->qkgd", probabilities, values, preferred_element_type=jnp.float32
    )
    attended = attended.reshape(length, HEADS * HEAD_DIM).astype(jnp.bfloat16)
    return (query, keys, values, attended, log_total)


def attend_backward(query, keys, values, attended, log_total, d_attended, visible):
    length = query.shape[0]
    per_group = HEADS // KV_HEADS
    scores = masked_scores(query, keys, visible)
    probs_f32 = jnp.exp(scores - log_total)
    probs_half = probs_f32.astype(jnp.bfloat16)
    d_att4 = d_attended.reshape(length, KV_HEADS, per_group, HEAD_DIM)
    att_four = attended.reshape(length, KV_HEADS, per_group, HEAD_DIM)
    d_values = jnp.einsum("kgqp,qkgd->pkd", probs_half, d_att4, preferred_element_type=jnp.float32)
    d_probs = jnp.einsum("qkgd,pkd->kgqp", d_att4, values, preferred_element_type=jnp.float32)
    row_delta = jnp.einsum("qkgd,qkgd->kgq", d_att4, att_four, preferred_element_type=jnp.float32)
    d_scores = (probs_f32 * (d_probs - row_delta[..., None]) * score_scale).astype(jnp.bfloat16)
    d_query = jnp.einsum(
        "kgqp,pkd->qkgd", d_scores, keys, preferred_element_type=jnp.float32
    ).reshape(length, HEADS, HEAD_DIM)
    d_keys = jnp.einsum("kgqp,qkgd->pkd", d_scores, query, preferred_element_type=jnp.float32)
    return (d_query, d_keys, d_values)


def butterfly_sum(value, axes):
    for axis in axes:
        size = lax.axis_size(axis)
        step = 1
        while step < size:
            value = value + lax.ppermute(value, axis, [(i, i ^ step) for i in range(size)])
            step *= 2
    return value


def spread_over(axes, array):
    for axis in reversed(axes):
        array = lax.all_gather(array, axis, axis=0, tiled=True)
    return array


def sum_to_owner(axes, array):
    for axis in axes:
        array = lax.psum_scatter(array, axis, scatter_dimension=0, tiled=True)
    return array


def expert_pass(tokens, cotangents, gate, hit, w_up, w_dn):
    blocks = tokens.shape[0] // 128
    ranking = jnp.cumsum(hit.reshape(blocks, 128).astype(jnp.int32), axis=1) - 1
    slot = jnp.where(hit.reshape(blocks, 128), ranking, -1)
    select = slot[:, None, :] == jnp.arange(CAP, dtype=jnp.int32)[None, :, None]
    onehot = select.astype(jnp.bfloat16)
    rows = blocks * CAP
    picked = jnp.einsum(
        "bst,btd->bsd", onehot, tokens.reshape(blocks, 128, D), preferred_element_type=jnp.float32
    ).astype(jnp.bfloat16).reshape(rows, D)
    cot = jnp.einsum(
        "bst,btd->bsd",
        onehot,
        cotangents.reshape(blocks, 128, D),
        preferred_element_type=jnp.float32,
    ).reshape(rows, D)
    gate_slot = jnp.sum(
        jnp.where(select, gate.reshape(blocks, 1, 128), 0.0), axis=2
    ).reshape(rows, 1)
    pre_act = jnp.dot(picked, w_up, preferred_element_type=jnp.float32)
    activated = activate(pre_act).astype(jnp.bfloat16)
    result = (
        jnp.dot(activated, w_dn, preferred_element_type=jnp.float32)
        .astype(jnp.bfloat16)
        .astype(jnp.float32)
    )
    d_gate_slot = residual_scale * jnp.sum(cot * result, axis=1)
    d_gate = jnp.sum(jnp.where(select, d_gate_slot.reshape(blocks, CAP, 1), 0.0), axis=1)
    gated = (gate_slot * result).astype(jnp.bfloat16)
    mixed = jnp.einsum(
        "bst,bsd->btd", onehot, gated.reshape(blocks, CAP, D), preferred_element_type=jnp.float32
    ).reshape(blocks * 128, D)
    d_result = (residual_scale * gate_slot * cot).astype(jnp.bfloat16)
    d_act = jnp.dot(d_result, w_dn.T, preferred_element_type=jnp.float32)
    d_down = jnp.dot(activated.T, d_result, preferred_element_type=jnp.float32)
    d_pre = activate_backward(pre_act, d_act).astype(jnp.bfloat16)
    d_up = jnp.dot(picked.T, d_pre, preferred_element_type=jnp.float32)
    d_rows = jnp.dot(d_pre, w_up.T, preferred_element_type=jnp.float32).astype(jnp.bfloat16)
    back = jnp.einsum(
        "bst,bsd->btd", onehot, d_rows.reshape(blocks, CAP, D), preferred_element_type=jnp.float32
    ).reshape(blocks * 128, D)
    return (mixed, back, d_gate.reshape(blocks * 128), d_up, d_down)


def general_device(
    layer_input,
    segment_ids,
    expert_routes,
    first_gain,
    w_query,
    w_keyvalue,
    w_output,
    second_gain,
    w_router,
    w_gate_up,
    w_down,
    out_cotangent,
):
    length = layer_input.shape[0]
    owners = lax.axis_size("expert")
    groups = lax.axis_size("dp")
    group_at = lax.axis_index("dp")
    owner_at = lax.axis_index("expert")
    per_owner = w_gate_up.shape[0]
    shard = w_query.shape[0]
    part = shard // owners
    every = ("dp", "expert")

    def own_part(weight):
        return lax.dynamic_slice_in_dim(weight, owner_at * part, part, 0)

    router_rows = part * EXPERTS // D if part * EXPERTS % D == 0 else 0
    pack = jnp.concatenate([own_part(w_query), own_part(w_keyvalue), own_part(w_output)], axis=0)
    gathered = lax.all_gather(pack, every, axis=0).reshape(groups * owners, 3, part, D)
    full_query = gathered[:, 0].reshape(D, HEADS * HEAD_DIM)
    full_keyvalue = gathered[:, 1].reshape(D, 2 * KV_HEADS * HEAD_DIM)
    full_output = gathered[:, 2].reshape(HEADS * HEAD_DIM, D)
    full_router = lax.all_gather(own_part(w_router), every, axis=0, tiled=True)

    exchange = per_owner % groups == 0
    if exchange:
        local = per_owner // groups
        token_axes = ("expert", "dp")
        first_expert = owner_at * per_owner + group_at * local
        own_up = lax.all_to_all(w_gate_up, "dp", split_axis=0, concat_axis=1, tiled=True)
        own_down = lax.all_to_all(w_down, "dp", split_axis=0, concat_axis=1, tiled=True)
    else:
        local = per_owner
        token_axes = ("expert",)
        first_expert = owner_at * per_owner
        own_up = lax.all_gather(w_gate_up, "dp", axis=1, tiled=True)
        own_down = lax.all_gather(w_down, "dp", axis=1, tiled=True)
    all_routes = spread_over(token_axes, expert_routes)
    all_cotangents = spread_over(token_axes, out_cotangent)

    cosine, sine_table = rope_tables(length, HEAD_DIM)
    places = jnp.arange(length)
    visible = (places[:, None] >= places[None, :]) & (segment_ids[:, None] == segment_ids[None, :])
    inputs_f32 = layer_input.astype(jnp.float32)
    normed, inverse = norm_forward(inputs_f32, first_gain)
    normed = normed.astype(jnp.bfloat16)
    query, keys, values, attended, log_total = attend_forward(
        normed, full_query, full_keyvalue, visible, cosine, sine_table
    )
    hidden = inputs_f32 + residual_scale * jnp.dot(
        attended, full_output, preferred_element_type=jnp.float32
    )
    normed2, inverse2 = norm_forward(hidden, second_gain)
    normed2 = normed2.astype(jnp.bfloat16)
    all_normed2 = spread_over(token_axes, normed2)

    def gates_of(rows, routes):
        named = jnp.any(
            routes[:, :, None] == jnp.arange(EXPERTS, dtype=jnp.int32)[None, None, :], axis=1
        )
        logits = jnp.dot(rows, full_router, preferred_element_type=jnp.float32)
        highest = jnp.max(jnp.where(named, logits, -jnp.inf), axis=1, keepdims=True)
        exponent = jnp.where(named, jnp.exp(jnp.where(named, logits - highest, 0.0)), 0.0)
        return exponent / jnp.sum(exponent, axis=1, keepdims=True)

    all_gates = gates_of(all_normed2, all_routes)
    d_out = out_cotangent.astype(jnp.float32)
    mixed, back = 0.0, 0.0
    d_gate_list, up_list, down_list = [], [], []
    for j in range(local):
        hit = jnp.any(all_routes == first_expert + j, axis=1)
        gate = lax.dynamic_index_in_dim(all_gates, first_expert + j, 1, keepdims=False)
        one_mixed, one_back, d_gate, d_up, d_dn = expert_pass(
            all_normed2, all_cotangents, gate, hit, own_up[j], own_down[j]
        )
        mixed, back = mixed + one_mixed, back + one_back
        d_gate_list.append(d_gate)
        up_list.append(d_up.astype(jnp.bfloat16))
        down_list.append(d_dn.astype(jnp.bfloat16))
    back_own = sum_to_owner(token_axes, back.astype(jnp.bfloat16)).astype(jnp.float32)
    sources = EXPERTS // local
    d_gate_out = jnp.stack(d_gate_list).reshape(local, sources, length).transpose(1, 0, 2)
    d_gates = (
        lax.all_to_all(d_gate_out, token_axes, split_axis=0, concat_axis=0, tiled=True)
        .reshape(EXPERTS, length)
        .T
    )
    d_up_all, d_down_all = jnp.stack(up_list), jnp.stack(down_list)
    if exchange:
        gate_up_grad = lax.all_to_all(d_up_all, "dp", split_axis=1, concat_axis=0, tiled=True)
        down_grad = lax.all_to_all(d_down_all, "dp", split_axis=1, concat_axis=0, tiled=True)
    else:
        gate_up_grad = lax.psum_scatter(d_up_all, "dp", scatter_dimension=1, tiled=True)
        down_grad = lax.psum_scatter(d_down_all, "dp", scatter_dimension=1, tiled=True)
    mixed_own = sum_to_owner(token_axes, mixed.astype(jnp.bfloat16)).astype(jnp.float32)
    layer_output = (hidden + residual_scale * mixed_own).astype(jnp.bfloat16)

    gates = gates_of(normed2, expert_routes)
    d_logits = (gates * (d_gates - jnp.sum(gates * d_gates, axis=1, keepdims=True))).astype(
        jnp.bfloat16
    )
    d_router = jnp.dot(normed2.T, d_logits, preferred_element_type=jnp.float32)
    d_normed2 = back_own + jnp.dot(d_logits, full_router.T, preferred_element_type=jnp.float32)
    d_second_gain, d_through = norm_backward(hidden, inverse2, second_gain, d_normed2)
    second_gain_grad = butterfly_sum(d_second_gain, ("expert", "dp"))
    d_hidden = d_out + d_through
    d_branch = (residual_scale * d_hidden).astype(jnp.bfloat16)
    d_wout = jnp.dot(attended.T, d_branch, preferred_element_type=jnp.float32)
    d_attended = jnp.dot(d_branch, full_output.T, preferred_element_type=jnp.float32).astype(
        jnp.bfloat16
    )
    d_query, d_keys, d_values = attend_backward(
        query, keys, values, attended, log_total, d_attended, visible
    )
    d_query = (
        rotate(d_query, cosine, sine_table, -1.0)
        .reshape(length, HEADS * HEAD_DIM)
        .astype(jnp.bfloat16)
    )
    d_keys = rotate(d_keys, cosine, sine_table, -1.0)
    d_keyvalue = (
        jnp.stack([d_keys, d_values], axis=1)
        .reshape(length, 2 * KV_HEADS * HEAD_DIM)
        .astype(jnp.bfloat16)
    )
    d_wquery = jnp.dot(normed.T, d_query, preferred_element_type=jnp.float32)
    d_wkeyvalue = jnp.dot(normed.T, d_keyvalue, preferred_element_type=jnp.float32)
    d_normed = jnp.dot(d_query, full_query.T, preferred_element_type=jnp.float32) + jnp.dot(
        d_keyvalue, full_keyvalue.T, preferred_element_type=jnp.float32
    )
    d_first_gain, d_inputs = norm_backward(inputs_f32, inverse, first_gain, d_normed)
    first_gain_grad = butterfly_sum(d_first_gain, ("expert", "dp"))
    input_grad = (d_hidden + d_inputs).astype(jnp.bfloat16)

    def reduced(*grads):
        packed = jnp.stack([g.astype(jnp.bfloat16) for g in grads])
        count, width = len(grads), grads[0].shape[1]
        packed = packed.reshape(count, groups, owners, part, width).transpose(2, 1, 0, 3, 4)
        packed = packed.reshape(owners * groups * count * part, width)
        mine = sum_to_owner(("expert", "dp"), packed).reshape(1, count, part, width)
        whole = lax.all_gather(mine, "expert", axis=0, tiled=True)
        whole = whole.transpose(1, 0, 2, 3).reshape(count, owners * part, width)
        return [whole[i].astype(jnp.float32) for i in range(count)]

    output_grad, query_grad, keyvalue_grad = reduced(d_wout, d_wquery, d_wkeyvalue)
    (router_grad,) = reduced(d_router)
    return (
        layer_output,
        input_grad,
        first_gain_grad,
        query_grad,
        keyvalue_grad,
        output_grad,
        second_gain_grad,
        router_grad,
        gate_up_grad.astype(jnp.float32),
        down_grad.astype(jnp.float32),
    )


def expert_kernel(*refs):
    place_ref = refs[0]
    tok_a, tok_b, cot_a, cot_b = refs[1:5], refs[5:9], refs[9:13], refs[13:17]
    routes_ref, router_ref, up_ref, down_ref = refs[17:21]
    mix_a, mix_b, back_a, back_b = refs[21:25], refs[25:29], refs[29:33], refs[33:37]
    dgate_ref, d_up_ref, d_down_ref = refs[37:40]
    (
        tok_buf,
        cot_buf,
        mix_buf,
        back_buf,
        rows_scr,
        act_scr,
        dres_scr,
        dpre_scr,
        cot_scr,
        gate_scr,
        slot_scr,
        tri_scr,
        in_sem,
        out_sem,
    ) = refs[40:]
    half = D // 2
    expert = place_ref[0]
    owner = place_ref[1]
    chunk_rows = 8 * CAP

    def in_copies(kk, slot):
        c, y = kk // 2, kk % 2
        found = []
        for a, b, buf, base in ((tok_a, tok_b, tok_buf, 0), (cot_a, cot_b, cot_buf, 3)):
            found.append(
                pltpu.make_async_copy(
                    a[kk], buf.at[slot, :, pl.ds(0, half)], in_sem.at[slot, base]
                )
            )
            for x in range(2):
                found.append(
                    pltpu.make_async_copy(
                        b[2 * c + x].at[pl.ds(512 * y, 512), :],
                        buf.at[slot, pl.ds(512 * x, 512), pl.ds(half, half)],
                        in_sem.at[slot, base + 1 + x],
                    )
                )
        return found

    def out_copies(kk, slot):
        c, y = kk // 2, kk % 2
        found = []
        for a, b, buf, base in ((mix_a, mix_b, mix_buf, 0), (back_a, back_b, back_buf, 3)):
            found.append(
                pltpu.make_async_copy(
                    buf.at[slot, :, pl.ds(0, half)], a[kk], out_sem.at[slot, base]
                )
            )
            for x in range(2):
                found.append(
                    pltpu.make_async_copy(
                        buf.at[slot, pl.ds(512 * x, 512), pl.ds(half, half)],
                        b[2 * c + x].at[pl.ds(512 * y, 512), :],
                        out_sem.at[slot, base + 1 + x],
                    )
                )
        return found

    for copy in in_copies(0, 0):
        copy.start()
    before = lax.broadcasted_iota(jnp.int32, (256, 256), 0)
    after = lax.broadcasted_iota(jnp.int32, (256, 256), 1)
    tri_scr[...] = ((before <= after) & ((before < 128) == (after < 128))).astype(jnp.bfloat16)

    def pair_mask(pair):
        return slot_scr[pair] == lax.broadcasted_iota(jnp.int32, (2 * CAP, 256), 0)

    def chunk_step(k, carry):
        for kk in range(4):

            @pl.when(k == kk)
            def _():
                if kk < 3:
                    for copy in in_copies(kk + 1, (kk + 1) % 2):
                        copy.start()
                for copy in in_copies(kk, kk % 2):
                    copy.wait()
                if kk >= 2:
                    for copy in out_copies(kk - 2, kk % 2):
                        copy.wait()

        at = lax.rem(k, 2)
        base = pl.multiple_of(k * chunk_rows, chunk_rows)
        away = k // 2 + 4 * lax.rem(k, 2)
        for pair in range(4):
            device = jnp.bitwise_xor(owner, away + 2 * (pair // 2)) * 4 + 2 * (pair % 2)
            routes = jnp.concatenate([routes_ref[device], routes_ref[device + 1]], axis=1)
            hit = jnp.max((routes == expert).astype(jnp.float32), axis=0, keepdims=True)
            rank = jnp.dot(
                jnp.broadcast_to(hit, (16, 256)).astype(jnp.bfloat16),
                tri_scr[...],
                preferred_element_type=jnp.float32,
            )[0:1]
            second = lax.broadcasted_iota(jnp.int32, (1, 256), 1) >= 128
            slot = rank.astype(jnp.int32) - 1 + jnp.where(second, CAP, 0)
            slot_scr[pair] = jnp.where(hit > 0.5, slot, -1)
            mask = pair_mask(pair)
            onehot = mask.astype(jnp.bfloat16)
            token_rows = tok_buf[at, pl.ds(256 * pair, 256), :]
            logits = lax.dot_general(
                router_ref[...],
                token_rows,
                (((1,), (1,)), ((), ())),
                preferred_element_type=jnp.float32,
            )
            names = lax.broadcasted_iota(jnp.int32, (EXPERTS, 256), 0)
            named = routes[0:1] == names
            for i in range(1, TOPK):
                named = named | (routes[i : i + 1] == names)
            highest = jnp.max(jnp.where(named, logits, -3e38), axis=0, keepdims=True)
            exponent = jnp.where(named, jnp.exp(jnp.where(named, logits - highest, 0.0)), 0.0)
            own = jnp.sum(jnp.where(names == expert, exponent, 0.0), axis=0, keepdims=True)
            gate = own / jnp.sum(exponent, axis=0, keepdims=True)
            gate_slot = jnp.sum(jnp.where(mask, gate, 0.0), axis=1, keepdims=True)
            gate_scr[pl.ds(2 * CAP * pair, 2 * CAP), :] = gate_slot
            place = pl.ds(base + 2 * CAP * pair, 2 * CAP)
            rows_scr[place, :] = jnp.dot(
                onehot, token_rows, preferred_element_type=jnp.float32
            ).astype(jnp.bfloat16)
            cot = jnp.dot(
                onehot, cot_buf[at, pl.ds(256 * pair, 256), :], preferred_element_type=jnp.float32
            )
            cot_scr[pl.ds(2 * CAP * pair, 2 * CAP), :] = cot.astype(jnp.bfloat16)
            dres_scr[place, :] = (residual_scale * gate_slot * cot).astype(jnp.bfloat16)
        here = pl.ds(base, chunk_rows)
        pre = jnp.dot(rows_scr[here, :], up_ref[...], preferred_element_type=jnp.float32)
        gate_half, up_half = pre[:, :F], pre[:, F:]
        sigmoid_gate = 1.0 / (1.0 + jnp.exp(-gate_half))
        swish = gate_half * sigmoid_gate
        activated = (swish * up_half).astype(jnp.bfloat16)
        act_scr[here, :] = activated
        d_act = lax.dot_general(
            dres_scr[here, :],
            down_ref[...],
            (((1,), (1,)), ((), ())),
            preferred_element_type=jnp.float32,
        )
        dpre_scr[here, 0:F] = (
            d_act * up_half * sigmoid_gate * (1.0 + gate_half * (1.0 - sigmoid_gate))
        ).astype(jnp.bfloat16)
        dpre_scr[here, F : 2 * F] = (d_act * swish).astype(jnp.bfloat16)
        result = (
            jnp.dot(activated, down_ref[...], preferred_element_type=jnp.float32)
            .astype(jnp.bfloat16)
            .astype(jnp.float32)
        )
        d_gate_slot = residual_scale * jnp.sum(
            cot_scr[...].astype(jnp.float32) * result, axis=1, keepdims=True
        )
        gated = (gate_scr[...] * result).astype(jnp.bfloat16)
        d_rows = lax.dot_general(
            dpre_scr[here, :],
            up_ref[...],
            (((1,), (1,)), ((), ())),
            preferred_element_type=jnp.float32,
        ).astype(jnp.bfloat16)
        for pair in range(4):
            device = jnp.bitwise_xor(owner, away + 2 * (pair // 2)) * 4 + 2 * (pair % 2)
            mask = pair_mask(pair)
            onehot = mask.astype(jnp.bfloat16)
            mine = slice(2 * CAP * pair, 2 * CAP * (pair + 1))
            d_gate = jnp.sum(jnp.where(mask, d_gate_slot[mine], 0.0), axis=0, keepdims=True)
            dgate_ref[device] = d_gate[:, :128]
            dgate_ref[device + 1] = d_gate[:, 128:]
            rows = pl.ds(256 * pair, 256)
            mix_buf[at, rows, :] = lax.dot_general(
                onehot,
                gated[mine],
                (((0,), (0,)), ((), ())),
                preferred_element_type=jnp.float32,
            ).astype(jnp.bfloat16)
            back_buf[at, rows, :] = lax.dot_general(
                onehot,
                d_rows[mine],
                (((0,), (0,)), ((), ())),
                preferred_element_type=jnp.float32,
            ).astype(jnp.bfloat16)
        for kk in range(4):

            @pl.when(k == kk)
            def _():
                for copy in out_copies(kk, kk % 2):
                    copy.start()

        return carry

    lax.fori_loop(0, 4, chunk_step, 0)

    def up_step(t, carry):
        rows = pl.ds(pl.multiple_of(t * 256, 256), 256)
        d_up_ref[rows, :] = lax.dot_general(
            rows_scr[:, rows],
            dpre_scr[...],
            (((0,), (0,)), ((), ())),
            preferred_element_type=jnp.float32,
        ).astype(jnp.bfloat16)
        return carry

    lax.fori_loop(0, D // 256, up_step, 0)

    def down_step(t, carry):
        rows = pl.ds(pl.multiple_of(t * 256, 256), 256)
        d_down_ref[rows, :] = lax.dot_general(
            act_scr[:, rows],
            dres_scr[...],
            (((0,), (0,)), ((), ())),
            preferred_element_type=jnp.float32,
        ).astype(jnp.bfloat16)
        return carry

    lax.fori_loop(0, F // 256, down_step, 0)
    for kk in (2, 3):
        for copy in out_copies(kk, kk % 2):
            copy.wait()


def expert_call(place, tok_a, tok_b, cot_a, cot_b, routes, router, w_up, w_dn):
    half = D // 2
    token_count = 1024
    hbm = pl.BlockSpec(memory_space=pl.ANY)
    vmem = pl.BlockSpec(memory_space=pltpu.VMEM)
    slots = 32 * CAP
    piece = jax.ShapeDtypeStruct((token_count, half), jnp.bfloat16)
    outs = pl.pallas_call(
        expert_kernel,
        in_specs=[pl.BlockSpec(memory_space=pltpu.SMEM)] + [hbm] * 16 + [vmem] * 4,
        out_specs=[hbm] * 16 + [vmem] * 3,
        out_shape=[piece] * 16
        + [
            jax.ShapeDtypeStruct((32, 1, 128), jnp.float32),
            jax.ShapeDtypeStruct((D, 2 * F), jnp.bfloat16),
            jax.ShapeDtypeStruct((F, D), jnp.bfloat16),
        ],
        scratch_shapes=[
            pltpu.VMEM((2, token_count, D), jnp.bfloat16),
            pltpu.VMEM((2, token_count, D), jnp.bfloat16),
            pltpu.VMEM((2, token_count, D), jnp.bfloat16),
            pltpu.VMEM((2, token_count, D), jnp.bfloat16),
            pltpu.VMEM((slots, D), jnp.bfloat16),
            pltpu.VMEM((slots, F), jnp.bfloat16),
            pltpu.VMEM((slots, D), jnp.bfloat16),
            pltpu.VMEM((slots, 2 * F), jnp.bfloat16),
            pltpu.VMEM((8 * CAP, D), jnp.bfloat16),
            pltpu.VMEM((8 * CAP, 1), jnp.float32),
            pltpu.VMEM((4, 1, 256), jnp.int32),
            pltpu.VMEM((256, 256), jnp.bfloat16),
            pltpu.SemaphoreType.DMA((2, 6)),
            pltpu.SemaphoreType.DMA((2, 6)),
        ],
        compiler_params=pltpu.CompilerParams(vmem_limit_bytes=56 * 1024 * 1024),
        name="experts",
    )(place, *tok_a, *tok_b, *cot_a, *cot_b, routes, router, w_up, w_dn)
    return outs[0:4], outs[4:8], outs[8:12], outs[12:16], outs[16], outs[17], outs[18]


def rope_constants(length):
    frequency = rope_base ** (-2.0 * np.arange(HEAD_DIM // 2) / HEAD_DIM)
    angles = np.arange(length)[:, None] * frequency[None, :]
    cosine = np.tile(np.cos(angles), (1, 4)).astype(np.float32)
    sine = np.sin(angles)
    signed = np.concatenate([-sine, sine, -sine, sine], axis=1).astype(np.float32)
    return cosine, signed


def turn(slab, cosine, signed):
    low = (lax.broadcasted_iota(jnp.int32, slab.shape, 1) & 32) == 0
    swapped = jnp.where(low, pltpu.roll(slab, 96, 1), pltpu.roll(slab, 32, 1))
    return slab * cosine + swapped * signed


def halves_stacked(slab, low):
    zero = jnp.zeros_like(slab)
    return jnp.concatenate([jnp.where(low, slab, zero), jnp.where(low, zero, slab)], axis=0)


def doubled(slab, low, second):
    other = pltpu.roll(slab, 64, 1)
    return jnp.where(low, other, slab) if second else jnp.where(low, slab, other)


def weight_copies(pieces_a, pieces_b, whole, sems, owner, kind, outward):
    half = D // 2
    copies = []
    for rel in range(8):
        c, x, y = rel & 1, (rel >> 1) & 1, (rel >> 2) & 1
        at = jnp.bitwise_xor(owner, rel)
        rows = pl.ds(32 * kind, 32)
        ends = (
            (pieces_a[2 * c + y].at[x, :, rows, :], whole.at[kind, :, at, :, pl.ds(0, half)]),
            (pieces_b[2 * c + x].at[y, :, rows, :], whole.at[kind, :, at, :, pl.ds(half, half)]),
        )
        for i, (piece, place) in enumerate(ends):
            pair = (place, piece) if outward else (piece, place)
            copies.append(pltpu.make_async_copy(*pair, sems.at[kind, rel, i]))
    return copies


def attention_forward_kernel(*refs):
    place_ref = refs[0]
    pieces_a, pieces_b = refs[1:5], refs[5:9]
    x_ref, seg_row, seg_col, gain1_ref, gain2_ref, cos_ref, sin_ref = refs[9:16]
    (normed_ref, inv1_ref, q_ref, k_ref, v_ref, att_ref, lse_ref, hidden_ref, inv2_ref, normed2_ref) = refs[16:26]
    whole, sems = refs[26:]
    owner = place_ref[1]
    half = D // 2
    for kind in range(3):
        for copy in weight_copies(pieces_a, pieces_b, whole, sems, owner, kind, False):
            copy.start()
    inputs = x_ref[...].astype(jnp.float32)
    inverse = lax.rsqrt(jnp.mean(inputs * inputs, axis=1, keepdims=True) + epsilon)
    normed = (inputs * inverse * gain1_ref[...]).astype(jnp.bfloat16)
    normed_ref[...] = normed
    inv1_ref[...] = inverse
    cosine, signed = cos_ref[...], sin_ref[...]
    for kind in range(2):
        for copy in weight_copies(pieces_a, pieces_b, whole, sems, owner, kind, False):
            copy.wait()
    query = jnp.dot(normed, whole[0].reshape(D, D), preferred_element_type=jnp.float32)
    keyval = jnp.dot(normed, whole[1].reshape(D, D), preferred_element_type=jnp.float32)
    for s in range(8):
        cols = slice(128 * s, 128 * s + 128)
        q_ref[:, cols] = turn(query[:, cols], cosine, signed).astype(jnp.bfloat16)
    for s in range(4):
        cols = slice(128 * s, 128 * s + 128)
        k_ref[:, cols] = turn(keyval[:, cols], cosine, signed).astype(jnp.bfloat16)
    v_ref[...] = keyval[:, half:].astype(jnp.bfloat16)
    rows_at = lax.broadcasted_iota(jnp.int32, (128, 128), 0)
    cols_at = lax.broadcasted_iota(jnp.int32, (128, 128), 1)
    visible = (rows_at >= cols_at) & (seg_col[...] == seg_row[...])
    visible2 = jnp.concatenate([visible, visible], axis=0)
    low = cols_at < 64
    for head in range(KV_HEADS):
        slab = slice(128 * (head // 2), 128 * (head // 2) + 128)
        q2 = halves_stacked(q_ref[:, 128 * head : 128 * head + 128], low)
        k2 = doubled(k_ref[:, slab], low, head % 2)
        v2 = doubled(v_ref[:, slab], low, head % 2)
        scores = lax.dot_general(
            q2, k2, (((1,), (1,)), ((), ())), preferred_element_type=jnp.float32
        )
        scores = jnp.where(visible2, scores * score_scale, -1e30)
        highest = jnp.max(scores, axis=1, keepdims=True)
        log_total = highest + jnp.log(jnp.sum(jnp.exp(scores - highest), axis=1, keepdims=True))
        probabilities = jnp.exp(scores - log_total).astype(jnp.bfloat16)
        lse_ref[head] = log_total
        mixed = jnp.dot(probabilities, v2, preferred_element_type=jnp.float32)
        att_ref[:, 128 * head : 128 * head + 128] = jnp.where(
            low, mixed[:128], mixed[128:]
        ).astype(jnp.bfloat16)
    for copy in weight_copies(pieces_a, pieces_b, whole, sems, owner, 2, False):
        copy.wait()
    hidden = inputs + residual_scale * jnp.dot(
        att_ref[...], whole[2].reshape(D, D), preferred_element_type=jnp.float32
    )
    inverse2 = lax.rsqrt(jnp.mean(hidden * hidden, axis=1, keepdims=True) + epsilon)
    normed2 = (hidden * inverse2 * gain2_ref[...]).astype(jnp.bfloat16)
    hidden_ref[...] = hidden
    inv2_ref[...] = inverse2
    normed2_ref[0] = normed2[:, :half]
    normed2_ref[1] = normed2[:, half:]


def attention_forward(place, pieces_a, pieces_b, x, seg, gain1, gain2, cosine, signed):
    hbm = pl.BlockSpec(memory_space=pl.ANY)
    vmem = pl.BlockSpec(memory_space=pltpu.VMEM)
    f32, b16 = jnp.float32, jnp.bfloat16
    shapes = [
        ((128, D), b16),
        ((128, 1), f32),
        ((128, D), b16),
        ((128, D // 2), b16),
        ((128, D // 2), b16),
        ((128, D), b16),
        ((KV_HEADS, 256, 1), f32),
        ((128, D), f32),
        ((128, 1), f32),
        ((2, 128, D // 2), b16),
    ]
    return pl.pallas_call(
        attention_forward_kernel,
        in_specs=[pl.BlockSpec(memory_space=pltpu.SMEM)] + [hbm] * 8 + [vmem] * 7,
        out_specs=[vmem] * 10,
        out_shape=[jax.ShapeDtypeStruct(s, t) for s, t in shapes],
        scratch_shapes=[
            pltpu.VMEM((3, 4, 8, 32, D), b16),
            pltpu.SemaphoreType.DMA((3, 8, 2)),
        ],
        compiler_params=pltpu.CompilerParams(vmem_limit_bytes=40 * 1024 * 1024),
        name="attention_forward",
    )(place, *pieces_a, *pieces_b, x, seg[None, :], seg[:, None], gain1, gain2, cosine, signed)


def attention_backward_kernel(*refs):
    place_ref = refs[0]
    pieces_a, pieces_b = refs[1:5], refs[5:9]
    (
        x_ref,
        seg_row,
        seg_col,
        gain1_ref,
        gain2_ref,
        cos_ref,
        sin_ref,
        normed_ref,
        inv1_ref,
        q_ref,
        k_ref,
        v_ref,
        att_ref,
        lse_ref,
        hidden_ref,
        inv2_ref,
        normed2_ref,
        dout_ref,
        back_ref,
        dgate_ref,
        routes_ref,
        router_ref,
    ) = refs[9:31]
    grads_a, grads_b = refs[31:35], refs[35:39]
    input_grad_ref, gains_ref, router_grad_ref = refs[39:42]
    whole, grad, datt_scr, dq_scr, dkv_scr, sems, out_sems = refs[42:]
    owner = place_ref[1]
    half = D // 2
    for kind in (2, 0, 1):
        for copy in weight_copies(pieces_a, pieces_b, whole, sems, owner, kind, False):
            copy.start()
    normed2 = jnp.concatenate([normed2_ref[0], normed2_ref[1]], axis=1)
    names = lax.broadcasted_iota(jnp.int32, (EXPERTS, 128), 0)
    routes = routes_ref[...]
    named = routes[0:1] == names
    for i in range(1, TOPK):
        named = named | (routes[i : i + 1] == names)
    logits = lax.dot_general(
        router_ref[...], normed2, (((1,), (1,)), ((), ())), preferred_element_type=jnp.float32
    )
    highest = jnp.max(jnp.where(named, logits, -3e38), axis=0, keepdims=True)
    exponent = jnp.where(named, jnp.exp(jnp.where(named, logits - highest, 0.0)), 0.0)
    gates = exponent / jnp.sum(exponent, axis=0, keepdims=True)
    d_gates = dgate_ref[...]
    d_logits = (gates * (d_gates - jnp.sum(gates * d_gates, axis=0, keepdims=True))).astype(
        jnp.bfloat16
    )
    router_grad_ref[...] = jnp.dot(d_logits, normed2, preferred_element_type=jnp.float32)
    back = [
        sum(back_ref[z, i].astype(jnp.float32) for z in range(4)) for i in range(2)
    ]
    d_normed2 = jnp.concatenate(back, axis=1) + lax.dot_general(
        d_logits, router_ref[...], (((0,), (0,)), ((), ())), preferred_element_type=jnp.float32
    )
    hidden, inverse2 = hidden_ref[...], inv2_ref[...]
    gains_ref[1:2, :] = jnp.sum(d_normed2 * hidden * inverse2, axis=0, keepdims=True)
    weighted = d_normed2 * gain2_ref[...]
    d_hidden = (
        dout_ref[...].astype(jnp.float32)
        + inverse2 * weighted
        - hidden
        * (inverse2 * inverse2 * inverse2)
        * jnp.mean(weighted * hidden, axis=1, keepdims=True)
    )
    d_branch = (residual_scale * d_hidden).astype(jnp.bfloat16)
    tn = (((0,), (0,)), ((), ()))
    nt = (((1,), (1,)), ((), ()))
    for z in range(4):
        grad[2, z] = (
            lax.dot_general(
                att_ref[:, 256 * z : 256 * z + 256], d_branch, tn, preferred_element_type=jnp.float32
            )
            .astype(jnp.bfloat16)
            .reshape(8, 32, D)
        )
    for copy in weight_copies(grads_a, grads_b, grad, out_sems, owner, 2, True):
        copy.start()
    for copy in weight_copies(pieces_a, pieces_b, whole, sems, owner, 2, False):
        copy.wait()
    datt_scr[...] = lax.dot_general(
        d_branch, whole[2].reshape(D, D), nt, preferred_element_type=jnp.float32
    ).astype(jnp.bfloat16)
    cosine, signed = cos_ref[...], -sin_ref[...]
    rows_at = lax.broadcasted_iota(jnp.int32, (128, 128), 0)
    cols_at = lax.broadcasted_iota(jnp.int32, (128, 128), 1)
    visible = (rows_at >= cols_at) & (seg_col[...] == seg_row[...])
    visible2 = jnp.concatenate([visible, visible], axis=0)
    low = cols_at < 64
    keep_k = keep_v = None
    for head in range(KV_HEADS):
        cols = slice(128 * head, 128 * head + 128)
        slab = slice(128 * (head // 2), 128 * (head // 2) + 128)
        q2 = halves_stacked(q_ref[:, cols], low)
        k2 = doubled(k_ref[:, slab], low, head % 2)
        v2 = doubled(v_ref[:, slab], low, head % 2)
        d_att = datt_scr[:, cols]
        da2 = halves_stacked(d_att, low)
        scores = lax.dot_general(q2, k2, nt, preferred_element_type=jnp.float32)
        scores = jnp.where(visible2, scores * score_scale, -1e30)
        probs = jnp.exp(scores - lse_ref[head])
        d_value = lax.dot_general(
            probs.astype(jnp.bfloat16), da2, tn, preferred_element_type=jnp.float32
        )
        d_probs = lax.dot_general(da2, v2, nt, preferred_element_type=jnp.float32)
        product = d_att.astype(jnp.float32) * att_ref[:, cols].astype(jnp.float32)
        delta = jnp.sum(halves_stacked(product, low), axis=1, keepdims=True)
        d_scores = (probs * (d_probs - delta) * score_scale).astype(jnp.bfloat16)
        d_q2 = jnp.dot(d_scores, k2, preferred_element_type=jnp.float32)
        d_query = jnp.where(low, d_q2[:128], d_q2[128:])
        dq_scr[:, cols] = turn(d_query, cosine, signed).astype(jnp.bfloat16)
        d_key = lax.dot_general(d_scores, q2, tn, preferred_element_type=jnp.float32)
        d_key = d_key + pltpu.roll(d_key, 64, 1)
        d_value = d_value + pltpu.roll(d_value, 64, 1)
        if head % 2 == 0:
            keep_k, keep_v = d_key, d_value
        else:
            dkv_scr[:, slab] = turn(jnp.where(low, keep_k, d_key), cosine, signed).astype(
                jnp.bfloat16
            )
            dkv_scr[:, half + slab.start : half + slab.stop] = jnp.where(
                low, keep_v, d_value
            ).astype(jnp.bfloat16)
    for kind, source in ((0, dq_scr), (1, dkv_scr)):
        for z in range(4):
            grad[kind, z] = (
                lax.dot_general(
                    normed_ref[:, 256 * z : 256 * z + 256],
                    source[...],
                    tn,
                    preferred_element_type=jnp.float32,
                )
                .astype(jnp.bfloat16)
                .reshape(8, 32, D)
            )
        for copy in weight_copies(grads_a, grads_b, grad, out_sems, owner, kind, True):
            copy.start()
    for kind in range(2):
        for copy in weight_copies(pieces_a, pieces_b, whole, sems, owner, kind, False):
            copy.wait()
    d_normed = lax.dot_general(
        dq_scr[...], whole[0].reshape(D, D), nt, preferred_element_type=jnp.float32
    ) + lax.dot_general(
        dkv_scr[...], whole[1].reshape(D, D), nt, preferred_element_type=jnp.float32
    )
    inputs, inverse = x_ref[...].astype(jnp.float32), inv1_ref[...]
    gains_ref[0:1, :] = jnp.sum(d_normed * inputs * inverse, axis=0, keepdims=True)
    weighted = d_normed * gain1_ref[...]
    input_grad_ref[...] = (
        d_hidden
        + inverse * weighted
        - inputs
        * (inverse * inverse * inverse)
        * jnp.mean(weighted * inputs, axis=1, keepdims=True)
    ).astype(jnp.bfloat16)
    for kind in range(3):
        for copy in weight_copies(grads_a, grads_b, grad, out_sems, owner, kind, True):
            copy.wait()


def attention_backward(place, pieces_a, pieces_b, *rest):
    hbm = pl.BlockSpec(memory_space=pl.ANY)
    vmem = pl.BlockSpec(memory_space=pltpu.VMEM)
    f32, b16 = jnp.float32, jnp.bfloat16
    piece = jax.ShapeDtypeStruct((2, 4, 96, D // 2), b16)
    outs = pl.pallas_call(
        attention_backward_kernel,
        in_specs=[pl.BlockSpec(memory_space=pltpu.SMEM)] + [hbm] * 8 + [vmem] * len(rest),
        out_specs=[hbm] * 8 + [vmem] * 3,
        out_shape=[piece] * 8
        + [
            jax.ShapeDtypeStruct((128, D), b16),
            jax.ShapeDtypeStruct((2, D), f32),
            jax.ShapeDtypeStruct((EXPERTS, D), f32),
        ],
        scratch_shapes=[
            pltpu.VMEM((3, 4, 8, 32, D), b16),
            pltpu.VMEM((3, 4, 8, 32, D), b16),
            pltpu.VMEM((128, D), b16),
            pltpu.VMEM((128, D), b16),
            pltpu.VMEM((128, D), b16),
            pltpu.SemaphoreType.DMA((3, 8, 2)),
            pltpu.SemaphoreType.DMA((3, 8, 2)),
        ],
        compiler_params=pltpu.CompilerParams(vmem_limit_bytes=48 * 1024 * 1024),
        name="attention_backward",
    )(place, *pieces_a, *pieces_b, *rest)
    return outs[0:4], outs[4:8], outs[8], outs[9], outs[10]


CORE, ACROSS, ALONG = 1, 2, 4


def swap(array, bit):
    return lax.ppermute(array, "expert", [(i, i ^ bit) for i in range(8)])


def to_group(array, axes, count):
    spread = jnp.broadcast_to(array[None], (count,) + array.shape)
    return lax.all_to_all(spread, axes, split_axis=0, concat_axis=0, tiled=True)


def gather_halves(halves):
    column = to_group(halves, "dp", 4)
    a0, b0 = column[:, 0], column[:, 1]
    a = jnp.stack([a0, swap(a0, ACROSS)])
    b = jnp.stack([b0, swap(b0, ALONG)])
    a_far, b_far = swap(a, ALONG), swap(b, ACROSS)
    pieces_a = [a, a_far, swap(a, CORE), swap(a_far, CORE)]
    pieces_b = [b, b_far, swap(b, CORE), swap(b_far, CORE)]
    return pieces_a, pieces_b


def add(one, two):
    return (one.astype(jnp.float32) + two.astype(jnp.float32)).astype(jnp.bfloat16)


def scatter_halves(pieces_a, pieces_b):
    a_far = add(pieces_a[1], swap(pieces_a[3], CORE))
    b_far = add(pieces_b[1], swap(pieces_b[3], CORE))
    a_near = add(pieces_a[0], swap(pieces_a[2], CORE))
    b_near = add(pieces_b[0], swap(pieces_b[2], CORE))
    a = add(a_near, swap(a_far, ALONG))
    b = add(b_near, swap(b_far, ACROSS))
    a_own = add(a[0], swap(a[1], ACROSS))
    b_own = add(b[0], swap(b[1], ALONG))
    out = jnp.stack([a_own, b_own], axis=1)
    return lax.all_to_all(out, "dp", split_axis=0, concat_axis=0, tiled=True)


def joined(halves):
    return jnp.concatenate([halves[0], halves[1]], axis=-1)


def block_device(
    layer_input,
    segment_ids,
    expert_routes,
    first_gain,
    w_query,
    w_keyvalue,
    w_output,
    second_gain,
    w_router,
    w_gate_up,
    w_down,
    out_cotangent,
):
    half = D // 2
    group_at, owner_at = lax.axis_index("dp"), lax.axis_index("expert")
    place = jnp.stack([owner_at * 4 + group_at, owner_at]).astype(jnp.int32)

    def own_part(weight):
        return lax.dynamic_slice_in_dim(weight, owner_at * 32, 32, 0)

    def split(rows):
        return jnp.stack([rows[:, :half], rows[:, half:]])

    pack = jnp.concatenate([own_part(w_query), own_part(w_keyvalue), own_part(w_output)], axis=0)
    weights_a, weights_b = gather_halves(split(pack))
    full_router = to_group(own_part(w_router), ("dp", "expert"), 32).reshape(D, EXPERTS)
    router = full_router.T
    routes = expert_routes.T
    all_routes = to_group(routes, ("expert", "dp"), 32)
    own_up = lax.all_to_all(w_gate_up, "dp", split_axis=0, concat_axis=0, tiled=True)
    own_down = lax.all_to_all(w_down, "dp", split_axis=0, concat_axis=0, tiled=True)
    cot_a, cot_b = gather_halves(split(out_cotangent))

    cosine, signed = (jnp.asarray(t) for t in rope_constants(128))
    gain1, gain2 = first_gain[None, :], second_gain[None, :]
    saved = attention_forward(
        place, weights_a, weights_b, layer_input, segment_ids, gain1, gain2, cosine, signed
    )
    normed, inv1, query, keys, values, attended, lse, hidden, inv2, normed2 = saved
    tok_a, tok_b = gather_halves(normed2)

    def flat(pieces):
        return [p.reshape(1024, half) for p in pieces]

    mix_a, mix_b, back_a, back_b, d_gate, d_up, d_dn = expert_call(
        place,
        flat(tok_a),
        flat(tok_b),
        flat(cot_a),
        flat(cot_b),
        all_routes,
        router,
        own_up.reshape(D, 2 * F),
        own_down.reshape(F, D),
    )

    def deep(pieces):
        return [p.reshape(2, 4, 128, half) for p in pieces]

    back = scatter_halves(deep(back_a), deep(back_b))
    d_gates = lax.all_to_all(
        d_gate, ("expert", "dp"), split_axis=0, concat_axis=0, tiled=True
    ).reshape(EXPERTS, 128)
    grads_a, grads_b, input_grad, d_gains, d_router = attention_backward(
        place,
        weights_a,
        weights_b,
        layer_input,
        segment_ids[None, :],
        segment_ids[:, None],
        gain1,
        gain2,
        cosine,
        signed,
        normed,
        inv1,
        query,
        keys,
        values,
        attended,
        lse,
        hidden,
        inv2,
        normed2,
        out_cotangent,
        back,
        d_gates,
        routes,
        router,
    )
    gate_up_grad = lax.all_to_all(
        d_up.reshape(4, 256, 2 * F), "dp", split_axis=0, concat_axis=0, tiled=True
    ).astype(jnp.float32)
    down_grad = lax.all_to_all(
        d_dn.reshape(4, 128, D), "dp", split_axis=0, concat_axis=0, tiled=True
    ).astype(jnp.float32)

    mixed = jnp.sum(scatter_halves(deep(mix_a), deep(mix_b)).astype(jnp.float32), axis=0)
    layer_output = (hidden + residual_scale * joined(mixed)).astype(jnp.bfloat16)

    summed = jnp.sum(scatter_halves(grads_a, grads_b).astype(jnp.float32), axis=0)
    summed = to_group(summed.astype(jnp.bfloat16), "expert", 8)
    summed = summed.reshape(8, 2, 3, 32, half).transpose(2, 0, 3, 1, 4).reshape(3, 256, D)
    query_grad, keyvalue_grad, output_grad = (summed[i].astype(jnp.float32) for i in range(3))

    small = jnp.concatenate(
        [
            jnp.broadcast_to(d_gains.reshape(1, 2 * D), (32, 2 * D)),
            d_router.reshape(EXPERTS, 32, 32).transpose(1, 2, 0).reshape(32, D),
        ],
        axis=1,
    )
    small = lax.all_to_all(small, ("dp", "expert"), split_axis=0, concat_axis=0, tiled=True)
    small = jnp.sum(small, axis=0)
    first_gain_grad, second_gain_grad = small[:D], small[D : 2 * D]
    router_grad = to_group(small[2 * D :].reshape(32, EXPERTS), "expert", 8).reshape(256, EXPERTS)
    return (
        layer_output,
        input_grad,
        first_gain_grad,
        query_grad,
        keyvalue_grad,
        output_grad,
        second_gain_grad,
        router_grad,
        gate_up_grad,
        down_grad,
    )


def solution(mesh):
    sizes = (mesh.shape["dp"], mesh.shape["expert"])
    return jax.shard_map(
        block_device if sizes == (4, 8) else general_device,
        mesh=mesh,
        in_specs=(
            P(("dp", "expert"), None),
            P(("dp", "expert")),
            P(("dp", "expert"), None),
            P(),
            P("dp", None),
            P("dp", None),
            P("dp", None),
            P(),
            P("dp", None),
            P("expert", "dp", None),
            P("expert", "dp", None),
            P(("dp", "expert"), None),
        ),
        out_specs=(
            P(("dp", "expert"), None),
            P(("dp", "expert"), None),
            P(),
            P("dp", None),
            P("dp", None),
            P("dp", None),
            P(),
            P("dp", None),
            P("expert", "dp", None),
            P("expert", "dp", None),
        ),
        check_vma=False,
    )
```

```python
import jax
import jax.numpy as jnp
import numpy as np
from jax import lax
from jax.experimental import pallas as pl
from jax.experimental.pallas import tpu as pltpu
from jax.sharding import PartitionSpec as P

D = 1024
HEADS = 16
KV_HEADS = 8
HEAD_DIM = 64
F = 512
EXPERTS = 32
TOPK = 8
CAP = 40


epsilon = 1e-06
residual_scale = 0.22
score_scale = 0.015625
rope_base = 10000.0


def rope_tables(length, head_width):
    halfway = head_width // 2
    frequency = jnp.exp(
        -jnp.log(rope_base) * (2.0 * jnp.arange(halfway, dtype=jnp.float32) / head_width)
    )
    angles = jnp.arange(length, dtype=jnp.float32)[:, None] * frequency[None, :]
    cosine = jnp.concatenate([jnp.cos(angles), jnp.cos(angles)], axis=1)
    sine_table = jnp.concatenate([jnp.sin(angles), jnp.sin(angles)], axis=1)
    return (cosine, sine_table)


def rotate(values, cosine, sine_table, direction):
    halfway = values.shape[-1] // 2
    turned = jnp.concatenate([-values[..., halfway:], values[..., :halfway]], axis=-1)
    return values * cosine[:, None, :] + direction * turned * sine_table[:, None, :]


def norm_forward(inputs_f32, gain_vector):
    inverse = lax.rsqrt(jnp.mean(inputs_f32 * inputs_f32, axis=-1, keepdims=True) + epsilon)
    return (inputs_f32 * inverse * gain_vector, inverse)


def norm_backward(inputs_f32, inverse, gain_vector, upstream):
    weighted = upstream * gain_vector
    gain_part = jnp.sum(upstream * inputs_f32 * inverse, axis=0)
    through = inverse * weighted - inputs_f32 * (inverse * inverse * inverse) * jnp.mean(
        weighted * inputs_f32, axis=-1, keepdims=True
    )
    return (gain_part, through)


def activate(pre_act):
    gate_half = pre_act[..., :F]
    up_half = pre_act[..., F:]
    return gate_half * jax.nn.sigmoid(gate_half) * up_half


def activate_backward(pre_act, d_act):
    gate_half = pre_act[..., :F]
    up_half = pre_act[..., F:]
    sigmoid_gate = jax.nn.sigmoid(gate_half)
    d_gate = d_act * up_half * sigmoid_gate * (1.0 + gate_half * (1.0 - sigmoid_gate))
    d_up = d_act * gate_half * sigmoid_gate
    return jnp.concatenate([d_gate, d_up], axis=-1)


def masked_scores(query, keys, visible):
    raw_scores = (
        jnp.einsum("qkgd,pkd->kgqp", query, keys, preferred_element_type=jnp.float32) * score_scale
    )
    return jnp.where(visible[None, None], raw_scores, -1e30)


def attend_forward(normed, full_query, full_keyvalue, visible, cosine, sine_table):
    length = normed.shape[0]
    per_group = HEADS // KV_HEADS
    query_raw = jnp.dot(normed, full_query, preferred_element_type=jnp.float32).reshape(
        length, HEADS, HEAD_DIM
    )
    keyval = jnp.dot(normed, full_keyvalue, preferred_element_type=jnp.float32).reshape(
        length, 2, KV_HEADS, HEAD_DIM
    )
    query = (
        rotate(query_raw, cosine, sine_table, 1.0)
        .astype(jnp.bfloat16)
        .reshape(length, KV_HEADS, per_group, HEAD_DIM)
    )
    keys = rotate(keyval[:, 0], cosine, sine_table, 1.0).astype(jnp.bfloat16)
    values = keyval[:, 1].astype(jnp.bfloat16)
    scores = masked_scores(query, keys, visible)
    highest = jnp.max(scores, axis=-1, keepdims=True)
    log_total = highest + jnp.log(jnp.sum(jnp.exp(scores - highest), axis=-1, keepdims=True))
    probabilities = jnp.exp(scores - log_total).astype(jnp.bfloat16)
    attended = jnp.einsum(
        "kgqp,pkd->qkgd", probabilities, values, preferred_element_type=jnp.float32
    )
    attended = attended.reshape(length, HEADS * HEAD_DIM).astype(jnp.bfloat16)
    return (query, keys, values, attended, log_total)


def attend_backward(query, keys, values, attended, log_total, d_attended, visible):
    length = query.shape[0]
    per_group = HEADS // KV_HEADS
    scores = masked_scores(query, keys, visible)
    probs_f32 = jnp.exp(scores - log_total)
    probs_half = probs_f32.astype(jnp.bfloat16)
    d_att4 = d_attended.reshape(length, KV_HEADS, per_group, HEAD_DIM)
    att_four = attended.reshape(length, KV_HEADS, per_group, HEAD_DIM)
    d_values = jnp.einsum("kgqp,qkgd->pkd", probs_half, d_att4, preferred_element_type=jnp.float32)
    d_probs = jnp.einsum("qkgd,pkd->kgqp", d_att4, values, preferred_element_type=jnp.float32)
    row_delta = jnp.einsum("qkgd,qkgd->kgq", d_att4, att_four, preferred_element_type=jnp.float32)
    d_scores = (probs_f32 * (d_probs - row_delta[..., None]) * score_scale).astype(jnp.bfloat16)
    d_query = jnp.einsum(
        "kgqp,pkd->qkgd", d_scores, keys, preferred_element_type=jnp.float32
    ).reshape(length, HEADS, HEAD_DIM)
    d_keys = jnp.einsum("kgqp,qkgd->pkd", d_scores, query, preferred_element_type=jnp.float32)
    return (d_query, d_keys, d_values)


DP, EX = "dp", "expert"


def butterfly_sum(value, axes):
    for axis in axes:
        size = lax.axis_size(axis)
        step = 1
        while step < size:
            value = value + lax.ppermute(value, axis, [(i, i ^ step) for i in range(size)])
            step *= 2
    return value


def spread_over(axes, array):
    for axis in reversed(axes):
        array = lax.all_gather(array, axis, axis=0, tiled=True)
    return array


def sum_to_owner(axes, array):
    for axis in axes:
        array = lax.psum_scatter(array, axis, scatter_dimension=0, tiled=True)
    return array


def expert_pass(tokens, cotangents, gate, hit, w_up, w_dn):
    blocks = tokens.shape[0] // 128
    ranking = jnp.cumsum(hit.reshape(blocks, 128).astype(jnp.int32), axis=1) - 1
    slot = jnp.where(hit.reshape(blocks, 128), ranking, -1)
    select = slot[:, None, :] == jnp.arange(CAP, dtype=jnp.int32)[None, :, None]
    onehot = select.astype(jnp.bfloat16)
    rows = blocks * CAP
    picked = jnp.einsum(
        "bst,btd->bsd", onehot, tokens.reshape(blocks, 128, D), preferred_element_type=jnp.float32
    ).astype(jnp.bfloat16).reshape(rows, D)
    cot = jnp.einsum(
        "bst,btd->bsd",
        onehot,
        cotangents.reshape(blocks, 128, D),
        preferred_element_type=jnp.float32,
    ).reshape(rows, D)
    gate_slot = jnp.sum(
        jnp.where(select, gate.reshape(blocks, 1, 128), 0.0), axis=2
    ).reshape(rows, 1)
    pre_act = jnp.dot(picked, w_up, preferred_element_type=jnp.float32)
    activated = activate(pre_act).astype(jnp.bfloat16)
    result = (
        jnp.dot(activated, w_dn, preferred_element_type=jnp.float32)
        .astype(jnp.bfloat16)
        .astype(jnp.float32)
    )
    d_gate_slot = residual_scale * jnp.sum(cot * result, axis=1)
    d_gate = jnp.sum(jnp.where(select, d_gate_slot.reshape(blocks, CAP, 1), 0.0), axis=1)
    gated = (gate_slot * result).astype(jnp.bfloat16)
    mixed = jnp.einsum(
        "bst,bsd->btd", onehot, gated.reshape(blocks, CAP, D), preferred_element_type=jnp.float32
    ).reshape(blocks * 128, D)
    d_result = (residual_scale * gate_slot * cot).astype(jnp.bfloat16)
    d_act = jnp.dot(d_result, w_dn.T, preferred_element_type=jnp.float32)
    d_down = jnp.dot(activated.T, d_result, preferred_element_type=jnp.float32)
    d_pre = activate_backward(pre_act, d_act).astype(jnp.bfloat16)
    d_up = jnp.dot(picked.T, d_pre, preferred_element_type=jnp.float32)
    d_rows = jnp.dot(d_pre, w_up.T, preferred_element_type=jnp.float32).astype(jnp.bfloat16)
    back = jnp.einsum(
        "bst,bsd->btd", onehot, d_rows.reshape(blocks, CAP, D), preferred_element_type=jnp.float32
    ).reshape(blocks * 128, D)
    return (mixed, back, d_gate.reshape(blocks * 128), d_up, d_down)


def general_device(
    layer_input,
    segment_ids,
    expert_routes,
    first_gain,
    w_query,
    w_keyvalue,
    w_output,
    second_gain,
    w_router,
    w_gate_up,
    w_down,
    out_cotangent,
):
    length = layer_input.shape[0]
    owners = lax.axis_size(EX)
    groups = lax.axis_size(DP)
    group_at = lax.axis_index(DP)
    owner_at = lax.axis_index(EX)
    per_owner = w_gate_up.shape[0]
    shard = w_query.shape[0]
    part = shard // owners
    every = (DP, EX)

    def own_part(weight):
        return lax.dynamic_slice_in_dim(weight, owner_at * part, part, 0)

    pack = jnp.concatenate([own_part(w_query), own_part(w_keyvalue), own_part(w_output)], axis=0)
    gathered = lax.all_gather(pack, every, axis=0).reshape(groups * owners, 3, part, D)
    full_query = gathered[:, 0].reshape(D, HEADS * HEAD_DIM)
    full_keyvalue = gathered[:, 1].reshape(D, 2 * KV_HEADS * HEAD_DIM)
    full_output = gathered[:, 2].reshape(HEADS * HEAD_DIM, D)
    full_router = lax.all_gather(own_part(w_router), every, axis=0, tiled=True)

    exchange = per_owner % groups == 0
    if exchange:
        local = per_owner // groups
        token_axes = (EX, DP)
        first_expert = owner_at * per_owner + group_at * local
        own_up = lax.all_to_all(w_gate_up, DP, split_axis=0, concat_axis=1, tiled=True)
        own_down = lax.all_to_all(w_down, DP, split_axis=0, concat_axis=1, tiled=True)
    else:
        local = per_owner
        token_axes = (EX,)
        first_expert = owner_at * per_owner
        own_up = lax.all_gather(w_gate_up, DP, axis=1, tiled=True)
        own_down = lax.all_gather(w_down, DP, axis=1, tiled=True)
    all_routes = spread_over(token_axes, expert_routes)
    all_cotangents = spread_over(token_axes, out_cotangent)

    cosine, sine_table = rope_tables(length, HEAD_DIM)
    places = jnp.arange(length)
    visible = (places[:, None] >= places[None, :]) & (segment_ids[:, None] == segment_ids[None, :])
    inputs_f32 = layer_input.astype(jnp.float32)
    normed, inverse = norm_forward(inputs_f32, first_gain)
    normed = normed.astype(jnp.bfloat16)
    query, keys, values, attended, log_total = attend_forward(
        normed, full_query, full_keyvalue, visible, cosine, sine_table
    )
    hidden = inputs_f32 + residual_scale * jnp.dot(
        attended, full_output, preferred_element_type=jnp.float32
    )
    normed2, inverse2 = norm_forward(hidden, second_gain)
    normed2 = normed2.astype(jnp.bfloat16)
    all_normed2 = spread_over(token_axes, normed2)

    def gates_of(rows, routes):
        named = jnp.any(
            routes[:, :, None] == jnp.arange(EXPERTS, dtype=jnp.int32)[None, None, :], axis=1
        )
        logits = jnp.dot(rows, full_router, preferred_element_type=jnp.float32)
        highest = jnp.max(jnp.where(named, logits, -jnp.inf), axis=1, keepdims=True)
        exponent = jnp.where(named, jnp.exp(jnp.where(named, logits - highest, 0.0)), 0.0)
        return exponent / jnp.sum(exponent, axis=1, keepdims=True)

    all_gates = gates_of(all_normed2, all_routes)
    d_out = out_cotangent.astype(jnp.float32)
    mixed, back = 0.0, 0.0
    d_gate_list, up_list, down_list = [], [], []
    for j in range(local):
        hit = jnp.any(all_routes == first_expert + j, axis=1)
        gate = lax.dynamic_index_in_dim(all_gates, first_expert + j, 1, keepdims=False)
        one_mixed, one_back, d_gate, d_up, d_dn = expert_pass(
            all_normed2, all_cotangents, gate, hit, own_up[j], own_down[j]
        )
        mixed, back = mixed + one_mixed, back + one_back
        d_gate_list.append(d_gate)
        up_list.append(d_up.astype(jnp.bfloat16))
        down_list.append(d_dn.astype(jnp.bfloat16))
    back_own = sum_to_owner(token_axes, back.astype(jnp.bfloat16)).astype(jnp.float32)
    sources = EXPERTS // local
    d_gate_out = jnp.stack(d_gate_list).reshape(local, sources, length).transpose(1, 0, 2)
    d_gates = (
        lax.all_to_all(d_gate_out, token_axes, split_axis=0, concat_axis=0, tiled=True)
        .reshape(EXPERTS, length)
        .T
    )
    d_up_all, d_down_all = jnp.stack(up_list), jnp.stack(down_list)
    if exchange:
        gate_up_grad = lax.all_to_all(d_up_all, DP, split_axis=1, concat_axis=0, tiled=True)
        down_grad = lax.all_to_all(d_down_all, DP, split_axis=1, concat_axis=0, tiled=True)
    else:
        gate_up_grad = lax.psum_scatter(d_up_all, DP, scatter_dimension=1, tiled=True)
        down_grad = lax.psum_scatter(d_down_all, DP, scatter_dimension=1, tiled=True)
    mixed_own = sum_to_owner(token_axes, mixed.astype(jnp.bfloat16)).astype(jnp.float32)
    layer_output = (hidden + residual_scale * mixed_own).astype(jnp.bfloat16)

    gates = gates_of(normed2, expert_routes)
    d_logits = (gates * (d_gates - jnp.sum(gates * d_gates, axis=1, keepdims=True))).astype(
        jnp.bfloat16
    )
    d_router = jnp.dot(normed2.T, d_logits, preferred_element_type=jnp.float32)
    d_normed2 = back_own + jnp.dot(d_logits, full_router.T, preferred_element_type=jnp.float32)
    d_second_gain, d_through = norm_backward(hidden, inverse2, second_gain, d_normed2)
    second_gain_grad = butterfly_sum(d_second_gain, (EX, DP))
    d_hidden = d_out + d_through
    d_branch = (residual_scale * d_hidden).astype(jnp.bfloat16)
    d_wout = jnp.dot(attended.T, d_branch, preferred_element_type=jnp.float32)
    d_attended = jnp.dot(d_branch, full_output.T, preferred_element_type=jnp.float32).astype(
        jnp.bfloat16
    )
    d_query, d_keys, d_values = attend_backward(
        query, keys, values, attended, log_total, d_attended, visible
    )
    d_query = (
        rotate(d_query, cosine, sine_table, -1.0)
        .reshape(length, HEADS * HEAD_DIM)
        .astype(jnp.bfloat16)
    )
    d_keys = rotate(d_keys, cosine, sine_table, -1.0)
    d_keyvalue = (
        jnp.stack([d_keys, d_values], axis=1)
        .reshape(length, 2 * KV_HEADS * HEAD_DIM)
        .astype(jnp.bfloat16)
    )
    d_wquery = jnp.dot(normed.T, d_query, preferred_element_type=jnp.float32)
    d_wkeyvalue = jnp.dot(normed.T, d_keyvalue, preferred_element_type=jnp.float32)
    d_normed = jnp.dot(d_query, full_query.T, preferred_element_type=jnp.float32) + jnp.dot(
        d_keyvalue, full_keyvalue.T, preferred_element_type=jnp.float32
    )
    d_first_gain, d_inputs = norm_backward(inputs_f32, inverse, first_gain, d_normed)
    first_gain_grad = butterfly_sum(d_first_gain, (EX, DP))
    input_grad = (d_hidden + d_inputs).astype(jnp.bfloat16)

    def reduced(*grads):
        packed = jnp.stack([g.astype(jnp.bfloat16) for g in grads])
        count, width = len(grads), grads[0].shape[1]
        packed = packed.reshape(count, groups, owners, part, width).transpose(2, 1, 0, 3, 4)
        packed = packed.reshape(owners * groups * count * part, width)
        mine = sum_to_owner((EX, DP), packed).reshape(1, count, part, width)
        whole = lax.all_gather(mine, EX, axis=0, tiled=True)
        whole = whole.transpose(1, 0, 2, 3).reshape(count, owners * part, width)
        return [whole[i].astype(jnp.float32) for i in range(count)]

    output_grad, query_grad, keyvalue_grad = reduced(d_wout, d_wquery, d_wkeyvalue)
    (router_grad,) = reduced(d_router)
    return (
        layer_output,
        input_grad,
        first_gain_grad,
        query_grad,
        keyvalue_grad,
        output_grad,
        second_gain_grad,
        router_grad,
        gate_up_grad.astype(jnp.float32),
        down_grad.astype(jnp.float32),
    )


def expert_kernel(*refs):
    tok_a, tok_b, cot_a, cot_b = refs[0:4], refs[4:8], refs[8:12], refs[12:16]
    up_pieces, down_pieces = refs[16:20], refs[20:24]
    routes_ref, router_ref = refs[24:26]
    mix_a, mix_b, back_a, back_b = refs[26:30], refs[30:34], refs[34:38], refs[38:42]
    d_up_pieces, d_down_pieces = refs[42:46], refs[46:50]
    dgate_ref = refs[50]
    (
        tok_buf,
        cot_buf,
        mix_buf,
        back_buf,
        rows_scr,
        act_scr,
        dres_scr,
        dpre_scr,
        cot_scr,
        gate_scr,
        slot_scr,
        tri_scr,
        up_scr,
        down_scr,
        d_up_scr,
        d_down_scr,
        in_sem,
        out_sem,
        weight_sem,
        grad_sem,
    ) = refs[51:]
    half = D // 2
    owner, group = lax.axis_index(EX), lax.axis_index(DP)
    expert = owner * 4 + group
    chunk_rows = 8 * CAP

    def chunk_copies(kk, slot, sources, sem, outward):
        c, y = kk // 2, kk % 2
        ends = []
        for a, b, buf in sources:
            ends.append((a[kk], buf.at[slot, :, pl.ds(0, half)]))
            for x in range(2):
                ends.append(
                    (
                        b[2 * c + x].at[pl.ds(512 * y, 512), :],
                        buf.at[slot, pl.ds(512 * x, 512), pl.ds(half, half)],
                    )
                )
        if outward:
            ends = [(there, here) for here, there in ends]
        return [
            pltpu.make_async_copy(*pair, sem.at[slot, i]) for i, pair in enumerate(ends)
        ]

    def in_copies(kk, slot):
        sources = ((tok_a, tok_b, tok_buf), (cot_a, cot_b, cot_buf))
        return chunk_copies(kk, slot, sources, in_sem, False)

    def out_copies(kk, slot):
        sources = ((back_a, back_b, back_buf), (mix_a, mix_b, mix_buf))
        return chunk_copies(kk, slot, sources, out_sem, True)

    def weight_pairs():
        found = []
        for s in range(4):
            at = jnp.bitwise_xor(group, s)
            up_from = up_pieces[s].at[group] if s == 0 else up_pieces[s]
            down_from = down_pieces[s].at[group] if s == 0 else down_pieces[s]
            found.append(pltpu.make_async_copy(up_from, up_scr.at[at], weight_sem.at[0, s]))
            found.append(pltpu.make_async_copy(down_from, down_scr.at[at], weight_sem.at[1, s]))
        return found

    for copy in in_copies(0, 0) + weight_pairs():
        copy.start()
    before = lax.broadcasted_iota(jnp.int32, (256, 256), 0)
    after = lax.broadcasted_iota(jnp.int32, (256, 256), 1)
    tri_scr[...] = ((before <= after) & ((before < 128) == (after < 128))).astype(jnp.bfloat16)

    def pair_mask(pair):
        return slot_scr[pair] == lax.broadcasted_iota(jnp.int32, (2 * CAP, 256), 0)

    def chunk_step(k, carry):
        for kk in range(4):

            @pl.when(k == kk)
            def _():
                if kk < 3:
                    for copy in in_copies(kk + 1, (kk + 1) % 2):
                        copy.start()
                for copy in in_copies(kk, kk % 2):
                    copy.wait()
                if kk >= 2:
                    for copy in out_copies(kk - 2, kk % 2):
                        copy.wait()

        at = lax.rem(k, 2)
        base = pl.multiple_of(k * chunk_rows, chunk_rows)
        away = k // 2 + 4 * lax.rem(k, 2)
        for pair in range(4):
            device = jnp.bitwise_xor(owner, away + 2 * (pair // 2)) * 4 + 2 * (pair % 2)
            routes = jnp.concatenate([routes_ref[device], routes_ref[device + 1]], axis=1)
            hit = jnp.max((routes == expert).astype(jnp.float32), axis=0, keepdims=True)
            rank = jnp.dot(
                jnp.broadcast_to(hit, (16, 256)).astype(jnp.bfloat16),
                tri_scr[...],
                preferred_element_type=jnp.float32,
            )[0:1]
            second = lax.broadcasted_iota(jnp.int32, (1, 256), 1) >= 128
            slot = rank.astype(jnp.int32) - 1 + jnp.where(second, CAP, 0)
            slot_scr[pair] = jnp.where(hit > 0.5, slot, -1)
            mask = pair_mask(pair)
            onehot = mask.astype(jnp.bfloat16)
            token_rows = tok_buf[at, pl.ds(256 * pair, 256), :]
            logits = lax.dot_general(
                router_ref[...],
                token_rows,
                (((1,), (1,)), ((), ())),
                preferred_element_type=jnp.float32,
            )
            names = lax.broadcasted_iota(jnp.int32, (EXPERTS, 256), 0)
            named = routes[0:1] == names
            for i in range(1, TOPK):
                named = named | (routes[i : i + 1] == names)
            highest = jnp.max(jnp.where(named, logits, -3e38), axis=0, keepdims=True)
            exponent = jnp.where(named, jnp.exp(jnp.where(named, logits - highest, 0.0)), 0.0)
            own = jnp.sum(jnp.where(names == expert, exponent, 0.0), axis=0, keepdims=True)
            gate = own / jnp.sum(exponent, axis=0, keepdims=True)
            gate_slot = jnp.sum(jnp.where(mask, gate, 0.0), axis=1, keepdims=True)
            gate_scr[pl.ds(2 * CAP * pair, 2 * CAP), :] = gate_slot
            place = pl.ds(base + 2 * CAP * pair, 2 * CAP)
            rows_scr[place, :] = jnp.dot(
                onehot, token_rows, preferred_element_type=jnp.float32
            ).astype(jnp.bfloat16)
            cot = jnp.dot(
                onehot, cot_buf[at, pl.ds(256 * pair, 256), :], preferred_element_type=jnp.float32
            )
            cot_scr[pl.ds(2 * CAP * pair, 2 * CAP), :] = cot.astype(jnp.bfloat16)
            dres_scr[place, :] = (residual_scale * gate_slot * cot).astype(jnp.bfloat16)

        @pl.when(k == 0)
        def _():
            for copy in weight_pairs():
                copy.wait()

        here = pl.ds(base, chunk_rows)
        pre = jnp.dot(rows_scr[here, :], up_scr[...].reshape(D, 2 * F), preferred_element_type=jnp.float32)
        gate_half, up_half = pre[:, :F], pre[:, F:]
        sigmoid_gate = 1.0 / (1.0 + jnp.exp(-gate_half))
        swish = gate_half * sigmoid_gate
        activated = (swish * up_half).astype(jnp.bfloat16)
        act_scr[here, :] = activated
        d_act = lax.dot_general(
            dres_scr[here, :],
            down_scr[...].reshape(F, D),
            (((1,), (1,)), ((), ())),
            preferred_element_type=jnp.float32,
        )
        dpre_scr[here, 0:F] = (
            d_act * up_half * sigmoid_gate * (1.0 + gate_half * (1.0 - sigmoid_gate))
        ).astype(jnp.bfloat16)
        dpre_scr[here, F : 2 * F] = (d_act * swish).astype(jnp.bfloat16)
        result = (
            jnp.dot(activated, down_scr[...].reshape(F, D), preferred_element_type=jnp.float32)
            .astype(jnp.bfloat16)
            .astype(jnp.float32)
        )
        d_gate_slot = residual_scale * jnp.sum(
            cot_scr[...].astype(jnp.float32) * result, axis=1, keepdims=True
        )
        gated = (gate_scr[...] * result).astype(jnp.bfloat16)
        d_rows = lax.dot_general(
            dpre_scr[here, :],
            up_scr[...].reshape(D, 2 * F),
            (((1,), (1,)), ((), ())),
            preferred_element_type=jnp.float32,
        ).astype(jnp.bfloat16)
        for pair in range(4):
            device = jnp.bitwise_xor(owner, away + 2 * (pair // 2)) * 4 + 2 * (pair % 2)
            mask = pair_mask(pair)
            onehot = mask.astype(jnp.bfloat16)
            mine = slice(2 * CAP * pair, 2 * CAP * (pair + 1))
            d_gate = jnp.sum(jnp.where(mask, d_gate_slot[mine], 0.0), axis=0, keepdims=True)
            dgate_ref[device] = d_gate[:, :128]
            dgate_ref[device + 1] = d_gate[:, 128:]
            rows = pl.ds(256 * pair, 256)
            mix_buf[at, rows, :] = lax.dot_general(
                onehot,
                gated[mine],
                (((0,), (0,)), ((), ())),
                preferred_element_type=jnp.float32,
            ).astype(jnp.bfloat16)
            back_buf[at, rows, :] = lax.dot_general(
                onehot,
                d_rows[mine],
                (((0,), (0,)), ((), ())),
                preferred_element_type=jnp.float32,
            ).astype(jnp.bfloat16)
        for kk in range(4):

            @pl.when(k == kk)
            def _():
                for copy in out_copies(kk, kk % 2):
                    copy.start()

        return carry

    lax.fori_loop(0, 4, chunk_step, 0)

    def up_step(t, carry):
        at = jnp.bitwise_xor(group, t)
        d_up_scr[t] = lax.dot_general(
            rows_scr[:, pl.ds(pl.multiple_of(at * 256, 256), 256)],
            dpre_scr[...],
            (((0,), (0,)), ((), ())),
            preferred_element_type=jnp.float32,
        ).astype(jnp.bfloat16)
        d_down_scr[t] = lax.dot_general(
            act_scr[:, pl.ds(pl.multiple_of(at * 128, 128), 128)],
            dres_scr[...],
            (((0,), (0,)), ((), ())),
            preferred_element_type=jnp.float32,
        ).astype(jnp.bfloat16)
        for s in range(4):

            @pl.when(t == s)
            def _():
                for copy in grad_copies(s):
                    copy.start()

        return carry

    def grad_copies(s):
        return (
            pltpu.make_async_copy(d_up_scr.at[s], d_up_pieces[s], grad_sem.at[0, s]),
            pltpu.make_async_copy(d_down_scr.at[s], d_down_pieces[s], grad_sem.at[1, s]),
        )

    lax.fori_loop(0, 4, up_step, 0)
    for kk in (2, 3):
        for copy in out_copies(kk, kk % 2):
            copy.wait()
    for s in range(4):
        for copy in grad_copies(s):
            copy.wait()


def expert_call(tok_a, tok_b, cot_a, cot_b, up_pieces, down_pieces, routes, router):
    half = D // 2
    token_count = 1024
    hbm = pl.BlockSpec(memory_space=pltpu.HBM)
    vmem = pl.BlockSpec(memory_space=pltpu.VMEM)
    slots = 32 * CAP
    b16 = jnp.bfloat16
    piece = jax.ShapeDtypeStruct((token_count, half), b16)
    outs = pl.pallas_call(
        expert_kernel,
        in_specs=[hbm] * 24 + [vmem] * 2,
        out_specs=[hbm] * 24 + [vmem],
        out_shape=[piece] * 16
        + [jax.ShapeDtypeStruct((256, 2 * F), b16)] * 4
        + [jax.ShapeDtypeStruct((128, D), b16)] * 4
        + [jax.ShapeDtypeStruct((32, 1, 128), jnp.float32)],
        scratch_shapes=[pltpu.VMEM((2, token_count, D), b16)] * 4
        + [
            pltpu.VMEM((slots, D), b16),
            pltpu.VMEM((slots, F), b16),
            pltpu.VMEM((slots, D), b16),
            pltpu.VMEM((slots, 2 * F), b16),
            pltpu.VMEM((8 * CAP, D), b16),
            pltpu.VMEM((8 * CAP, 1), jnp.float32),
            pltpu.VMEM((4, 1, 256), jnp.int32),
            pltpu.VMEM((256, 256), b16),
            pltpu.VMEM((4, 256, 2 * F), b16),
            pltpu.VMEM((4, 128, D), b16),
            pltpu.VMEM((4, 256, 2 * F), b16),
            pltpu.VMEM((4, 128, D), b16),
            pltpu.SemaphoreType.DMA((2, 6)),
            pltpu.SemaphoreType.DMA((2, 6)),
            pltpu.SemaphoreType.DMA((2, 4)),
            pltpu.SemaphoreType.DMA((2, 4)),
        ],
        compiler_params=pltpu.CompilerParams(vmem_limit_bytes=48 * 1024 * 1024),
    )(*tok_a, *tok_b, *cot_a, *cot_b, *up_pieces, *down_pieces, routes, router)
    groups = [outs[4 * i : 4 * i + 4] for i in range(6)]
    return (*groups, outs[24])


def rope_constants(length):
    frequency = rope_base ** (-2.0 * np.arange(HEAD_DIM // 2) / HEAD_DIM)
    angles = np.arange(length)[:, None] * frequency[None, :]
    cosine = np.tile(np.cos(angles), (1, 4)).astype(np.float32)
    sine = np.sin(angles)
    signed = np.concatenate([-sine, sine, -sine, sine], axis=1).astype(np.float32)
    return cosine, signed


def turn(slab, cosine, signed):
    low = (lax.broadcasted_iota(jnp.int32, slab.shape, 1) & 32) == 0
    swapped = jnp.where(low, pltpu.roll(slab, 96, 1), pltpu.roll(slab, 32, 1))
    return slab * cosine + swapped * signed


def halves_stacked(slab, low):
    zero = jnp.zeros_like(slab)
    return jnp.concatenate([jnp.where(low, slab, zero), jnp.where(low, zero, slab)], axis=0)


def doubled(slab, low, second):
    other = pltpu.roll(slab, 64, 1)
    return jnp.where(low, other, slab) if second else jnp.where(low, slab, other)


def weight_copies(pieces_a, pieces_b, whole, sems, owner, kind, outward):
    half = D // 2
    copies = []
    for rel in range(8):
        c, x, y = rel & 1, (rel >> 1) & 1, (rel >> 2) & 1
        at = jnp.bitwise_xor(owner, rel)
        rows = pl.ds(32 * kind, 32)
        ends = (
            (pieces_a[2 * c + y].at[x, :, rows, :], whole.at[kind, :, at, :, pl.ds(0, half)]),
            (pieces_b[2 * c + x].at[y, :, rows, :], whole.at[kind, :, at, :, pl.ds(half, half)]),
        )
        for i, (piece, place) in enumerate(ends):
            pair = (place, piece) if outward else (piece, place)
            copies.append(pltpu.make_async_copy(*pair, sems.at[kind, rel, i]))
    return copies


def packed_views(pack_ref):
    starts = (0, D, 2 * D, 2 * D + D // 2, 3 * D, 4 * D)
    return [pack_ref.at[:, pl.ds(a, b - a)] for a, b in zip(starts[:-1], starts[1:])]


def attention_forward_kernel(*refs):
    pieces_a, pieces_b = refs[0:4], refs[4:8]
    x_ref, seg_row, seg_col, gain_ref, rope_ref = refs[8:13]
    finals = refs[13:17]
    pack_ref, hidden_ref, small_ref, normed2_ref, whole, sems, out_sems = refs[17:]
    outs = [
        pltpu.make_async_copy(here, there, out_sems.at[i])
        for i, (here, there) in enumerate(zip(refs[17:21], finals))
    ]
    normed_ref, q_ref, k_ref, v_ref, att_ref = packed_views(pack_ref)
    owner = lax.axis_index(EX)
    half = D // 2
    for kind in range(3):
        for copy in weight_copies(pieces_a, pieces_b, whole, sems, owner, kind, False):
            copy.start()
    inputs = x_ref[...].astype(jnp.float32)
    inverse = lax.rsqrt(jnp.mean(inputs * inputs, axis=1, keepdims=True) + epsilon)
    normed = (inputs * inverse * gain_ref[0:1, :]).astype(jnp.bfloat16)
    normed_ref[...] = normed
    small_ref[:128, 8:9] = inverse
    small_ref[:128, 10:11] = seg_col[...].astype(jnp.float32)
    cosine, signed = rope_ref[0], rope_ref[1]
    for kind in range(2):
        for copy in weight_copies(pieces_a, pieces_b, whole, sems, owner, kind, False):
            copy.wait()
    query = jnp.dot(normed, whole[0].reshape(D, D), preferred_element_type=jnp.float32)
    keyval = jnp.dot(normed, whole[1].reshape(D, D), preferred_element_type=jnp.float32)
    for s in range(8):
        cols = slice(128 * s, 128 * s + 128)
        q_ref[:, cols] = turn(query[:, cols], cosine, signed).astype(jnp.bfloat16)
    for s in range(4):
        cols = slice(128 * s, 128 * s + 128)
        k_ref[:, cols] = turn(keyval[:, cols], cosine, signed).astype(jnp.bfloat16)
    v_ref[...] = keyval[:, half:].astype(jnp.bfloat16)
    rows_at = lax.broadcasted_iota(jnp.int32, (128, 128), 0)
    cols_at = lax.broadcasted_iota(jnp.int32, (128, 128), 1)
    visible = (rows_at >= cols_at) & (seg_col[...] == seg_row[...])
    visible2 = jnp.concatenate([visible, visible], axis=0)
    low = cols_at < 64
    for head in range(KV_HEADS):
        slab = slice(128 * (head // 2), 128 * (head // 2) + 128)
        q2 = halves_stacked(q_ref[:, 128 * head : 128 * head + 128], low)
        k2 = doubled(k_ref[:, slab], low, head % 2)
        v2 = doubled(v_ref[:, slab], low, head % 2)
        scores = lax.dot_general(
            q2, k2, (((1,), (1,)), ((), ())), preferred_element_type=jnp.float32
        )
        scores = jnp.where(visible2, scores * score_scale, -1e30)
        highest = jnp.max(scores, axis=1, keepdims=True)
        log_total = highest + jnp.log(jnp.sum(jnp.exp(scores - highest), axis=1, keepdims=True))
        probabilities = jnp.exp(scores - log_total).astype(jnp.bfloat16)
        small_ref[:, head : head + 1] = log_total
        mixed = jnp.dot(probabilities, v2, preferred_element_type=jnp.float32)
        att_ref[:, 128 * head : 128 * head + 128] = jnp.where(
            low, mixed[:128], mixed[128:]
        ).astype(jnp.bfloat16)
    for copy in weight_copies(pieces_a, pieces_b, whole, sems, owner, 2, False):
        copy.wait()
    outs[0].start()
    hidden = inputs + residual_scale * jnp.dot(
        att_ref[...], whole[2].reshape(D, D), preferred_element_type=jnp.float32
    )
    inverse2 = lax.rsqrt(jnp.mean(hidden * hidden, axis=1, keepdims=True) + epsilon)
    normed2 = (hidden * inverse2 * gain_ref[1:2, :]).astype(jnp.bfloat16)
    hidden_ref[...] = hidden
    small_ref[:128, 9:10] = inverse2
    outs[1].start()
    outs[2].start()
    for z in range(4):
        normed2_ref[z, 0] = normed2[:, :half]
        normed2_ref[z, 1] = normed2[:, half:]
    outs[3].start()
    for out in outs:
        out.wait()


def attention_forward(pieces_a, pieces_b, x, seg, gains, rope):
    hbm = pl.BlockSpec(memory_space=pltpu.HBM)
    vmem = pl.BlockSpec(memory_space=pltpu.VMEM)
    f32, b16 = jnp.float32, jnp.bfloat16
    shapes = [
        ((128, 4 * D), b16),
        ((128, D), f32),
        ((256, 16), f32),
        ((4, 2, 128, D // 2), b16),
    ]
    return pl.pallas_call(
        attention_forward_kernel,
        in_specs=[hbm] * 8 + [vmem] * 5,
        out_specs=[hbm] * 4,
        out_shape=[pltpu.HBM(s, t) for s, t in shapes],
        scratch_shapes=[pltpu.VMEM(s, t) for s, t in shapes]
        + [
            pltpu.VMEM((3, 4, 8, 32, D), b16),
            pltpu.SemaphoreType.DMA((3, 8, 2)),
            pltpu.SemaphoreType.DMA((4,)),
        ],
        compiler_params=pltpu.CompilerParams(vmem_limit_bytes=40 * 1024 * 1024),
    )(*pieces_a, *pieces_b, x, seg[None, :], seg[:, None], gains, rope)


def attention_backward_kernel(*refs):
    pieces_a, pieces_b = refs[0:4], refs[4:8]
    arrays = refs[8:20]
    grads_a, grads_b = refs[20:24], refs[24:28]
    finals = refs[28:31]
    buffers = refs[31:43]
    (
        x_ref,
        seg_row,
        gain_ref,
        rope_ref,
        pack_ref,
        hidden_ref,
        small_ref,
        dout_ref,
        back_ref,
        dgate_ref,
        routes_ref,
        router_ref,
    ) = buffers
    input_grad_ref, gains_ref, router_grad_ref = refs[43:46]
    whole, grad, datt_scr, dq_scr, dkv_scr, sems, out_sems, load_sems, last_sems = refs[46:]
    loads = [
        pltpu.make_async_copy(there, here, load_sems.at[i])
        for i, (there, here) in enumerate(zip(arrays, buffers))
    ]
    lasts = [
        pltpu.make_async_copy(here, there, last_sems.at[i])
        for i, (here, there) in enumerate(zip(refs[43:46], finals))
    ]
    for load in loads:
        load.start()
    normed_ref, q_ref, k_ref, v_ref, att_ref = packed_views(pack_ref)
    owner = lax.axis_index(EX)
    half = D // 2
    for kind in (2, 0, 1):
        for copy in weight_copies(pieces_a, pieces_b, whole, sems, owner, kind, False):
            copy.start()
    for load in loads:
        load.wait()
    hidden, inverse2 = hidden_ref[...], small_ref[:128, 9:10]
    normed2 = (hidden * inverse2 * gain_ref[1:2, :]).astype(jnp.bfloat16)
    names = lax.broadcasted_iota(jnp.int32, (EXPERTS, 128), 0)
    routes = routes_ref[...]
    named = routes[0:1] == names
    for i in range(1, TOPK):
        named = named | (routes[i : i + 1] == names)
    logits = lax.dot_general(
        router_ref[...], normed2, (((1,), (1,)), ((), ())), preferred_element_type=jnp.float32
    )
    highest = jnp.max(jnp.where(named, logits, -3e38), axis=0, keepdims=True)
    exponent = jnp.where(named, jnp.exp(jnp.where(named, logits - highest, 0.0)), 0.0)
    gates = exponent / jnp.sum(exponent, axis=0, keepdims=True)
    d_gates = dgate_ref[...]
    d_logits = (gates * (d_gates - jnp.sum(gates * d_gates, axis=0, keepdims=True))).astype(
        jnp.bfloat16
    )
    router_grad_ref[...] = jnp.dot(d_logits, normed2, preferred_element_type=jnp.float32)
    back = [
        sum(back_ref[z, i].astype(jnp.float32) for z in range(4)) for i in range(2)
    ]
    d_normed2 = jnp.concatenate(back, axis=1) + lax.dot_general(
        d_logits, router_ref[...], (((0,), (0,)), ((), ())), preferred_element_type=jnp.float32
    )
    gains_ref[1:2, :] = jnp.sum(d_normed2 * hidden * inverse2, axis=0, keepdims=True)
    weighted = d_normed2 * gain_ref[1:2, :]
    d_hidden = (
        dout_ref[...].astype(jnp.float32)
        + inverse2 * weighted
        - hidden
        * (inverse2 * inverse2 * inverse2)
        * jnp.mean(weighted * hidden, axis=1, keepdims=True)
    )
    d_branch = (residual_scale * d_hidden).astype(jnp.bfloat16)
    tn = (((0,), (0,)), ((), ()))
    nt = (((1,), (1,)), ((), ()))
    for z in range(4):
        grad[2, z] = (
            lax.dot_general(
                att_ref[:, 256 * z : 256 * z + 256], d_branch, tn, preferred_element_type=jnp.float32
            )
            .astype(jnp.bfloat16)
            .reshape(8, 32, D)
        )
    for copy in weight_copies(grads_a, grads_b, grad, out_sems, owner, 2, True):
        copy.start()
    for copy in weight_copies(pieces_a, pieces_b, whole, sems, owner, 2, False):
        copy.wait()
    datt_scr[...] = lax.dot_general(
        d_branch, whole[2].reshape(D, D), nt, preferred_element_type=jnp.float32
    ).astype(jnp.bfloat16)
    cosine, signed = rope_ref[0], -rope_ref[1]
    rows_at = lax.broadcasted_iota(jnp.int32, (128, 128), 0)
    cols_at = lax.broadcasted_iota(jnp.int32, (128, 128), 1)
    visible = (rows_at >= cols_at) & (
        small_ref[:128, 10:11] == seg_row[...].astype(jnp.float32)
    )
    visible2 = jnp.concatenate([visible, visible], axis=0)
    low = cols_at < 64
    keep_k = keep_v = None
    for head in range(KV_HEADS):
        cols = slice(128 * head, 128 * head + 128)
        slab = slice(128 * (head // 2), 128 * (head // 2) + 128)
        q2 = halves_stacked(q_ref[:, cols], low)
        k2 = doubled(k_ref[:, slab], low, head % 2)
        v2 = doubled(v_ref[:, slab], low, head % 2)
        d_att = datt_scr[:, cols]
        da2 = halves_stacked(d_att, low)
        scores = lax.dot_general(q2, k2, nt, preferred_element_type=jnp.float32)
        scores = jnp.where(visible2, scores * score_scale, -1e30)
        probs = jnp.exp(scores - small_ref[:, head : head + 1])
        d_value = lax.dot_general(
            probs.astype(jnp.bfloat16), da2, tn, preferred_element_type=jnp.float32
        )
        d_probs = lax.dot_general(da2, v2, nt, preferred_element_type=jnp.float32)
        product = d_att.astype(jnp.float32) * att_ref[:, cols].astype(jnp.float32)
        delta = jnp.sum(halves_stacked(product, low), axis=1, keepdims=True)
        d_scores = (probs * (d_probs - delta) * score_scale).astype(jnp.bfloat16)
        d_q2 = jnp.dot(d_scores, k2, preferred_element_type=jnp.float32)
        d_query = jnp.where(low, d_q2[:128], d_q2[128:])
        dq_scr[:, cols] = turn(d_query, cosine, signed).astype(jnp.bfloat16)
        d_key = lax.dot_general(d_scores, q2, tn, preferred_element_type=jnp.float32)
        d_key = d_key + pltpu.roll(d_key, 64, 1)
        d_value = d_value + pltpu.roll(d_value, 64, 1)
        if head % 2 == 0:
            keep_k, keep_v = d_key, d_value
        else:
            dkv_scr[:, slab] = turn(jnp.where(low, keep_k, d_key), cosine, signed).astype(
                jnp.bfloat16
            )
            dkv_scr[:, half + slab.start : half + slab.stop] = jnp.where(
                low, keep_v, d_value
            ).astype(jnp.bfloat16)
    for kind, source in ((0, dq_scr), (1, dkv_scr)):
        for z in range(4):
            grad[kind, z] = (
                lax.dot_general(
                    normed_ref[:, 256 * z : 256 * z + 256],
                    source[...],
                    tn,
                    preferred_element_type=jnp.float32,
                )
                .astype(jnp.bfloat16)
                .reshape(8, 32, D)
            )
        for copy in weight_copies(grads_a, grads_b, grad, out_sems, owner, kind, True):
            copy.start()
    for kind in range(2):
        for copy in weight_copies(pieces_a, pieces_b, whole, sems, owner, kind, False):
            copy.wait()
    d_normed = lax.dot_general(
        dq_scr[...], whole[0].reshape(D, D), nt, preferred_element_type=jnp.float32
    ) + lax.dot_general(
        dkv_scr[...], whole[1].reshape(D, D), nt, preferred_element_type=jnp.float32
    )
    inputs, inverse = x_ref[...].astype(jnp.float32), small_ref[:128, 8:9]
    gains_ref[0:1, :] = jnp.sum(d_normed * inputs * inverse, axis=0, keepdims=True)
    weighted = d_normed * gain_ref[0:1, :]
    input_grad_ref[...] = (
        d_hidden
        + inverse * weighted
        - inputs
        * (inverse * inverse * inverse)
        * jnp.mean(weighted * inputs, axis=1, keepdims=True)
    ).astype(jnp.bfloat16)
    for last in lasts:
        last.start()
    for kind in range(3):
        for copy in weight_copies(grads_a, grads_b, grad, out_sems, owner, kind, True):
            copy.wait()
    for last in lasts:
        last.wait()


def attention_backward(pieces_a, pieces_b, *rest):
    hbm = pl.BlockSpec(memory_space=pltpu.HBM)
    f32, b16 = jnp.float32, jnp.bfloat16
    piece = jax.ShapeDtypeStruct((2, 4, 96, D // 2), b16)
    shapes = [((128, D), b16), ((2, D), f32), ((EXPERTS, D), f32)]
    outs = pl.pallas_call(
        attention_backward_kernel,
        in_specs=[hbm] * (8 + len(rest)),
        out_specs=[hbm] * 11,
        out_shape=[piece] * 8 + [jax.ShapeDtypeStruct(*pair) for pair in shapes],
        scratch_shapes=[pltpu.VMEM(array.shape, array.dtype) for array in rest]
        + [pltpu.VMEM(*pair) for pair in shapes]
        + [
            pltpu.VMEM((3, 4, 8, 32, D), b16),
            pltpu.VMEM((3, 4, 8, 32, D), b16),
            pltpu.VMEM((128, D), b16),
            pltpu.VMEM((128, D), b16),
            pltpu.VMEM((128, D), b16),
            pltpu.SemaphoreType.DMA((3, 8, 2)),
            pltpu.SemaphoreType.DMA((3, 8, 2)),
            pltpu.SemaphoreType.DMA((len(rest),)),
            pltpu.SemaphoreType.DMA((3,)),
        ],
        compiler_params=pltpu.CompilerParams(vmem_limit_bytes=48 * 1024 * 1024),
    )(*pieces_a, *pieces_b, *rest)
    return outs[0:4], outs[4:8], outs[8], outs[9], outs[10]


def slice_kernel(*refs):
    weights, outs, buffers, sems = refs[0:2], refs[2:8], refs[8:14], refs[14]
    group = lax.axis_index(DP)
    loads, stores = [], []
    for i, weight in enumerate(weights):
        for s in range(1, 4):
            j = 3 * i + s - 1
            source = weight.at[jnp.bitwise_xor(group, s)]
            loads.append(pltpu.make_async_copy(source, buffers[j], sems.at[0, j]))
            stores.append(pltpu.make_async_copy(buffers[j], outs[j], sems.at[1, j]))
    for load in loads:
        load.start()
    for load, store in zip(loads, stores):
        load.wait()
        store.start()
    for store in stores:
        store.wait()


def sliced(up, down):
    hbm = pl.BlockSpec(memory_space=pltpu.HBM)
    outs = pl.pallas_call(
        slice_kernel,
        in_specs=[hbm] * 2,
        out_specs=[hbm] * 6,
        out_shape=[jax.ShapeDtypeStruct(up.shape[1:], up.dtype)] * 3
        + [jax.ShapeDtypeStruct(down.shape[1:], down.dtype)] * 3,
        scratch_shapes=[pltpu.VMEM(up.shape[1:], up.dtype)] * 3
        + [pltpu.VMEM(down.shape[1:], down.dtype)] * 3
        + [pltpu.SemaphoreType.DMA((2, 6))],
    )(up, down)
    return outs[:3], outs[3:]


def finish_experts_kernel(*refs):
    up, down, up_out, down_out = refs[0:4], refs[4:8], refs[8], refs[9]
    for s in range(4):
        at = jnp.bitwise_xor(lax.axis_index(DP), s)
        up_out[at] = up[s][...].astype(jnp.float32)
        down_out[at] = down[s][...].astype(jnp.float32)


def finish_experts(up, down):
    vmem = pl.BlockSpec(memory_space=pltpu.VMEM)
    return pl.pallas_call(
        finish_experts_kernel,
        in_specs=[vmem] * 8,
        out_specs=[vmem] * 2,
        out_shape=[
            jax.ShapeDtypeStruct((4, 256, 2 * F), jnp.float32),
            jax.ShapeDtypeStruct((4, 128, D), jnp.float32),
        ],
    )(*up, *down)


def finish_weights_kernel(*refs):
    pieces_a, pieces_b, outs, router_out = refs[0:4], refs[4:8], refs[8:11], refs[11]
    half = D // 2
    owner = lax.axis_index(EX)
    for rel in range(8):
        c, x, y = rel & 1, (rel >> 1) & 1, (rel >> 2) & 1
        at = jnp.bitwise_xor(owner, rel)
        rows = pl.ds(pl.multiple_of(at * 32, 32), 32)
        for i, piece in enumerate((pieces_a[2 * c + y].at[x], pieces_b[2 * c + x].at[y])):
            cols = pl.ds(half * i, half)
            for kind in range(3):
                outs[kind][rows, cols] = piece[32 * kind : 32 * kind + 32, :].astype(jnp.float32)
            router_out[at, :, cols] = piece[96:97, :].astype(jnp.float32)


def finish_weights(pieces_a, pieces_b):
    vmem = pl.BlockSpec(memory_space=pltpu.VMEM)
    return pl.pallas_call(
        finish_weights_kernel,
        in_specs=[vmem] * 8,
        out_specs=[vmem] * 4,
        out_shape=[jax.ShapeDtypeStruct((256, D), jnp.float32)] * 3
        + [jax.ShapeDtypeStruct((8, 1, D), jnp.float32)],
    )(*pieces_a, *pieces_b)


CORE, ACROSS, ALONG = 1, 2, 4


def swap(array, bit):
    return lax.ppermute(array, EX, [(i, i ^ bit) for i in range(8)])


def trade(array, step):
    return lax.ppermute(array, DP, [(i, i ^ step) for i in range(4)])


def everyone(array, axes):
    return lax.all_to_all(array, axes, split_axis=0, concat_axis=0, tiled=True)


def to_group(array, axes, count):
    return everyone(jnp.broadcast_to(array[None], (count,) + array.shape), axes)


def gather_halves(halves):
    column = everyone(halves, DP)
    return gather_plane(column[:, 0], column[:, 1])


def gather_plane(a0, b0):
    a = jnp.stack([a0, swap(a0, ACROSS)])
    b = jnp.stack([b0, swap(b0, ALONG)])
    a_far, b_far = swap(a, ALONG), swap(b, ACROSS)
    pieces_a = [a, a_far, swap(a, CORE), swap(a_far, CORE)]
    pieces_b = [b, b_far, swap(b, CORE), swap(b_far, CORE)]
    return pieces_a, pieces_b


def add(one, two):
    return (one.astype(jnp.float32) + two.astype(jnp.float32)).astype(jnp.bfloat16)


def scatter_halves(pieces_a, pieces_b):
    a_far = add(pieces_a[1], swap(pieces_a[3], CORE))
    b_far = add(pieces_b[1], swap(pieces_b[3], CORE))
    a_near = add(pieces_a[0], swap(pieces_a[2], CORE))
    b_near = add(pieces_b[0], swap(pieces_b[2], CORE))
    a = add(a_near, swap(a_far, ALONG))
    b = add(b_near, swap(b_far, ACROSS))
    a_own = add(a[0], swap(a[1], ACROSS))
    b_own = add(b[0], swap(b[1], ALONG))
    return everyone(jnp.stack([a_own, b_own], axis=1), DP)


def block_inner(
    layer_input,
    segment_ids,
    expert_routes,
    first_gain,
    w_query,
    w_keyvalue,
    w_output,
    second_gain,
    w_router,
    w_gate_up,
    w_down,
    out_cotangent,
):
    half = D // 2
    owner_at = lax.axis_index(EX)

    def own_part(weight):
        return lax.dynamic_slice_in_dim(weight, owner_at * 32, 32, 0)

    def split(rows):
        return jnp.stack([rows[:, :half], rows[:, half:]])

    pack = jnp.concatenate([own_part(w_query), own_part(w_keyvalue), own_part(w_output)], axis=0)
    weights_a, weights_b = gather_halves(jnp.broadcast_to(split(pack)[None], (4, 2, 96, half)))
    routes = expert_routes.T
    small = jnp.stack(
        [routes.astype(jnp.bfloat16).reshape(D), own_part(w_router).T.reshape(32 * EXPERTS)]
    )
    small = to_group(small, (EX, DP), 32)
    all_routes = small[:, 0].astype(jnp.int32).reshape(32, TOPK, 128)
    router = small[:, 1].reshape(8, 4, EXPERTS, 32).transpose(2, 1, 0, 3).reshape(EXPERTS, D)

    def exchange(pieces):
        return [pieces[0]] + [trade(pieces[s], s) for s in range(1, 4)]

    up_sent, down_sent = sliced(w_gate_up, w_down)
    up_pieces, down_pieces = exchange([w_gate_up, *up_sent]), exchange([w_down, *down_sent])
    cot_a, cot_b = gather_halves(jnp.broadcast_to(split(out_cotangent)[None], (4, 2, 128, half)))

    rope = jnp.asarray(np.stack(rope_constants(128)))
    gains = jnp.stack([first_gain, second_gain])
    saved = attention_forward(
        weights_a, weights_b, layer_input, segment_ids, gains, rope
    )
    packed, hidden, scalars, normed2 = saved
    tok_a, tok_b = gather_halves(normed2)

    def flat(pieces):
        return [p.reshape(1024, half) for p in pieces]

    mix_a, mix_b, back_a, back_b, d_up, d_down, d_gate = expert_call(
        flat(tok_a),
        flat(tok_b),
        flat(cot_a),
        flat(cot_b),
        up_pieces,
        down_pieces,
        all_routes,
        router,
    )

    def deep(pieces):
        return [p.reshape(2, 4, 128, half) for p in pieces]

    back = scatter_halves(deep(back_a), deep(back_b))
    d_gates = everyone(d_gate, (EX, DP)).reshape(EXPERTS, 128)
    grads_a, grads_b, input_grad, d_gains, d_router = attention_backward(
        weights_a,
        weights_b,
        layer_input,
        segment_ids[None, :],
        gains,
        rope,
        packed,
        hidden,
        scalars,
        out_cotangent,
        back,
        d_gates,
        routes,
        router,
    )
    d_up, d_down = exchange(d_up), exchange(d_down)
    gate_up_grad, down_grad = finish_experts(d_up, d_down)
    mixed = jnp.sum(scatter_halves(deep(mix_a), deep(mix_b)).astype(jnp.float32), axis=0)
    mixed = jnp.concatenate([mixed[0], mixed[1]], axis=1)
    layer_output = (hidden + residual_scale * mixed).astype(jnp.bfloat16)

    small = jnp.concatenate(
        [
            jnp.broadcast_to(d_gains.reshape(1, 2 * D), (32, 2 * D)),
            d_router.reshape(EXPERTS, 32, 32).transpose(1, 2, 0).reshape(32, D),
        ],
        axis=1,
    )
    small = jnp.sum(everyone(small, (DP, EX)), axis=0)
    first_gain_grad, second_gain_grad = small[:D], small[D : 2 * D]

    summed = jnp.sum(scatter_halves(grads_a, grads_b).astype(jnp.float32), axis=0)
    summed = jnp.concatenate([summed, small[2 * D :].reshape(2, 1, half)], axis=1)
    summed = summed.astype(jnp.bfloat16)
    whole_a, whole_b = gather_plane(summed[0], summed[1])
    query_grad, keyvalue_grad, output_grad, router_grad = finish_weights(whole_a, whole_b)
    router_grad = router_grad.reshape(256, EXPERTS)
    return (
        layer_output,
        input_grad,
        first_gain_grad,
        query_grad,
        keyvalue_grad,
        output_grad,
        second_gain_grad,
        router_grad,
        gate_up_grad,
        down_grad,
    )


def block_device(*args):
    return block_inner(*args)


def solution(mesh):
    sizes = (mesh.shape[DP], mesh.shape[EX])
    return jax.shard_map(
        block_device if sizes == (4, 8) else general_device,
        mesh=mesh,
        in_specs=(
            P((DP, EX), None),
            P((DP, EX)),
            P((DP, EX), None),
            P(),
            P(DP, None),
            P(DP, None),
            P(DP, None),
            P(),
            P(DP, None),
            P(EX, DP, None),
            P(EX, DP, None),
            P((DP, EX), None),
        ),
        out_specs=(
            P((DP, EX), None),
            P((DP, EX), None),
            P(),
            P(DP, None),
            P(DP, None),
            P(DP, None),
            P(),
            P(DP, None),
            P(EX, DP, None),
            P(EX, DP, None),
        ),
        check_vma=False,
    )
```

```python
import jax
import jax.numpy as jnp
import numpy as np
from jax import lax
from jax.experimental import pallas as pl
from jax.experimental.pallas import tpu as pltpu
from jax.sharding import PartitionSpec as P

D = 1024
HEADS = 16
KV_HEADS = 8
HEAD_DIM = 64
F = 512
EXPERTS = 32
TOPK = 8
CAP = 40


epsilon = 1e-06
residual_scale = 0.22
score_scale = 0.015625
rope_base = 10000.0


def rope_tables(length, head_width):
    halfway = head_width // 2
    frequency = jnp.exp(
        -jnp.log(rope_base) * (2.0 * jnp.arange(halfway, dtype=jnp.float32) / head_width)
    )
    angles = jnp.arange(length, dtype=jnp.float32)[:, None] * frequency[None, :]
    cosine = jnp.concatenate([jnp.cos(angles), jnp.cos(angles)], axis=1)
    sine_table = jnp.concatenate([jnp.sin(angles), jnp.sin(angles)], axis=1)
    return (cosine, sine_table)


def rotate(values, cosine, sine_table, direction):
    halfway = values.shape[-1] // 2
    turned = jnp.concatenate([-values[..., halfway:], values[..., :halfway]], axis=-1)
    return values * cosine[:, None, :] + direction * turned * sine_table[:, None, :]


def norm_forward(inputs_f32, gain_vector):
    inverse = lax.rsqrt(jnp.mean(inputs_f32 * inputs_f32, axis=-1, keepdims=True) + epsilon)
    return (inputs_f32 * inverse * gain_vector, inverse)


def norm_backward(inputs_f32, inverse, gain_vector, upstream):
    weighted = upstream * gain_vector
    gain_part = jnp.sum(upstream * inputs_f32 * inverse, axis=0)
    through = inverse * weighted - inputs_f32 * (inverse * inverse * inverse) * jnp.mean(
        weighted * inputs_f32, axis=-1, keepdims=True
    )
    return (gain_part, through)


def activate(pre_act):
    gate_half = pre_act[..., :F]
    up_half = pre_act[..., F:]
    return gate_half * jax.nn.sigmoid(gate_half) * up_half


def activate_backward(pre_act, d_act):
    gate_half = pre_act[..., :F]
    up_half = pre_act[..., F:]
    sigmoid_gate = jax.nn.sigmoid(gate_half)
    d_gate = d_act * up_half * sigmoid_gate * (1.0 + gate_half * (1.0 - sigmoid_gate))
    d_up = d_act * gate_half * sigmoid_gate
    return jnp.concatenate([d_gate, d_up], axis=-1)


def masked_scores(query, keys, visible):
    raw_scores = (
        jnp.einsum("qkgd,pkd->kgqp", query, keys, preferred_element_type=jnp.float32) * score_scale
    )
    return jnp.where(visible[None, None], raw_scores, -1e30)


def attend_forward(normed, full_query, full_keyvalue, visible, cosine, sine_table):
    length = normed.shape[0]
    per_group = HEADS // KV_HEADS
    query_raw = jnp.dot(normed, full_query, preferred_element_type=jnp.float32).reshape(
        length, HEADS, HEAD_DIM
    )
    keyval = jnp.dot(normed, full_keyvalue, preferred_element_type=jnp.float32).reshape(
        length, 2, KV_HEADS, HEAD_DIM
    )
    query = (
        rotate(query_raw, cosine, sine_table, 1.0)
        .astype(jnp.bfloat16)
        .reshape(length, KV_HEADS, per_group, HEAD_DIM)
    )
    keys = rotate(keyval[:, 0], cosine, sine_table, 1.0).astype(jnp.bfloat16)
    values = keyval[:, 1].astype(jnp.bfloat16)
    scores = masked_scores(query, keys, visible)
    highest = jnp.max(scores, axis=-1, keepdims=True)
    log_total = highest + jnp.log(jnp.sum(jnp.exp(scores - highest), axis=-1, keepdims=True))
    probabilities = jnp.exp(scores - log_total).astype(jnp.bfloat16)
    attended = jnp.einsum(
        "kgqp,pkd->qkgd", probabilities, values, preferred_element_type=jnp.float32
    )
    attended = attended.reshape(length, HEADS * HEAD_DIM).astype(jnp.bfloat16)
    return (query, keys, values, attended, log_total)


def attend_backward(query, keys, values, attended, log_total, d_attended, visible):
    length = query.shape[0]
    per_group = HEADS // KV_HEADS
    scores = masked_scores(query, keys, visible)
    probs_f32 = jnp.exp(scores - log_total)
    probs_half = probs_f32.astype(jnp.bfloat16)
    d_att4 = d_attended.reshape(length, KV_HEADS, per_group, HEAD_DIM)
    att_four = attended.reshape(length, KV_HEADS, per_group, HEAD_DIM)
    d_values = jnp.einsum("kgqp,qkgd->pkd", probs_half, d_att4, preferred_element_type=jnp.float32)
    d_probs = jnp.einsum("qkgd,pkd->kgqp", d_att4, values, preferred_element_type=jnp.float32)
    row_delta = jnp.einsum("qkgd,qkgd->kgq", d_att4, att_four, preferred_element_type=jnp.float32)
    d_scores = (probs_f32 * (d_probs - row_delta[..., None]) * score_scale).astype(jnp.bfloat16)
    d_query = jnp.einsum(
        "kgqp,pkd->qkgd", d_scores, keys, preferred_element_type=jnp.float32
    ).reshape(length, HEADS, HEAD_DIM)
    d_keys = jnp.einsum("kgqp,qkgd->pkd", d_scores, query, preferred_element_type=jnp.float32)
    return (d_query, d_keys, d_values)


DP, EX = "dp", "expert"


def butterfly_sum(value, axes):
    for axis in axes:
        size = lax.axis_size(axis)
        step = 1
        while step < size:
            value = value + lax.ppermute(value, axis, [(i, i ^ step) for i in range(size)])
            step *= 2
    return value


def spread_over(axes, array):
    for axis in reversed(axes):
        array = lax.all_gather(array, axis, axis=0, tiled=True)
    return array


def sum_to_owner(axes, array):
    for axis in axes:
        array = lax.psum_scatter(array, axis, scatter_dimension=0, tiled=True)
    return array


def expert_pass(tokens, cotangents, gate, hit, w_up, w_dn):
    blocks = tokens.shape[0] // 128
    ranking = jnp.cumsum(hit.reshape(blocks, 128).astype(jnp.int32), axis=1) - 1
    slot = jnp.where(hit.reshape(blocks, 128), ranking, -1)
    select = slot[:, None, :] == jnp.arange(CAP, dtype=jnp.int32)[None, :, None]
    onehot = select.astype(jnp.bfloat16)
    rows = blocks * CAP
    picked = jnp.einsum(
        "bst,btd->bsd", onehot, tokens.reshape(blocks, 128, D), preferred_element_type=jnp.float32
    ).astype(jnp.bfloat16).reshape(rows, D)
    cot = jnp.einsum(
        "bst,btd->bsd",
        onehot,
        cotangents.reshape(blocks, 128, D),
        preferred_element_type=jnp.float32,
    ).reshape(rows, D)
    gate_slot = jnp.sum(
        jnp.where(select, gate.reshape(blocks, 1, 128), 0.0), axis=2
    ).reshape(rows, 1)
    pre_act = jnp.dot(picked, w_up, preferred_element_type=jnp.float32)
    activated = activate(pre_act).astype(jnp.bfloat16)
    result = (
        jnp.dot(activated, w_dn, preferred_element_type=jnp.float32)
        .astype(jnp.bfloat16)
        .astype(jnp.float32)
    )
    d_gate_slot = residual_scale * jnp.sum(cot * result, axis=1)
    d_gate = jnp.sum(jnp.where(select, d_gate_slot.reshape(blocks, CAP, 1), 0.0), axis=1)
    gated = (gate_slot * result).astype(jnp.bfloat16)
    mixed = jnp.einsum(
        "bst,bsd->btd", onehot, gated.reshape(blocks, CAP, D), preferred_element_type=jnp.float32
    ).reshape(blocks * 128, D)
    d_result = (residual_scale * gate_slot * cot).astype(jnp.bfloat16)
    d_act = jnp.dot(d_result, w_dn.T, preferred_element_type=jnp.float32)
    d_down = jnp.dot(activated.T, d_result, preferred_element_type=jnp.float32)
    d_pre = activate_backward(pre_act, d_act).astype(jnp.bfloat16)
    d_up = jnp.dot(picked.T, d_pre, preferred_element_type=jnp.float32)
    d_rows = jnp.dot(d_pre, w_up.T, preferred_element_type=jnp.float32).astype(jnp.bfloat16)
    back = jnp.einsum(
        "bst,bsd->btd", onehot, d_rows.reshape(blocks, CAP, D), preferred_element_type=jnp.float32
    ).reshape(blocks * 128, D)
    return (mixed, back, d_gate.reshape(blocks * 128), d_up, d_down)


def general_device(
    layer_input,
    segment_ids,
    expert_routes,
    first_gain,
    w_query,
    w_keyvalue,
    w_output,
    second_gain,
    w_router,
    w_gate_up,
    w_down,
    out_cotangent,
):
    length = layer_input.shape[0]
    owners = lax.axis_size(EX)
    groups = lax.axis_size(DP)
    group_at = lax.axis_index(DP)
    owner_at = lax.axis_index(EX)
    per_owner = w_gate_up.shape[0]
    shard = w_query.shape[0]
    part = shard // owners
    every = (DP, EX)

    def own_part(weight):
        return lax.dynamic_slice_in_dim(weight, owner_at * part, part, 0)

    pack = jnp.concatenate([own_part(w_query), own_part(w_keyvalue), own_part(w_output)], axis=0)
    gathered = lax.all_gather(pack, every, axis=0).reshape(groups * owners, 3, part, D)
    full_query = gathered[:, 0].reshape(D, HEADS * HEAD_DIM)
    full_keyvalue = gathered[:, 1].reshape(D, 2 * KV_HEADS * HEAD_DIM)
    full_output = gathered[:, 2].reshape(HEADS * HEAD_DIM, D)
    full_router = lax.all_gather(own_part(w_router), every, axis=0, tiled=True)

    exchange = per_owner % groups == 0
    if exchange:
        local = per_owner // groups
        token_axes = (EX, DP)
        first_expert = owner_at * per_owner + group_at * local
        own_up = lax.all_to_all(w_gate_up, DP, split_axis=0, concat_axis=1, tiled=True)
        own_down = lax.all_to_all(w_down, DP, split_axis=0, concat_axis=1, tiled=True)
    else:
        local = per_owner
        token_axes = (EX,)
        first_expert = owner_at * per_owner
        own_up = lax.all_gather(w_gate_up, DP, axis=1, tiled=True)
        own_down = lax.all_gather(w_down, DP, axis=1, tiled=True)
    all_routes = spread_over(token_axes, expert_routes)
    all_cotangents = spread_over(token_axes, out_cotangent)

    cosine, sine_table = rope_tables(length, HEAD_DIM)
    places = jnp.arange(length)
    visible = (places[:, None] >= places[None, :]) & (segment_ids[:, None] == segment_ids[None, :])
    inputs_f32 = layer_input.astype(jnp.float32)
    normed, inverse = norm_forward(inputs_f32, first_gain)
    normed = normed.astype(jnp.bfloat16)
    query, keys, values, attended, log_total = attend_forward(
        normed, full_query, full_keyvalue, visible, cosine, sine_table
    )
    hidden = inputs_f32 + residual_scale * jnp.dot(
        attended, full_output, preferred_element_type=jnp.float32
    )
    normed2, inverse2 = norm_forward(hidden, second_gain)
    normed2 = normed2.astype(jnp.bfloat16)
    all_normed2 = spread_over(token_axes, normed2)

    def gates_of(rows, routes):
        named = jnp.any(
            routes[:, :, None] == jnp.arange(EXPERTS, dtype=jnp.int32)[None, None, :], axis=1
        )
        logits = jnp.dot(rows, full_router, preferred_element_type=jnp.float32)
        highest = jnp.max(jnp.where(named, logits, -jnp.inf), axis=1, keepdims=True)
        exponent = jnp.where(named, jnp.exp(jnp.where(named, logits - highest, 0.0)), 0.0)
        return exponent / jnp.sum(exponent, axis=1, keepdims=True)

    all_gates = gates_of(all_normed2, all_routes)
    d_out = out_cotangent.astype(jnp.float32)
    mixed, back = 0.0, 0.0
    d_gate_list, up_list, down_list = [], [], []
    for j in range(local):
        hit = jnp.any(all_routes == first_expert + j, axis=1)
        gate = lax.dynamic_index_in_dim(all_gates, first_expert + j, 1, keepdims=False)
        one_mixed, one_back, d_gate, d_up, d_dn = expert_pass(
            all_normed2, all_cotangents, gate, hit, own_up[j], own_down[j]
        )
        mixed, back = mixed + one_mixed, back + one_back
        d_gate_list.append(d_gate)
        up_list.append(d_up.astype(jnp.bfloat16))
        down_list.append(d_dn.astype(jnp.bfloat16))
    back_own = sum_to_owner(token_axes, back.astype(jnp.bfloat16)).astype(jnp.float32)
    sources = EXPERTS // local
    d_gate_out = jnp.stack(d_gate_list).reshape(local, sources, length).transpose(1, 0, 2)
    d_gates = (
        lax.all_to_all(d_gate_out, token_axes, split_axis=0, concat_axis=0, tiled=True)
        .reshape(EXPERTS, length)
        .T
    )
    d_up_all, d_down_all = jnp.stack(up_list), jnp.stack(down_list)
    if exchange:
        gate_up_grad = lax.all_to_all(d_up_all, DP, split_axis=1, concat_axis=0, tiled=True)
        down_grad = lax.all_to_all(d_down_all, DP, split_axis=1, concat_axis=0, tiled=True)
    else:
        gate_up_grad = lax.psum_scatter(d_up_all, DP, scatter_dimension=1, tiled=True)
        down_grad = lax.psum_scatter(d_down_all, DP, scatter_dimension=1, tiled=True)
    mixed_own = sum_to_owner(token_axes, mixed.astype(jnp.bfloat16)).astype(jnp.float32)
    layer_output = (hidden + residual_scale * mixed_own).astype(jnp.bfloat16)

    gates = gates_of(normed2, expert_routes)
    d_logits = (gates * (d_gates - jnp.sum(gates * d_gates, axis=1, keepdims=True))).astype(
        jnp.bfloat16
    )
    d_router = jnp.dot(normed2.T, d_logits, preferred_element_type=jnp.float32)
    d_normed2 = back_own + jnp.dot(d_logits, full_router.T, preferred_element_type=jnp.float32)
    d_second_gain, d_through = norm_backward(hidden, inverse2, second_gain, d_normed2)
    second_gain_grad = butterfly_sum(d_second_gain, (EX, DP))
    d_hidden = d_out + d_through
    d_branch = (residual_scale * d_hidden).astype(jnp.bfloat16)
    d_wout = jnp.dot(attended.T, d_branch, preferred_element_type=jnp.float32)
    d_attended = jnp.dot(d_branch, full_output.T, preferred_element_type=jnp.float32).astype(
        jnp.bfloat16
    )
    d_query, d_keys, d_values = attend_backward(
        query, keys, values, attended, log_total, d_attended, visible
    )
    d_query = (
        rotate(d_query, cosine, sine_table, -1.0)
        .reshape(length, HEADS * HEAD_DIM)
        .astype(jnp.bfloat16)
    )
    d_keys = rotate(d_keys, cosine, sine_table, -1.0)
    d_keyvalue = (
        jnp.stack([d_keys, d_values], axis=1)
        .reshape(length, 2 * KV_HEADS * HEAD_DIM)
        .astype(jnp.bfloat16)
    )
    d_wquery = jnp.dot(normed.T, d_query, preferred_element_type=jnp.float32)
    d_wkeyvalue = jnp.dot(normed.T, d_keyvalue, preferred_element_type=jnp.float32)
    d_normed = jnp.dot(d_query, full_query.T, preferred_element_type=jnp.float32) + jnp.dot(
        d_keyvalue, full_keyvalue.T, preferred_element_type=jnp.float32
    )
    d_first_gain, d_inputs = norm_backward(inputs_f32, inverse, first_gain, d_normed)
    first_gain_grad = butterfly_sum(d_first_gain, (EX, DP))
    input_grad = (d_hidden + d_inputs).astype(jnp.bfloat16)

    def reduced(*grads):
        packed = jnp.stack([g.astype(jnp.bfloat16) for g in grads])
        count, width = len(grads), grads[0].shape[1]
        packed = packed.reshape(count, groups, owners, part, width).transpose(2, 1, 0, 3, 4)
        packed = packed.reshape(owners * groups * count * part, width)
        mine = sum_to_owner((EX, DP), packed).reshape(1, count, part, width)
        whole = lax.all_gather(mine, EX, axis=0, tiled=True)
        whole = whole.transpose(1, 0, 2, 3).reshape(count, owners * part, width)
        return [whole[i].astype(jnp.float32) for i in range(count)]

    output_grad, query_grad, keyvalue_grad = reduced(d_wout, d_wquery, d_wkeyvalue)
    (router_grad,) = reduced(d_router)
    return (
        layer_output,
        input_grad,
        first_gain_grad,
        query_grad,
        keyvalue_grad,
        output_grad,
        second_gain_grad,
        router_grad,
        gate_up_grad.astype(jnp.float32),
        down_grad.astype(jnp.float32),
    )


def expert_kernel(*refs):
    tok_a, tok_b, cot_a, cot_b = refs[0:4], refs[4:8], refs[8:12], refs[12:16]
    own_up, own_down, pieces = refs[16], refs[17], refs[18:21]
    routes_ref, router_ref = refs[21:23]
    mix_a, mix_b, back_a, back_b = refs[23:27], refs[27:31], refs[31:35], refs[35:39]
    grad_pieces, dgate_ref = refs[39:43], refs[43]
    (
        tok_buf,
        cot_buf,
        mix_buf,
        back_buf,
        rows_scr,
        act_scr,
        dres_scr,
        dpre_scr,
        cot_scr,
        gate_scr,
        slot_scr,
        tri_scr,
        up_scr,
        down_scr,
        d_up_scr,
        d_down_scr,
        in_sem,
        out_sem,
        weight_sem,
        grad_sem,
    ) = refs[44:]
    half = D // 2
    owner, group = lax.axis_index(EX), lax.axis_index(DP)
    expert = owner * 4 + group
    chunk_rows = 8 * CAP

    def chunk_copies(kk, slot, sources, sem, outward):
        c, y = kk // 2, kk % 2
        ends = []
        for a, b, buf in sources:
            ends.append((a[kk], buf.at[slot, :, pl.ds(0, half)]))
            for x in range(2):
                ends.append(
                    (
                        b[2 * c + x].at[pl.ds(512 * y, 512), :],
                        buf.at[slot, pl.ds(512 * x, 512), pl.ds(half, half)],
                    )
                )
        if outward:
            ends = [(there, here) for here, there in ends]
        return [
            pltpu.make_async_copy(*pair, sem.at[slot, i]) for i, pair in enumerate(ends)
        ]

    def in_copies(kk, slot):
        sources = ((tok_a, tok_b, tok_buf), (cot_a, cot_b, cot_buf))
        return chunk_copies(kk, slot, sources, in_sem, False)

    def out_copies(kk, slot):
        sources = ((back_a, back_b, back_buf), (mix_a, mix_b, mix_buf))
        return chunk_copies(kk, slot, sources, out_sem, True)

    def weight_pairs():
        found = []
        for s in range(4):
            at = jnp.bitwise_xor(group, s)
            up_from, down_from = own_up.at[group], own_down.at[group]
            if s > 0:
                up_from = pieces[s - 1].at[pl.ds(0, 256), :]
                down_from = pieces[s - 1].at[pl.ds(256, 128), :]
            found.append(pltpu.make_async_copy(up_from, up_scr.at[at], weight_sem.at[0, s]))
            found.append(pltpu.make_async_copy(down_from, down_scr.at[at], weight_sem.at[1, s]))
        return found

    for copy in in_copies(0, 0) + weight_pairs():
        copy.start()
    before = lax.broadcasted_iota(jnp.int32, (256, 256), 0)
    after = lax.broadcasted_iota(jnp.int32, (256, 256), 1)
    tri_scr[...] = ((before <= after) & ((before < 128) == (after < 128))).astype(jnp.bfloat16)

    def pair_mask(pair):
        return slot_scr[pair] == lax.broadcasted_iota(jnp.int32, (2 * CAP, 256), 0)

    def chunk_step(k, carry):
        for kk in range(4):

            @pl.when(k == kk)
            def _():
                if kk < 3:
                    for copy in in_copies(kk + 1, (kk + 1) % 2):
                        copy.start()
                for copy in in_copies(kk, kk % 2):
                    copy.wait()
                if kk >= 2:
                    for copy in out_copies(kk - 2, kk % 2):
                        copy.wait()

        at = lax.rem(k, 2)
        base = pl.multiple_of(k * chunk_rows, chunk_rows)
        away = k // 2 + 4 * lax.rem(k, 2)
        for pair in range(4):
            device = jnp.bitwise_xor(owner, away + 2 * (pair // 2)) * 4 + 2 * (pair % 2)
            routes = jnp.concatenate([routes_ref[device], routes_ref[device + 1]], axis=1)
            hit = jnp.max((routes == expert).astype(jnp.float32), axis=0, keepdims=True)
            rank = jnp.dot(
                jnp.broadcast_to(hit, (16, 256)).astype(jnp.bfloat16),
                tri_scr[...],
                preferred_element_type=jnp.float32,
            )[0:1]
            second = lax.broadcasted_iota(jnp.int32, (1, 256), 1) >= 128
            slot = rank.astype(jnp.int32) - 1 + jnp.where(second, CAP, 0)
            slot_scr[pair] = jnp.where(hit > 0.5, slot, -1)
            mask = pair_mask(pair)
            onehot = mask.astype(jnp.bfloat16)
            token_rows = tok_buf[at, pl.ds(256 * pair, 256), :]
            logits = lax.dot_general(
                router_ref[...],
                token_rows,
                (((1,), (1,)), ((), ())),
                preferred_element_type=jnp.float32,
            )
            names = lax.broadcasted_iota(jnp.int32, (EXPERTS, 256), 0)
            named = routes[0:1] == names
            for i in range(1, TOPK):
                named = named | (routes[i : i + 1] == names)
            highest = jnp.max(jnp.where(named, logits, -3e38), axis=0, keepdims=True)
            exponent = jnp.where(named, jnp.exp(jnp.where(named, logits - highest, 0.0)), 0.0)
            own = jnp.sum(jnp.where(names == expert, exponent, 0.0), axis=0, keepdims=True)
            gate = own / jnp.sum(exponent, axis=0, keepdims=True)
            gate_slot = jnp.sum(jnp.where(mask, gate, 0.0), axis=1, keepdims=True)
            gate_scr[pl.ds(2 * CAP * pair, 2 * CAP), :] = gate_slot
            place = pl.ds(base + 2 * CAP * pair, 2 * CAP)
            rows_scr[place, :] = jnp.dot(
                onehot, token_rows, preferred_element_type=jnp.float32
            ).astype(jnp.bfloat16)
            cot = jnp.dot(
                onehot, cot_buf[at, pl.ds(256 * pair, 256), :], preferred_element_type=jnp.float32
            )
            cot_scr[pl.ds(2 * CAP * pair, 2 * CAP), :] = cot.astype(jnp.bfloat16)
            dres_scr[place, :] = (residual_scale * gate_slot * cot).astype(jnp.bfloat16)

        @pl.when(k == 0)
        def _():
            for copy in weight_pairs():
                copy.wait()

        here = pl.ds(base, chunk_rows)
        pre = jnp.dot(rows_scr[here, :], up_scr[...].reshape(D, 2 * F), preferred_element_type=jnp.float32)
        gate_half, up_half = pre[:, :F], pre[:, F:]
        sigmoid_gate = 1.0 / (1.0 + jnp.exp(-gate_half))
        swish = gate_half * sigmoid_gate
        activated = (swish * up_half).astype(jnp.bfloat16)
        act_scr[here, :] = activated
        d_act = lax.dot_general(
            dres_scr[here, :],
            down_scr[...].reshape(F, D),
            (((1,), (1,)), ((), ())),
            preferred_element_type=jnp.float32,
        )
        dpre_scr[here, 0:F] = (
            d_act * up_half * sigmoid_gate * (1.0 + gate_half * (1.0 - sigmoid_gate))
        ).astype(jnp.bfloat16)
        dpre_scr[here, F : 2 * F] = (d_act * swish).astype(jnp.bfloat16)
        result = (
            jnp.dot(activated, down_scr[...].reshape(F, D), preferred_element_type=jnp.float32)
            .astype(jnp.bfloat16)
            .astype(jnp.float32)
        )
        d_gate_slot = residual_scale * jnp.sum(
            cot_scr[...].astype(jnp.float32) * result, axis=1, keepdims=True
        )
        gated = (gate_scr[...] * result).astype(jnp.bfloat16)
        d_rows = lax.dot_general(
            dpre_scr[here, :],
            up_scr[...].reshape(D, 2 * F),
            (((1,), (1,)), ((), ())),
            preferred_element_type=jnp.float32,
        ).astype(jnp.bfloat16)
        for pair in range(4):
            device = jnp.bitwise_xor(owner, away + 2 * (pair // 2)) * 4 + 2 * (pair % 2)
            mask = pair_mask(pair)
            onehot = mask.astype(jnp.bfloat16)
            mine = slice(2 * CAP * pair, 2 * CAP * (pair + 1))
            d_gate = jnp.sum(jnp.where(mask, d_gate_slot[mine], 0.0), axis=0, keepdims=True)
            dgate_ref[device] = d_gate[:, :128]
            dgate_ref[device + 1] = d_gate[:, 128:]
            rows = pl.ds(256 * pair, 256)
            mix_buf[at, rows, :] = lax.dot_general(
                onehot,
                gated[mine],
                (((0,), (0,)), ((), ())),
                preferred_element_type=jnp.float32,
            ).astype(jnp.bfloat16)
            back_buf[at, rows, :] = lax.dot_general(
                onehot,
                d_rows[mine],
                (((0,), (0,)), ((), ())),
                preferred_element_type=jnp.float32,
            ).astype(jnp.bfloat16)
        for kk in range(4):

            @pl.when(k == kk)
            def _():
                for copy in out_copies(kk, kk % 2):
                    copy.start()

        return carry

    lax.fori_loop(0, 4, chunk_step, 0)

    def up_step(t, carry):
        at = jnp.bitwise_xor(group, t)
        d_up_scr[t] = lax.dot_general(
            rows_scr[:, pl.ds(pl.multiple_of(at * 256, 256), 256)],
            dpre_scr[...],
            (((0,), (0,)), ((), ())),
            preferred_element_type=jnp.float32,
        ).astype(jnp.bfloat16)
        d_down_scr[t] = lax.dot_general(
            act_scr[:, pl.ds(pl.multiple_of(at * 128, 128), 128)],
            dres_scr[...],
            (((0,), (0,)), ((), ())),
            preferred_element_type=jnp.float32,
        ).astype(jnp.bfloat16)
        for s in range(4):

            @pl.when(t == s)
            def _():
                for copy in grad_copies(s):
                    copy.start()

        return carry

    def grad_copies(s):
        return (
            pltpu.make_async_copy(
                d_up_scr.at[s], grad_pieces[s].at[pl.ds(0, 256), :], grad_sem.at[0, s]
            ),
            pltpu.make_async_copy(
                d_down_scr.at[s], grad_pieces[s].at[pl.ds(256, 128), :], grad_sem.at[1, s]
            ),
        )

    lax.fori_loop(0, 4, up_step, 0)
    for kk in (2, 3):
        for copy in out_copies(kk, kk % 2):
            copy.wait()
    for s in range(4):
        for copy in grad_copies(s):
            copy.wait()


def expert_call(tok_a, tok_b, cot_a, cot_b, weights, routes, router):
    half = D // 2
    token_count = 1024
    hbm = pl.BlockSpec(memory_space=pltpu.HBM)
    vmem = pl.BlockSpec(memory_space=pltpu.VMEM)
    slots = 32 * CAP
    b16 = jnp.bfloat16
    piece = jax.ShapeDtypeStruct((token_count, half), b16)
    far = pltpu.HBM((token_count, half), b16)
    outs = pl.pallas_call(
        expert_kernel,
        in_specs=[hbm] * 21 + [vmem] * 2,
        out_specs=[hbm] * 20 + [vmem],
        out_shape=([piece] * 2 + [far] * 2) * 4
        + [jax.ShapeDtypeStruct((384, D), b16)]
        + [pltpu.HBM((384, D), b16)] * 3
        + [jax.ShapeDtypeStruct((32, 1, 128), jnp.float32)],
        scratch_shapes=[pltpu.VMEM((2, token_count, D), b16)] * 4
        + [
            pltpu.VMEM((slots, D), b16),
            pltpu.VMEM((slots, F), b16),
            pltpu.VMEM((slots, D), b16),
            pltpu.VMEM((slots, 2 * F), b16),
            pltpu.VMEM((8 * CAP, D), b16),
            pltpu.VMEM((8 * CAP, 1), jnp.float32),
            pltpu.VMEM((4, 1, 256), jnp.int32),
            pltpu.VMEM((256, 256), b16),
            pltpu.VMEM((4, 256, 2 * F), b16),
            pltpu.VMEM((4, 128, D), b16),
            pltpu.VMEM((4, 256, 2 * F), b16),
            pltpu.VMEM((4, 128, D), b16),
            pltpu.SemaphoreType.DMA((2, 6)),
            pltpu.SemaphoreType.DMA((2, 6)),
            pltpu.SemaphoreType.DMA((2, 4)),
            pltpu.SemaphoreType.DMA((2, 4)),
        ],
        compiler_params=pltpu.CompilerParams(vmem_limit_bytes=48 * 1024 * 1024),
    )(*tok_a, *tok_b, *cot_a, *cot_b, *weights, routes, router)
    groups = [outs[4 * i : 4 * i + 4] for i in range(5)]
    return (*groups, outs[20])


def rope_constants(length):
    frequency = rope_base ** (-2.0 * np.arange(HEAD_DIM // 2) / HEAD_DIM)
    angles = np.arange(length)[:, None] * frequency[None, :]
    cosine = np.tile(np.cos(angles), (1, 4)).astype(np.float32)
    sine = np.sin(angles)
    signed = np.concatenate([-sine, sine, -sine, sine], axis=1).astype(np.float32)
    return cosine, signed


def turn(slab, cosine, signed):
    low = (lax.broadcasted_iota(jnp.int32, slab.shape, 1) & 32) == 0
    swapped = jnp.where(low, pltpu.roll(slab, 96, 1), pltpu.roll(slab, 32, 1))
    return slab * cosine + swapped * signed


def halves_stacked(slab, low):
    zero = jnp.zeros_like(slab)
    return jnp.concatenate([jnp.where(low, slab, zero), jnp.where(low, zero, slab)], axis=0)


def doubled(slab, low, second):
    other = pltpu.roll(slab, 64, 1)
    return jnp.where(low, other, slab) if second else jnp.where(low, slab, other)


def weight_copies(pieces_a, pieces_b, whole, sems, owner, kind, outward):
    half = D // 2
    copies = []
    for rel in range(8):
        c, x, y = rel & 1, (rel >> 1) & 1, (rel >> 2) & 1
        at = jnp.bitwise_xor(owner, rel)
        rows = pl.ds(32 * kind, 32)
        ends = (
            (pieces_a[2 * c + y].at[x, :, rows, :], whole.at[kind, :, at, :, pl.ds(0, half)]),
            (pieces_b[2 * c + x].at[y, :, rows, :], whole.at[kind, :, at, :, pl.ds(half, half)]),
        )
        for i, (piece, place) in enumerate(ends):
            pair = (place, piece) if outward else (piece, place)
            copies.append(pltpu.make_async_copy(*pair, sems.at[kind, rel, i]))
    return copies


def seen(seg_row, rows_at, cols_at):
    row = seg_row.astype(jnp.float32)
    column = jnp.sum(jnp.where(rows_at == cols_at, row, 0.0), axis=1, keepdims=True)
    return (rows_at >= cols_at) & (column == row)


def packed_views(pack_ref):
    starts = (0, D, 2 * D, 2 * D + D // 2, 3 * D, 4 * D)
    return [pack_ref.at[:, pl.ds(a, b - a)] for a, b in zip(starts[:-1], starts[1:])]


def attention_forward_kernel(*refs):
    pieces_a, pieces_b = refs[0:4], refs[4:8]
    arrays, finals, buffers = refs[8:13], refs[13:17], refs[17:22]
    x_ref, seg_row, gain1_ref, gain2_ref, rope_ref = buffers
    pack_ref, hidden_ref, small_ref, normed2_ref, whole, sems, out_sems, load_sems = refs[22:]
    loads = [
        pltpu.make_async_copy(there, here, load_sems.at[i])
        for i, (there, here) in enumerate(zip(arrays, buffers))
    ]
    for load in loads:
        load.start()
    outs = [
        pltpu.make_async_copy(here, there, out_sems.at[i])
        for i, (here, there) in enumerate(zip(refs[22:26], finals))
    ]
    normed_ref, q_ref, k_ref, v_ref, att_ref = packed_views(pack_ref)
    owner = lax.axis_index(EX)
    half = D // 2
    for kind in range(3):
        for copy in weight_copies(pieces_a, pieces_b, whole, sems, owner, kind, False):
            copy.start()
    for load in loads:
        load.wait()
    inputs = x_ref[...].astype(jnp.float32)
    inverse = lax.rsqrt(jnp.mean(inputs * inputs, axis=1, keepdims=True) + epsilon)
    normed = (inputs * inverse * gain1_ref[...]).astype(jnp.bfloat16)
    normed_ref[...] = normed
    small_ref[:128, 8:9] = inverse
    cosine, signed = rope_ref[0], rope_ref[1]
    for kind in range(2):
        for copy in weight_copies(pieces_a, pieces_b, whole, sems, owner, kind, False):
            copy.wait()
    query = jnp.dot(normed, whole[0].reshape(D, D), preferred_element_type=jnp.float32)
    keyval = jnp.dot(normed, whole[1].reshape(D, D), preferred_element_type=jnp.float32)
    for s in range(8):
        cols = slice(128 * s, 128 * s + 128)
        q_ref[:, cols] = turn(query[:, cols], cosine, signed).astype(jnp.bfloat16)
    for s in range(4):
        cols = slice(128 * s, 128 * s + 128)
        k_ref[:, cols] = turn(keyval[:, cols], cosine, signed).astype(jnp.bfloat16)
    v_ref[...] = keyval[:, half:].astype(jnp.bfloat16)
    rows_at = lax.broadcasted_iota(jnp.int32, (128, 128), 0)
    cols_at = lax.broadcasted_iota(jnp.int32, (128, 128), 1)
    visible = seen(seg_row[...], rows_at, cols_at)
    visible2 = jnp.concatenate([visible, visible], axis=0)
    low = cols_at < 64
    for head in range(KV_HEADS):
        slab = slice(128 * (head // 2), 128 * (head // 2) + 128)
        q2 = halves_stacked(q_ref[:, 128 * head : 128 * head + 128], low)
        k2 = doubled(k_ref[:, slab], low, head % 2)
        v2 = doubled(v_ref[:, slab], low, head % 2)
        scores = lax.dot_general(
            q2, k2, (((1,), (1,)), ((), ())), preferred_element_type=jnp.float32
        )
        scores = jnp.where(visible2, scores * score_scale, -1e30)
        highest = jnp.max(scores, axis=1, keepdims=True)
        log_total = highest + jnp.log(jnp.sum(jnp.exp(scores - highest), axis=1, keepdims=True))
        probabilities = jnp.exp(scores - log_total).astype(jnp.bfloat16)
        small_ref[:, head : head + 1] = log_total
        mixed = jnp.dot(probabilities, v2, preferred_element_type=jnp.float32)
        att_ref[:, 128 * head : 128 * head + 128] = jnp.where(
            low, mixed[:128], mixed[128:]
        ).astype(jnp.bfloat16)
    for copy in weight_copies(pieces_a, pieces_b, whole, sems, owner, 2, False):
        copy.wait()
    outs[0].start()
    hidden = inputs + residual_scale * jnp.dot(
        att_ref[...], whole[2].reshape(D, D), preferred_element_type=jnp.float32
    )
    inverse2 = lax.rsqrt(jnp.mean(hidden * hidden, axis=1, keepdims=True) + epsilon)
    normed2 = (hidden * inverse2 * gain2_ref[...]).astype(jnp.bfloat16)
    hidden_ref[...] = hidden
    small_ref[:128, 9:10] = inverse2
    outs[1].start()
    outs[2].start()
    for z in range(4):
        normed2_ref[z, 0] = normed2[:, :half]
        normed2_ref[z, 1] = normed2[:, half:]
    outs[3].start()
    for out in outs:
        out.wait()


def attention_forward(pieces_a, pieces_b, *rest):
    hbm = pl.BlockSpec(memory_space=pltpu.HBM)
    f32, b16 = jnp.float32, jnp.bfloat16
    shapes = [
        ((128, 4 * D), b16),
        ((128, D), f32),
        ((256, 16), f32),
        ((4, 2, 128, D // 2), b16),
    ]
    return pl.pallas_call(
        attention_forward_kernel,
        in_specs=[hbm] * (8 + len(rest)),
        out_specs=[hbm] * 4,
        out_shape=[pltpu.HBM(s, t) for s, t in shapes],
        scratch_shapes=[pltpu.VMEM(array.shape, array.dtype) for array in rest]
        + [pltpu.VMEM(s, t) for s, t in shapes]
        + [
            pltpu.VMEM((3, 4, 8, 32, D), b16),
            pltpu.SemaphoreType.DMA((3, 8, 2)),
            pltpu.SemaphoreType.DMA((4,)),
            pltpu.SemaphoreType.DMA((len(rest),)),
        ],
        compiler_params=pltpu.CompilerParams(vmem_limit_bytes=40 * 1024 * 1024),
    )(*pieces_a, *pieces_b, *rest)


def attention_backward_kernel(*refs):
    pieces_a, pieces_b = refs[0:4], refs[4:8]
    arrays = refs[8:21]
    grads_a, grads_b = refs[21:25], refs[25:29]
    finals = refs[29:32]
    buffers = refs[32:45]
    (
        x_ref,
        seg_row,
        gain1_ref,
        gain2_ref,
        rope_ref,
        pack_ref,
        hidden_ref,
        small_ref,
        dout_ref,
        back_ref,
        dgate_ref,
        routes_ref,
        router_ref,
    ) = buffers
    input_grad_ref, gains_ref, router_grad_ref = refs[45:48]
    whole, grad, datt_scr, dq_scr, dkv_scr, sems, out_sems, load_sems, last_sems = refs[48:]
    loads = [
        pltpu.make_async_copy(there, here, load_sems.at[i])
        for i, (there, here) in enumerate(zip(arrays, buffers))
    ]
    lasts = [
        pltpu.make_async_copy(here, there, last_sems.at[i])
        for i, (here, there) in enumerate(zip(refs[45:48], finals))
    ]
    for load in loads:
        load.start()
    normed_ref, q_ref, k_ref, v_ref, att_ref = packed_views(pack_ref)
    owner = lax.axis_index(EX)
    half = D // 2
    for kind in (2, 0, 1):
        for copy in weight_copies(pieces_a, pieces_b, whole, sems, owner, kind, False):
            copy.start()
    for load in loads:
        load.wait()
    hidden, inverse2 = hidden_ref[...], small_ref[:128, 9:10]
    normed2 = (hidden * inverse2 * gain2_ref[...]).astype(jnp.bfloat16)
    names = lax.broadcasted_iota(jnp.int32, (EXPERTS, 128), 0)
    routes = routes_ref[...]
    named = routes[0:1] == names
    for i in range(1, TOPK):
        named = named | (routes[i : i + 1] == names)
    logits = lax.dot_general(
        router_ref[...], normed2, (((1,), (1,)), ((), ())), preferred_element_type=jnp.float32
    )
    highest = jnp.max(jnp.where(named, logits, -3e38), axis=0, keepdims=True)
    exponent = jnp.where(named, jnp.exp(jnp.where(named, logits - highest, 0.0)), 0.0)
    gates = exponent / jnp.sum(exponent, axis=0, keepdims=True)
    d_gates = dgate_ref[...]
    d_logits = (gates * (d_gates - jnp.sum(gates * d_gates, axis=0, keepdims=True))).astype(
        jnp.bfloat16
    )
    router_grad_ref[...] = jnp.dot(d_logits, normed2, preferred_element_type=jnp.float32)
    back = [
        sum(back_ref[z, i].astype(jnp.float32) for z in range(4)) for i in range(2)
    ]
    d_normed2 = jnp.concatenate(back, axis=1) + lax.dot_general(
        d_logits, router_ref[...], (((0,), (0,)), ((), ())), preferred_element_type=jnp.float32
    )
    gains_ref[1:2, :] = jnp.sum(d_normed2 * hidden * inverse2, axis=0, keepdims=True)
    weighted = d_normed2 * gain2_ref[...]
    d_hidden = (
        dout_ref[...].astype(jnp.float32)
        + inverse2 * weighted
        - hidden
        * (inverse2 * inverse2 * inverse2)
        * jnp.mean(weighted * hidden, axis=1, keepdims=True)
    )
    d_branch = (residual_scale * d_hidden).astype(jnp.bfloat16)
    tn = (((0,), (0,)), ((), ()))
    nt = (((1,), (1,)), ((), ()))
    for z in range(4):
        grad[2, z] = (
            lax.dot_general(
                att_ref[:, 256 * z : 256 * z + 256], d_branch, tn, preferred_element_type=jnp.float32
            )
            .astype(jnp.bfloat16)
            .reshape(8, 32, D)
        )
    for copy in weight_copies(grads_a, grads_b, grad, out_sems, owner, 2, True):
        copy.start()
    for copy in weight_copies(pieces_a, pieces_b, whole, sems, owner, 2, False):
        copy.wait()
    datt_scr[...] = lax.dot_general(
        d_branch, whole[2].reshape(D, D), nt, preferred_element_type=jnp.float32
    ).astype(jnp.bfloat16)
    cosine, signed = rope_ref[0], -rope_ref[1]
    rows_at = lax.broadcasted_iota(jnp.int32, (128, 128), 0)
    cols_at = lax.broadcasted_iota(jnp.int32, (128, 128), 1)
    visible = seen(seg_row[...], rows_at, cols_at)
    visible2 = jnp.concatenate([visible, visible], axis=0)
    low = cols_at < 64
    keep_k = keep_v = None
    for head in range(KV_HEADS):
        cols = slice(128 * head, 128 * head + 128)
        slab = slice(128 * (head // 2), 128 * (head // 2) + 128)
        q2 = halves_stacked(q_ref[:, cols], low)
        k2 = doubled(k_ref[:, slab], low, head % 2)
        v2 = doubled(v_ref[:, slab], low, head % 2)
        d_att = datt_scr[:, cols]
        da2 = halves_stacked(d_att, low)
        scores = lax.dot_general(q2, k2, nt, preferred_element_type=jnp.float32)
        scores = jnp.where(visible2, scores * score_scale, -1e30)
        probs = jnp.exp(scores - small_ref[:, head : head + 1])
        d_value = lax.dot_general(
            probs.astype(jnp.bfloat16), da2, tn, preferred_element_type=jnp.float32
        )
        d_probs = lax.dot_general(da2, v2, nt, preferred_element_type=jnp.float32)
        product = d_att.astype(jnp.float32) * att_ref[:, cols].astype(jnp.float32)
        delta = jnp.sum(halves_stacked(product, low), axis=1, keepdims=True)
        d_scores = (probs * (d_probs - delta) * score_scale).astype(jnp.bfloat16)
        d_q2 = jnp.dot(d_scores, k2, preferred_element_type=jnp.float32)
        d_query = jnp.where(low, d_q2[:128], d_q2[128:])
        dq_scr[:, cols] = turn(d_query, cosine, signed).astype(jnp.bfloat16)
        d_key = lax.dot_general(d_scores, q2, tn, preferred_element_type=jnp.float32)
        d_key = d_key + pltpu.roll(d_key, 64, 1)
        d_value = d_value + pltpu.roll(d_value, 64, 1)
        if head % 2 == 0:
            keep_k, keep_v = d_key, d_value
        else:
            dkv_scr[:, slab] = turn(jnp.where(low, keep_k, d_key), cosine, signed).astype(
                jnp.bfloat16
            )
            dkv_scr[:, half + slab.start : half + slab.stop] = jnp.where(
                low, keep_v, d_value
            ).astype(jnp.bfloat16)
    for kind, source in ((0, dq_scr), (1, dkv_scr)):
        for z in range(4):
            grad[kind, z] = (
                lax.dot_general(
                    normed_ref[:, 256 * z : 256 * z + 256],
                    source[...],
                    tn,
                    preferred_element_type=jnp.float32,
                )
                .astype(jnp.bfloat16)
                .reshape(8, 32, D)
            )
        for copy in weight_copies(grads_a, grads_b, grad, out_sems, owner, kind, True):
            copy.start()
    for kind in range(2):
        for copy in weight_copies(pieces_a, pieces_b, whole, sems, owner, kind, False):
            copy.wait()
    d_normed = lax.dot_general(
        dq_scr[...], whole[0].reshape(D, D), nt, preferred_element_type=jnp.float32
    ) + lax.dot_general(
        dkv_scr[...], whole[1].reshape(D, D), nt, preferred_element_type=jnp.float32
    )
    inputs, inverse = x_ref[...].astype(jnp.float32), small_ref[:128, 8:9]
    gains_ref[0:1, :] = jnp.sum(d_normed * inputs * inverse, axis=0, keepdims=True)
    weighted = d_normed * gain1_ref[...]
    input_grad_ref[...] = (
        d_hidden
        + inverse * weighted
        - inputs
        * (inverse * inverse * inverse)
        * jnp.mean(weighted * inputs, axis=1, keepdims=True)
    ).astype(jnp.bfloat16)
    for last in lasts:
        last.start()
    for kind in range(3):
        for copy in weight_copies(grads_a, grads_b, grad, out_sems, owner, kind, True):
            copy.wait()
    for last in lasts:
        last.wait()


def attention_backward(pieces_a, pieces_b, *rest):
    hbm = pl.BlockSpec(memory_space=pltpu.HBM)
    f32, b16 = jnp.float32, jnp.bfloat16
    piece = jax.ShapeDtypeStruct((2, 4, 96, D // 2), b16)
    far = pltpu.HBM((2, 4, 96, D // 2), b16)
    shapes = [((128, D), b16), ((2, D), f32), ((EXPERTS, D), f32)]
    outs = pl.pallas_call(
        attention_backward_kernel,
        in_specs=[hbm] * (8 + len(rest)),
        out_specs=[hbm] * 11,
        out_shape=([piece] * 2 + [far] * 2) * 2 + [pltpu.HBM(*pair) for pair in shapes],
        scratch_shapes=[pltpu.VMEM(array.shape, array.dtype) for array in rest]
        + [pltpu.VMEM(*pair) for pair in shapes]
        + [
            pltpu.VMEM((3, 4, 8, 32, D), b16),
            pltpu.VMEM((3, 4, 8, 32, D), b16),
            pltpu.VMEM((128, D), b16),
            pltpu.VMEM((128, D), b16),
            pltpu.VMEM((128, D), b16),
            pltpu.SemaphoreType.DMA((3, 8, 2)),
            pltpu.SemaphoreType.DMA((3, 8, 2)),
            pltpu.SemaphoreType.DMA((len(rest),)),
            pltpu.SemaphoreType.DMA((3,)),
        ],
        compiler_params=pltpu.CompilerParams(vmem_limit_bytes=48 * 1024 * 1024),
    )(*pieces_a, *pieces_b, *rest)
    return outs[0:4], outs[4:8], outs[8], outs[9], outs[10]


def slice_kernel(*refs):
    weights, outs, buffers, sems = refs[0:2], refs[2:5], refs[5:8], refs[8]
    group = lax.axis_index(DP)
    loads, stores = [], []
    for s in range(3):
        at = jnp.bitwise_xor(group, s + 1)
        for i, rows in enumerate((pl.ds(0, 256), pl.ds(256, 128))):
            loads.append(
                pltpu.make_async_copy(weights[i].at[at], buffers[s].at[rows, :], sems.at[i, s])
            )
        stores.append(pltpu.make_async_copy(buffers[s], outs[s], sems.at[2, s]))
    for load in loads:
        load.start()
    for s in range(3):
        loads[2 * s].wait()
        loads[2 * s + 1].wait()
        stores[s].start()
    for store in stores:
        store.wait()


def sliced(up, down):
    hbm = pl.BlockSpec(memory_space=pltpu.HBM)
    return pl.pallas_call(
        slice_kernel,
        in_specs=[hbm] * 2,
        out_specs=[hbm] * 3,
        out_shape=[pltpu.HBM((384, D), up.dtype)] * 3,
        scratch_shapes=[pltpu.VMEM((384, D), up.dtype)] * 3 + [pltpu.SemaphoreType.DMA((3, 3))],
    )(up, down)


def finish_experts_kernel(*refs):
    pieces, up_out, down_out = refs[0:4], refs[4], refs[5]
    for s in range(4):
        at = jnp.bitwise_xor(lax.axis_index(DP), s)
        up_out[at] = pieces[s][0:256, :].astype(jnp.float32)
        down_out[at] = pieces[s][256:384, :].astype(jnp.float32)


def finish_experts(pieces):
    vmem = pl.BlockSpec(memory_space=pltpu.VMEM)
    return pl.pallas_call(
        finish_experts_kernel,
        in_specs=[vmem] * 4,
        out_specs=[vmem] * 2,
        out_shape=[
            jax.ShapeDtypeStruct((4, 256, 2 * F), jnp.float32),
            jax.ShapeDtypeStruct((4, 128, D), jnp.float32),
        ],
    )(*pieces)


def finish_weights_kernel(*refs):
    pieces_a, pieces_b, outs, router_out = refs[0:4], refs[4:8], refs[8:11], refs[11]
    half = D // 2
    owner = lax.axis_index(EX)
    for rel in range(8):
        c, x, y = rel & 1, (rel >> 1) & 1, (rel >> 2) & 1
        at = jnp.bitwise_xor(owner, rel)
        rows = pl.ds(pl.multiple_of(at * 32, 32), 32)
        for i, piece in enumerate((pieces_a[2 * c + y].at[x], pieces_b[2 * c + x].at[y])):
            cols = pl.ds(half * i, half)
            for kind in range(3):
                outs[kind][rows, cols] = piece[32 * kind : 32 * kind + 32, :].astype(jnp.float32)
            router_out[at, :, cols] = piece[96:97, :].astype(jnp.float32)


def finish_weights(pieces_a, pieces_b):
    vmem = pl.BlockSpec(memory_space=pltpu.VMEM)
    return pl.pallas_call(
        finish_weights_kernel,
        in_specs=[vmem] * 8,
        out_specs=[vmem] * 4,
        out_shape=[jax.ShapeDtypeStruct((256, D), jnp.float32)] * 3
        + [jax.ShapeDtypeStruct((8, 1, D), jnp.float32)],
    )(*pieces_a, *pieces_b)


CORE, ACROSS, ALONG = 1, 2, 4


def swap(array, bit):
    return lax.ppermute(array, EX, [(i, i ^ bit) for i in range(8)])


def trade(array, step):
    return lax.ppermute(array, DP, [(i, i ^ step) for i in range(4)])


def everyone(array, axes):
    return lax.all_to_all(array, axes, split_axis=0, concat_axis=0, tiled=True)


def to_group(array, axes, count):
    return everyone(jnp.broadcast_to(array[None], (count,) + array.shape), axes)


def gather_halves(copies):
    column = everyone(copies, DP)
    return gather_plane(column[:, 0], column[:, 1])


def gather_traded(halves):
    traded = [halves] + [trade(halves, s) for s in range(1, 4)]
    here = lax.axis_index(DP)

    def at(place, column):
        picked = traded[3 ^ place][column]
        for z in range(2, -1, -1):
            picked = jnp.where(here == z, traded[z ^ place][column], picked)
        return picked

    a0, b0 = (jnp.stack([at(place, column) for place in range(4)]) for column in range(2))
    return gather_plane(a0, b0)


def gather_plane(a0, b0):
    a = jnp.stack([a0, swap(a0, ACROSS)])
    b = jnp.stack([b0, swap(b0, ALONG)])
    a_far, b_far = swap(a, ALONG), swap(b, ACROSS)
    pieces_a = [a, a_far, swap(a, CORE), swap(a_far, CORE)]
    pieces_b = [b, b_far, swap(b, CORE), swap(b_far, CORE)]
    return pieces_a, pieces_b


def add(one, two):
    return (one.astype(jnp.float32) + two.astype(jnp.float32)).astype(jnp.bfloat16)


def scatter_halves(pieces_a, pieces_b):
    a_far = add(pieces_a[1], swap(pieces_a[3], CORE))
    b_far = add(pieces_b[1], swap(pieces_b[3], CORE))
    a_near = add(pieces_a[0], swap(pieces_a[2], CORE))
    b_near = add(pieces_b[0], swap(pieces_b[2], CORE))
    a = add(a_near, swap(a_far, ALONG))
    b = add(b_near, swap(b_far, ACROSS))
    a_end, b_end = swap(a[1], ACROSS), swap(b[1], ALONG)
    a_own, b_own = add(a[0], a_end), add(b[0], b_end)
    return a_own, b_own


def block_inner(
    layer_input,
    segment_ids,
    expert_routes,
    first_gain,
    w_query,
    w_keyvalue,
    w_output,
    second_gain,
    w_router,
    w_gate_up,
    w_down,
    out_cotangent,
):
    half = D // 2
    owner_at = lax.axis_index(EX)

    def own_part(weight):
        return lax.dynamic_slice_in_dim(weight, owner_at * 32, 32, 0)

    def split(rows):
        return jnp.stack([rows[:, :half], rows[:, half:]])

    pack = jnp.concatenate([own_part(w_query), own_part(w_keyvalue), own_part(w_output)], axis=0)
    weights_a, weights_b = gather_halves(jnp.broadcast_to(split(pack)[None], (4, 2, 96, half)))
    routes = expert_routes.T
    small = jnp.stack(
        [routes.astype(jnp.bfloat16).reshape(D), own_part(w_router).T.reshape(32 * EXPERTS)]
    )
    small = to_group(small, (EX, DP), 32)
    all_routes = small[:, 0].astype(jnp.int32).reshape(32, TOPK, 128)
    router = small[:, 1].reshape(8, 4, EXPERTS, 32).transpose(2, 1, 0, 3)
    router = router.reshape(EXPERTS, D)

    sent = sliced(w_gate_up, w_down)
    weights = [w_gate_up, w_down] + [trade(sent[s - 1], s) for s in range(1, 4)]
    cot_a, cot_b = gather_traded(split(out_cotangent))

    def in_hbm(pieces):
        return [pltpu.with_memory_space_constraint(p, pltpu.HBM) for p in pieces]

    weights_a, weights_b = in_hbm(weights_a), in_hbm(weights_b)
    rope = jnp.asarray(np.stack(rope_constants(128)))
    shared = (segment_ids[None, :], first_gain[None, :], second_gain[None, :], rope)
    saved = attention_forward(weights_a, weights_b, layer_input, *shared)
    packed, hidden, scalars, normed2 = saved
    tok_a, tok_b = gather_halves(normed2)

    def flat(pieces):
        return [p.reshape(1024, half) for p in pieces]

    mix_a, mix_b, back_a, back_b, d_experts, d_gate = expert_call(
        flat(tok_a),
        flat(tok_b),
        flat(cot_a),
        flat(cot_b),
        weights,
        all_routes,
        router,
    )

    def deep(pieces):
        return [p.reshape(2, 4, 128, half) for p in pieces]

    back = everyone(jnp.stack(scatter_halves(deep(back_a), deep(back_b)), axis=1), DP)
    d_gates = everyone(d_gate, (EX, DP)).reshape(EXPERTS, 128)
    grads_a, grads_b, input_grad, d_gains, d_router = attention_backward(
        weights_a,
        weights_b,
        layer_input,
        *shared,
        packed,
        hidden,
        scalars,
        out_cotangent,
        back,
        d_gates,
        routes,
        router,
    )
    arrived = [d_experts[0]] + [trade(d_experts[s], s) for s in range(1, 4)]
    gate_up_grad, down_grad = finish_experts(arrived)
    mix_near = scatter_halves(deep(mix_a), deep(mix_b))
    group_at = lax.axis_index(DP)

    def part_for(step):
        at = jnp.bitwise_xor(group_at, step)
        pair = [lax.dynamic_index_in_dim(own, at, 0, keepdims=False) for own in mix_near]
        return jnp.stack(pair)

    mixed = part_for(0).astype(jnp.float32)
    for step in range(1, 4):
        mixed = mixed + trade(part_for(step), step).astype(jnp.float32)
    mixed = jnp.concatenate([mixed[0], mixed[1]], axis=1)
    layer_output = (hidden + residual_scale * mixed).astype(jnp.bfloat16)

    small = jnp.concatenate(
        [
            jnp.broadcast_to(d_gains.reshape(1, 2 * D), (32, 2 * D)),
            d_router.reshape(EXPERTS, 32, 32).transpose(1, 2, 0).reshape(32, D),
        ],
        axis=1,
    )
    small = jnp.sum(everyone(small, (DP, EX)), axis=0)
    first_gain_grad, second_gain_grad = small[:D], small[D : 2 * D]

    summed = jnp.stack(scatter_halves(grads_a, grads_b), axis=1)
    summed = everyone(summed, DP)
    summed = jnp.sum(summed.astype(jnp.float32), axis=0)
    summed = jnp.concatenate([summed, small[2 * D :].reshape(2, 1, half)], axis=1)
    summed = summed.astype(jnp.bfloat16)
    whole_a, whole_b = gather_plane(summed[0], summed[1])
    query_grad, keyvalue_grad, output_grad, router_grad = finish_weights(whole_a, whole_b)
    router_grad = router_grad.reshape(256, EXPERTS)
    return (
        layer_output,
        input_grad,
        first_gain_grad,
        query_grad,
        keyvalue_grad,
        output_grad,
        second_gain_grad,
        router_grad,
        gate_up_grad,
        down_grad,
    )


def block_device(*args):
    return block_inner(*args)


def solution(mesh):
    sizes = (mesh.shape[DP], mesh.shape[EX])
    return jax.shard_map(
        block_device if sizes == (4, 8) else general_device,
        mesh=mesh,
        in_specs=(
            P((DP, EX), None),
            P((DP, EX)),
            P((DP, EX), None),
            P(),
            P(DP, None),
            P(DP, None),
            P(DP, None),
            P(),
            P(DP, None),
            P(EX, DP, None),
            P(EX, DP, None),
            P((DP, EX), None),
        ),
        out_specs=(
            P((DP, EX), None),
            P((DP, EX), None),
            P(),
            P(DP, None),
            P(DP, None),
            P(DP, None),
            P(),
            P(DP, None),
            P(EX, DP, None),
            P(EX, DP, None),
        ),
        check_vma=False,
    )
```

```python
import jax
import jax.numpy as jnp
import numpy as np
from jax import lax
from jax.experimental import pallas as pl
from jax.experimental.pallas import tpu as pltpu
from jax.sharding import PartitionSpec as P

D = 1024
HEADS = 16
KV_HEADS = 8
HEAD_DIM = 64
F = 512
EXPERTS = 32
TOPK = 8
CAP = 40


epsilon = 1e-06
residual_scale = 0.22
score_scale = 0.015625
rope_base = 10000.0


def rope_tables(length, head_width):
    halfway = head_width // 2
    frequency = jnp.exp(
        -jnp.log(rope_base) * (2.0 * jnp.arange(halfway, dtype=jnp.float32) / head_width)
    )
    angles = jnp.arange(length, dtype=jnp.float32)[:, None] * frequency[None, :]
    cosine = jnp.concatenate([jnp.cos(angles), jnp.cos(angles)], axis=1)
    sine_table = jnp.concatenate([jnp.sin(angles), jnp.sin(angles)], axis=1)
    return (cosine, sine_table)


def rotate(values, cosine, sine_table, direction):
    halfway = values.shape[-1] // 2
    turned = jnp.concatenate([-values[..., halfway:], values[..., :halfway]], axis=-1)
    return values * cosine[:, None, :] + direction * turned * sine_table[:, None, :]


def norm_forward(inputs_f32, gain_vector):
    inverse = lax.rsqrt(jnp.mean(inputs_f32 * inputs_f32, axis=-1, keepdims=True) + epsilon)
    return (inputs_f32 * inverse * gain_vector, inverse)


def norm_backward(inputs_f32, inverse, gain_vector, upstream):
    weighted = upstream * gain_vector
    gain_part = jnp.sum(upstream * inputs_f32 * inverse, axis=0)
    through = inverse * weighted - inputs_f32 * (inverse * inverse * inverse) * jnp.mean(
        weighted * inputs_f32, axis=-1, keepdims=True
    )
    return (gain_part, through)


def activate(pre_act):
    gate_half = pre_act[..., :F]
    up_half = pre_act[..., F:]
    return gate_half * jax.nn.sigmoid(gate_half) * up_half


def activate_backward(pre_act, d_act):
    gate_half = pre_act[..., :F]
    up_half = pre_act[..., F:]
    sigmoid_gate = jax.nn.sigmoid(gate_half)
    d_gate = d_act * up_half * sigmoid_gate * (1.0 + gate_half * (1.0 - sigmoid_gate))
    d_up = d_act * gate_half * sigmoid_gate
    return jnp.concatenate([d_gate, d_up], axis=-1)


def masked_scores(query, keys, visible):
    raw_scores = (
        jnp.einsum("qkgd,pkd->kgqp", query, keys, preferred_element_type=jnp.float32) * score_scale
    )
    return jnp.where(visible[None, None], raw_scores, -1e30)


def attend_forward(normed, full_query, full_keyvalue, visible, cosine, sine_table):
    length = normed.shape[0]
    per_group = HEADS // KV_HEADS
    query_raw = jnp.dot(normed, full_query, preferred_element_type=jnp.float32).reshape(
        length, HEADS, HEAD_DIM
    )
    keyval = jnp.dot(normed, full_keyvalue, preferred_element_type=jnp.float32).reshape(
        length, 2, KV_HEADS, HEAD_DIM
    )
    query = (
        rotate(query_raw, cosine, sine_table, 1.0)
        .astype(jnp.bfloat16)
        .reshape(length, KV_HEADS, per_group, HEAD_DIM)
    )
    keys = rotate(keyval[:, 0], cosine, sine_table, 1.0).astype(jnp.bfloat16)
    values = keyval[:, 1].astype(jnp.bfloat16)
    scores = masked_scores(query, keys, visible)
    highest = jnp.max(scores, axis=-1, keepdims=True)
    log_total = highest + jnp.log(jnp.sum(jnp.exp(scores - highest), axis=-1, keepdims=True))
    probabilities = jnp.exp(scores - log_total).astype(jnp.bfloat16)
    attended = jnp.einsum(
        "kgqp,pkd->qkgd", probabilities, values, preferred_element_type=jnp.float32
    )
    attended = attended.reshape(length, HEADS * HEAD_DIM).astype(jnp.bfloat16)
    return (query, keys, values, attended, log_total)


def attend_backward(query, keys, values, attended, log_total, d_attended, visible):
    length = query.shape[0]
    per_group = HEADS // KV_HEADS
    scores = masked_scores(query, keys, visible)
    probs_f32 = jnp.exp(scores - log_total)
    probs_half = probs_f32.astype(jnp.bfloat16)
    d_att4 = d_attended.reshape(length, KV_HEADS, per_group, HEAD_DIM)
    att_four = attended.reshape(length, KV_HEADS, per_group, HEAD_DIM)
    d_values = jnp.einsum("kgqp,qkgd->pkd", probs_half, d_att4, preferred_element_type=jnp.float32)
    d_probs = jnp.einsum("qkgd,pkd->kgqp", d_att4, values, preferred_element_type=jnp.float32)
    row_delta = jnp.einsum("qkgd,qkgd->kgq", d_att4, att_four, preferred_element_type=jnp.float32)
    d_scores = (probs_f32 * (d_probs - row_delta[..., None]) * score_scale).astype(jnp.bfloat16)
    d_query = jnp.einsum(
        "kgqp,pkd->qkgd", d_scores, keys, preferred_element_type=jnp.float32
    ).reshape(length, HEADS, HEAD_DIM)
    d_keys = jnp.einsum("kgqp,qkgd->pkd", d_scores, query, preferred_element_type=jnp.float32)
    return (d_query, d_keys, d_values)


DP, EX = "dp", "expert"


def butterfly_sum(value, axes):
    for axis in axes:
        size = lax.axis_size(axis)
        step = 1
        while step < size:
            value = value + lax.ppermute(value, axis, [(i, i ^ step) for i in range(size)])
            step *= 2
    return value


def spread_over(axes, array):
    for axis in reversed(axes):
        array = lax.all_gather(array, axis, axis=0, tiled=True)
    return array


def sum_to_owner(axes, array):
    for axis in axes:
        array = lax.psum_scatter(array, axis, scatter_dimension=0, tiled=True)
    return array


def expert_pass(tokens, cotangents, gate, hit, w_up, w_dn):
    blocks = tokens.shape[0] // 128
    ranking = jnp.cumsum(hit.reshape(blocks, 128).astype(jnp.int32), axis=1) - 1
    slot = jnp.where(hit.reshape(blocks, 128), ranking, -1)
    select = slot[:, None, :] == jnp.arange(CAP, dtype=jnp.int32)[None, :, None]
    onehot = select.astype(jnp.bfloat16)
    rows = blocks * CAP
    picked = jnp.einsum(
        "bst,btd->bsd", onehot, tokens.reshape(blocks, 128, D), preferred_element_type=jnp.float32
    ).astype(jnp.bfloat16).reshape(rows, D)
    cot = jnp.einsum(
        "bst,btd->bsd",
        onehot,
        cotangents.reshape(blocks, 128, D),
        preferred_element_type=jnp.float32,
    ).reshape(rows, D)
    gate_slot = jnp.sum(
        jnp.where(select, gate.reshape(blocks, 1, 128), 0.0), axis=2
    ).reshape(rows, 1)
    pre_act = jnp.dot(picked, w_up, preferred_element_type=jnp.float32)
    activated = activate(pre_act).astype(jnp.bfloat16)
    result = (
        jnp.dot(activated, w_dn, preferred_element_type=jnp.float32)
        .astype(jnp.bfloat16)
        .astype(jnp.float32)
    )
    d_gate_slot = residual_scale * jnp.sum(cot * result, axis=1)
    d_gate = jnp.sum(jnp.where(select, d_gate_slot.reshape(blocks, CAP, 1), 0.0), axis=1)
    gated = (gate_slot * result).astype(jnp.bfloat16)
    mixed = jnp.einsum(
        "bst,bsd->btd", onehot, gated.reshape(blocks, CAP, D), preferred_element_type=jnp.float32
    ).reshape(blocks * 128, D)
    d_result = (residual_scale * gate_slot * cot).astype(jnp.bfloat16)
    d_act = jnp.dot(d_result, w_dn.T, preferred_element_type=jnp.float32)
    d_down = jnp.dot(activated.T, d_result, preferred_element_type=jnp.float32)
    d_pre = activate_backward(pre_act, d_act).astype(jnp.bfloat16)
    d_up = jnp.dot(picked.T, d_pre, preferred_element_type=jnp.float32)
    d_rows = jnp.dot(d_pre, w_up.T, preferred_element_type=jnp.float32).astype(jnp.bfloat16)
    back = jnp.einsum(
        "bst,bsd->btd", onehot, d_rows.reshape(blocks, CAP, D), preferred_element_type=jnp.float32
    ).reshape(blocks * 128, D)
    return (mixed, back, d_gate.reshape(blocks * 128), d_up, d_down)


def general_device(
    layer_input,
    segment_ids,
    expert_routes,
    first_gain,
    w_query,
    w_keyvalue,
    w_output,
    second_gain,
    w_router,
    w_gate_up,
    w_down,
    out_cotangent,
):
    length = layer_input.shape[0]
    owners = lax.axis_size(EX)
    groups = lax.axis_size(DP)
    group_at = lax.axis_index(DP)
    owner_at = lax.axis_index(EX)
    per_owner = w_gate_up.shape[0]
    shard = w_query.shape[0]
    part = shard // owners
    every = (DP, EX)

    def own_part(weight):
        return lax.dynamic_slice_in_dim(weight, owner_at * part, part, 0)

    pack = jnp.concatenate([own_part(w_query), own_part(w_keyvalue), own_part(w_output)], axis=0)
    gathered = lax.all_gather(pack, every, axis=0).reshape(groups * owners, 3, part, D)
    full_query = gathered[:, 0].reshape(D, HEADS * HEAD_DIM)
    full_keyvalue = gathered[:, 1].reshape(D, 2 * KV_HEADS * HEAD_DIM)
    full_output = gathered[:, 2].reshape(HEADS * HEAD_DIM, D)
    full_router = lax.all_gather(own_part(w_router), every, axis=0, tiled=True)

    exchange = per_owner % groups == 0
    if exchange:
        local = per_owner // groups
        token_axes = (EX, DP)
        first_expert = owner_at * per_owner + group_at * local
        own_up = lax.all_to_all(w_gate_up, DP, split_axis=0, concat_axis=1, tiled=True)
        own_down = lax.all_to_all(w_down, DP, split_axis=0, concat_axis=1, tiled=True)
    else:
        local = per_owner
        token_axes = (EX,)
        first_expert = owner_at * per_owner
        own_up = lax.all_gather(w_gate_up, DP, axis=1, tiled=True)
        own_down = lax.all_gather(w_down, DP, axis=1, tiled=True)
    all_routes = spread_over(token_axes, expert_routes)
    all_cotangents = spread_over(token_axes, out_cotangent)

    cosine, sine_table = rope_tables(length, HEAD_DIM)
    places = jnp.arange(length)
    visible = (places[:, None] >= places[None, :]) & (segment_ids[:, None] == segment_ids[None, :])
    inputs_f32 = layer_input.astype(jnp.float32)
    normed, inverse = norm_forward(inputs_f32, first_gain)
    normed = normed.astype(jnp.bfloat16)
    query, keys, values, attended, log_total = attend_forward(
        normed, full_query, full_keyvalue, visible, cosine, sine_table
    )
    hidden = inputs_f32 + residual_scale * jnp.dot(
        attended, full_output, preferred_element_type=jnp.float32
    )
    normed2, inverse2 = norm_forward(hidden, second_gain)
    normed2 = normed2.astype(jnp.bfloat16)
    all_normed2 = spread_over(token_axes, normed2)

    def gates_of(rows, routes):
        named = jnp.any(
            routes[:, :, None] == jnp.arange(EXPERTS, dtype=jnp.int32)[None, None, :], axis=1
        )
        logits = jnp.dot(rows, full_router, preferred_element_type=jnp.float32)
        highest = jnp.max(jnp.where(named, logits, -jnp.inf), axis=1, keepdims=True)
        exponent = jnp.where(named, jnp.exp(jnp.where(named, logits - highest, 0.0)), 0.0)
        return exponent / jnp.sum(exponent, axis=1, keepdims=True)

    all_gates = gates_of(all_normed2, all_routes)
    d_out = out_cotangent.astype(jnp.float32)
    mixed, back = 0.0, 0.0
    d_gate_list, up_list, down_list = [], [], []
    for j in range(local):
        hit = jnp.any(all_routes == first_expert + j, axis=1)
        gate = lax.dynamic_index_in_dim(all_gates, first_expert + j, 1, keepdims=False)
        one_mixed, one_back, d_gate, d_up, d_dn = expert_pass(
            all_normed2, all_cotangents, gate, hit, own_up[j], own_down[j]
        )
        mixed, back = mixed + one_mixed, back + one_back
        d_gate_list.append(d_gate)
        up_list.append(d_up.astype(jnp.bfloat16))
        down_list.append(d_dn.astype(jnp.bfloat16))
    back_own = sum_to_owner(token_axes, back.astype(jnp.bfloat16)).astype(jnp.float32)
    sources = EXPERTS // local
    d_gate_out = jnp.stack(d_gate_list).reshape(local, sources, length).transpose(1, 0, 2)
    d_gates = (
        lax.all_to_all(d_gate_out, token_axes, split_axis=0, concat_axis=0, tiled=True)
        .reshape(EXPERTS, length)
        .T
    )
    d_up_all, d_down_all = jnp.stack(up_list), jnp.stack(down_list)
    if exchange:
        gate_up_grad = lax.all_to_all(d_up_all, DP, split_axis=1, concat_axis=0, tiled=True)
        down_grad = lax.all_to_all(d_down_all, DP, split_axis=1, concat_axis=0, tiled=True)
    else:
        gate_up_grad = lax.psum_scatter(d_up_all, DP, scatter_dimension=1, tiled=True)
        down_grad = lax.psum_scatter(d_down_all, DP, scatter_dimension=1, tiled=True)
    mixed_own = sum_to_owner(token_axes, mixed.astype(jnp.bfloat16)).astype(jnp.float32)
    layer_output = (hidden + residual_scale * mixed_own).astype(jnp.bfloat16)

    gates = gates_of(normed2, expert_routes)
    d_logits = (gates * (d_gates - jnp.sum(gates * d_gates, axis=1, keepdims=True))).astype(
        jnp.bfloat16
    )
    d_router = jnp.dot(normed2.T, d_logits, preferred_element_type=jnp.float32)
    d_normed2 = back_own + jnp.dot(d_logits, full_router.T, preferred_element_type=jnp.float32)
    d_second_gain, d_through = norm_backward(hidden, inverse2, second_gain, d_normed2)
    second_gain_grad = butterfly_sum(d_second_gain, (EX, DP))
    d_hidden = d_out + d_through
    d_branch = (residual_scale * d_hidden).astype(jnp.bfloat16)
    d_wout = jnp.dot(attended.T, d_branch, preferred_element_type=jnp.float32)
    d_attended = jnp.dot(d_branch, full_output.T, preferred_element_type=jnp.float32).astype(
        jnp.bfloat16
    )
    d_query, d_keys, d_values = attend_backward(
        query, keys, values, attended, log_total, d_attended, visible
    )
    d_query = (
        rotate(d_query, cosine, sine_table, -1.0)
        .reshape(length, HEADS * HEAD_DIM)
        .astype(jnp.bfloat16)
    )
    d_keys = rotate(d_keys, cosine, sine_table, -1.0)
    d_keyvalue = (
        jnp.stack([d_keys, d_values], axis=1)
        .reshape(length, 2 * KV_HEADS * HEAD_DIM)
        .astype(jnp.bfloat16)
    )
    d_wquery = jnp.dot(normed.T, d_query, preferred_element_type=jnp.float32)
    d_wkeyvalue = jnp.dot(normed.T, d_keyvalue, preferred_element_type=jnp.float32)
    d_normed = jnp.dot(d_query, full_query.T, preferred_element_type=jnp.float32) + jnp.dot(
        d_keyvalue, full_keyvalue.T, preferred_element_type=jnp.float32
    )
    d_first_gain, d_inputs = norm_backward(inputs_f32, inverse, first_gain, d_normed)
    first_gain_grad = butterfly_sum(d_first_gain, (EX, DP))
    input_grad = (d_hidden + d_inputs).astype(jnp.bfloat16)

    def reduced(*grads):
        packed = jnp.stack([g.astype(jnp.bfloat16) for g in grads])
        count, width = len(grads), grads[0].shape[1]
        packed = packed.reshape(count, groups, owners, part, width).transpose(2, 1, 0, 3, 4)
        packed = packed.reshape(owners * groups * count * part, width)
        mine = sum_to_owner((EX, DP), packed).reshape(1, count, part, width)
        whole = lax.all_gather(mine, EX, axis=0, tiled=True)
        whole = whole.transpose(1, 0, 2, 3).reshape(count, owners * part, width)
        return [whole[i].astype(jnp.float32) for i in range(count)]

    output_grad, query_grad, keyvalue_grad = reduced(d_wout, d_wquery, d_wkeyvalue)
    (router_grad,) = reduced(d_router)
    return (
        layer_output,
        input_grad,
        first_gain_grad,
        query_grad,
        keyvalue_grad,
        output_grad,
        second_gain_grad,
        router_grad,
        gate_up_grad.astype(jnp.float32),
        down_grad.astype(jnp.float32),
    )


def expert_kernel(*refs):
    tok_a, tok_b, cot_a, cot_b = refs[0:4], refs[4:8], refs[8:12], refs[12:16]
    own_up, own_down, pieces = refs[16], refs[17], refs[18:21]
    routes_ref, router_ref = refs[21:23]
    mix_a, mix_b, back_a, back_b = refs[23:27], refs[27:31], refs[31:35], refs[35:39]
    grad_pieces, dgate_ref = refs[39:43], refs[43]
    (
        tok_buf,
        cot_buf,
        mix_buf,
        back_buf,
        rows_scr,
        act_scr,
        dres_scr,
        dpre_scr,
        cot_scr,
        gate_scr,
        slot_scr,
        tri_scr,
        up_scr,
        down_scr,
        d_up_scr,
        d_down_scr,
        in_sem,
        out_sem,
        weight_sem,
        grad_sem,
    ) = refs[44:]
    half = D // 2
    owner, group = lax.axis_index(EX), lax.axis_index(DP)
    expert = owner * 4 + group
    chunk_rows = 8 * CAP

    def chunk_copies(kk, slot, sources, sem, outward):
        c, y = kk // 2, kk % 2
        ends = []
        for a, b, buf in sources:
            ends.append((a[kk], buf.at[slot, :, pl.ds(0, half)]))
            for x in range(2):
                ends.append(
                    (
                        b[2 * c + x].at[pl.ds(512 * y, 512), :],
                        buf.at[slot, pl.ds(512 * x, 512), pl.ds(half, half)],
                    )
                )
        if outward:
            ends = [(there, here) for here, there in ends]
        return [
            pltpu.make_async_copy(*pair, sem.at[slot, i]) for i, pair in enumerate(ends)
        ]

    def in_copies(kk, slot):
        sources = ((tok_a, tok_b, tok_buf), (cot_a, cot_b, cot_buf))
        return chunk_copies(kk, slot, sources, in_sem, False)

    def out_copies(kk, slot):
        sources = ((back_a, back_b, back_buf), (mix_a, mix_b, mix_buf))
        return chunk_copies(kk, slot, sources, out_sem, True)

    def weight_pairs():
        found = []
        for s in range(4):
            at = jnp.bitwise_xor(group, s)
            up_from, down_from = own_up.at[group], own_down.at[group]
            if s > 0:
                up_from = pieces[s - 1].at[pl.ds(0, 256), :]
                down_from = pieces[s - 1].at[pl.ds(256, 128), :]
            found.append(pltpu.make_async_copy(up_from, up_scr.at[at], weight_sem.at[0, s]))
            found.append(pltpu.make_async_copy(down_from, down_scr.at[at], weight_sem.at[1, s]))
        return found

    for copy in in_copies(0, 0) + weight_pairs():
        copy.start()
    before = lax.broadcasted_iota(jnp.int32, (256, 256), 0)
    after = lax.broadcasted_iota(jnp.int32, (256, 256), 1)
    tri_scr[...] = ((before <= after) & ((before < 128) == (after < 128))).astype(jnp.bfloat16)

    def pair_mask(pair):
        return slot_scr[pair] == lax.broadcasted_iota(jnp.int32, (2 * CAP, 256), 0)

    def chunk_step(k, carry):
        for kk in range(4):

            @pl.when(k == kk)
            def _():
                if kk < 3:
                    for copy in in_copies(kk + 1, (kk + 1) % 2):
                        copy.start()
                for copy in in_copies(kk, kk % 2):
                    copy.wait()
                if kk >= 2:
                    for copy in out_copies(kk - 2, kk % 2):
                        copy.wait()

        at = lax.rem(k, 2)
        base = pl.multiple_of(k * chunk_rows, chunk_rows)
        away = k // 2 + 4 * lax.rem(k, 2)
        for pair in range(4):
            device = jnp.bitwise_xor(owner, away + 2 * (pair // 2)) * 4 + 2 * (pair % 2)
            routes = jnp.concatenate([routes_ref[device], routes_ref[device + 1]], axis=1)
            hit = jnp.max((routes == expert).astype(jnp.float32), axis=0, keepdims=True)
            rank = jnp.dot(
                jnp.broadcast_to(hit, (16, 256)).astype(jnp.bfloat16),
                tri_scr[...],
                preferred_element_type=jnp.float32,
            )[0:1]
            second = lax.broadcasted_iota(jnp.int32, (1, 256), 1) >= 128
            slot = rank.astype(jnp.int32) - 1 + jnp.where(second, CAP, 0)
            slot_scr[pair] = jnp.where(hit > 0.5, slot, -1)
            mask = pair_mask(pair)
            onehot = mask.astype(jnp.bfloat16)
            token_rows = tok_buf[at, pl.ds(256 * pair, 256), :]
            logits = lax.dot_general(
                router_ref[...],
                token_rows,
                (((1,), (1,)), ((), ())),
                preferred_element_type=jnp.float32,
            )
            names = lax.broadcasted_iota(jnp.int32, (EXPERTS, 256), 0)
            named = routes[0:1] == names
            for i in range(1, TOPK):
                named = named | (routes[i : i + 1] == names)
            highest = jnp.max(jnp.where(named, logits, -3e38), axis=0, keepdims=True)
            exponent = jnp.where(named, jnp.exp(jnp.where(named, logits - highest, 0.0)), 0.0)
            own = jnp.sum(jnp.where(names == expert, exponent, 0.0), axis=0, keepdims=True)
            gate = own / jnp.sum(exponent, axis=0, keepdims=True)
            gate_slot = jnp.sum(jnp.where(mask, gate, 0.0), axis=1, keepdims=True)
            gate_scr[pl.ds(2 * CAP * pair, 2 * CAP), :] = gate_slot
            place = pl.ds(base + 2 * CAP * pair, 2 * CAP)
            rows_scr[place, :] = jnp.dot(
                onehot, token_rows, preferred_element_type=jnp.float32
            ).astype(jnp.bfloat16)
            cot = jnp.dot(
                onehot, cot_buf[at, pl.ds(256 * pair, 256), :], preferred_element_type=jnp.float32
            )
            cot_scr[pl.ds(2 * CAP * pair, 2 * CAP), :] = cot.astype(jnp.bfloat16)
            dres_scr[place, :] = (residual_scale * gate_slot * cot).astype(jnp.bfloat16)

        @pl.when(k == 0)
        def _():
            for copy in weight_pairs():
                copy.wait()

        here = pl.ds(base, chunk_rows)
        pre = jnp.dot(rows_scr[here, :], up_scr[...].reshape(D, 2 * F), preferred_element_type=jnp.float32)
        gate_half, up_half = pre[:, :F], pre[:, F:]
        sigmoid_gate = 1.0 / (1.0 + jnp.exp(-gate_half))
        swish = gate_half * sigmoid_gate
        activated = (swish * up_half).astype(jnp.bfloat16)
        act_scr[here, :] = activated
        d_act = lax.dot_general(
            dres_scr[here, :],
            down_scr[...].reshape(F, D),
            (((1,), (1,)), ((), ())),
            preferred_element_type=jnp.float32,
        )
        dpre_scr[here, 0:F] = (
            d_act * up_half * sigmoid_gate * (1.0 + gate_half * (1.0 - sigmoid_gate))
        ).astype(jnp.bfloat16)
        dpre_scr[here, F : 2 * F] = (d_act * swish).astype(jnp.bfloat16)
        result = (
            jnp.dot(activated, down_scr[...].reshape(F, D), preferred_element_type=jnp.float32)
            .astype(jnp.bfloat16)
            .astype(jnp.float32)
        )
        d_gate_slot = residual_scale * jnp.sum(
            cot_scr[...].astype(jnp.float32) * result, axis=1, keepdims=True
        )
        gated = (gate_scr[...] * result).astype(jnp.bfloat16)
        d_rows = lax.dot_general(
            dpre_scr[here, :],
            up_scr[...].reshape(D, 2 * F),
            (((1,), (1,)), ((), ())),
            preferred_element_type=jnp.float32,
        ).astype(jnp.bfloat16)
        for pair in range(4):
            device = jnp.bitwise_xor(owner, away + 2 * (pair // 2)) * 4 + 2 * (pair % 2)
            mask = pair_mask(pair)
            onehot = mask.astype(jnp.bfloat16)
            mine = slice(2 * CAP * pair, 2 * CAP * (pair + 1))
            d_gate = jnp.sum(jnp.where(mask, d_gate_slot[mine], 0.0), axis=0, keepdims=True)
            dgate_ref[device] = d_gate[:, :128]
            dgate_ref[device + 1] = d_gate[:, 128:]
            rows = pl.ds(256 * pair, 256)
            mix_buf[at, rows, :] = lax.dot_general(
                onehot,
                gated[mine],
                (((0,), (0,)), ((), ())),
                preferred_element_type=jnp.float32,
            ).astype(jnp.bfloat16)
            back_buf[at, rows, :] = lax.dot_general(
                onehot,
                d_rows[mine],
                (((0,), (0,)), ((), ())),
                preferred_element_type=jnp.float32,
            ).astype(jnp.bfloat16)
        for kk in range(4):

            @pl.when(k == kk)
            def _():
                for copy in out_copies(kk, kk % 2):
                    copy.start()

        return carry

    lax.fori_loop(0, 4, chunk_step, 0)

    def up_step(t, carry):
        at = jnp.bitwise_xor(group, t)
        d_up_scr[t] = lax.dot_general(
            rows_scr[:, pl.ds(pl.multiple_of(at * 256, 256), 256)],
            dpre_scr[...],
            (((0,), (0,)), ((), ())),
            preferred_element_type=jnp.float32,
        ).astype(jnp.bfloat16)
        d_down_scr[t] = lax.dot_general(
            act_scr[:, pl.ds(pl.multiple_of(at * 128, 128), 128)],
            dres_scr[...],
            (((0,), (0,)), ((), ())),
            preferred_element_type=jnp.float32,
        ).astype(jnp.bfloat16)
        for s in range(4):

            @pl.when(t == s)
            def _():
                for copy in grad_copies(s):
                    copy.start()

        return carry

    def grad_copies(s):
        return (
            pltpu.make_async_copy(
                d_up_scr.at[s], grad_pieces[s].at[pl.ds(0, 256), :], grad_sem.at[0, s]
            ),
            pltpu.make_async_copy(
                d_down_scr.at[s], grad_pieces[s].at[pl.ds(256, 128), :], grad_sem.at[1, s]
            ),
        )

    lax.fori_loop(0, 4, up_step, 0)
    for kk in (2, 3):
        for copy in out_copies(kk, kk % 2):
            copy.wait()
    for s in range(4):
        for copy in grad_copies(s):
            copy.wait()


def expert_call(tok_a, tok_b, cot_a, cot_b, weights, routes, router):
    half = D // 2
    token_count = 1024
    hbm = pl.BlockSpec(memory_space=pltpu.HBM)
    vmem = pl.BlockSpec(memory_space=pltpu.VMEM)
    slots = 32 * CAP
    b16 = jnp.bfloat16
    piece = jax.ShapeDtypeStruct((token_count, half), b16)
    far = pltpu.HBM((token_count, half), b16)
    outs = pl.pallas_call(
        expert_kernel,
        in_specs=[hbm] * 21 + [vmem] * 2,
        out_specs=[hbm] * 20 + [vmem],
        out_shape=([piece] * 2 + [far] * 2) * 4
        + [jax.ShapeDtypeStruct((384, D), b16)]
        + [pltpu.HBM((384, D), b16)] * 3
        + [jax.ShapeDtypeStruct((32, 1, 128), jnp.float32)],
        scratch_shapes=[pltpu.VMEM((2, token_count, D), b16)] * 4
        + [
            pltpu.VMEM((slots, D), b16),
            pltpu.VMEM((slots, F), b16),
            pltpu.VMEM((slots, D), b16),
            pltpu.VMEM((slots, 2 * F), b16),
            pltpu.VMEM((8 * CAP, D), b16),
            pltpu.VMEM((8 * CAP, 1), jnp.float32),
            pltpu.VMEM((4, 1, 256), jnp.int32),
            pltpu.VMEM((256, 256), b16),
            pltpu.VMEM((4, 256, 2 * F), b16),
            pltpu.VMEM((4, 128, D), b16),
            pltpu.VMEM((4, 256, 2 * F), b16),
            pltpu.VMEM((4, 128, D), b16),
            pltpu.SemaphoreType.DMA((2, 6)),
            pltpu.SemaphoreType.DMA((2, 6)),
            pltpu.SemaphoreType.DMA((2, 4)),
            pltpu.SemaphoreType.DMA((2, 4)),
        ],
        compiler_params=pltpu.CompilerParams(vmem_limit_bytes=48 * 1024 * 1024),
    )(*tok_a, *tok_b, *cot_a, *cot_b, *weights, routes, router)
    groups = [outs[4 * i : 4 * i + 4] for i in range(5)]
    return (*groups, outs[20])


def rope_constants(length):
    frequency = rope_base ** (-2.0 * np.arange(HEAD_DIM // 2) / HEAD_DIM)
    angles = np.arange(length)[:, None] * frequency[None, :]
    cosine = np.tile(np.cos(angles), (1, 4)).astype(np.float32)
    sine = np.sin(angles)
    signed = np.concatenate([-sine, sine, -sine, sine], axis=1).astype(np.float32)
    return cosine, signed


def turn(slab, cosine, signed):
    low = (lax.broadcasted_iota(jnp.int32, slab.shape, 1) & 32) == 0
    swapped = jnp.where(low, pltpu.roll(slab, 96, 1), pltpu.roll(slab, 32, 1))
    return slab * cosine + swapped * signed


def halves_stacked(slab, low):
    zero = jnp.zeros_like(slab)
    return jnp.concatenate([jnp.where(low, slab, zero), jnp.where(low, zero, slab)], axis=0)


def doubled(slab, low, second):
    other = pltpu.roll(slab, 64, 1)
    return jnp.where(low, other, slab) if second else jnp.where(low, slab, other)


def weight_copies(pieces_a, pieces_b, whole, sems, owner, kind, outward):
    half = D // 2
    copies = []
    for rel in range(8):
        c, x, y = rel & 1, (rel >> 1) & 1, (rel >> 2) & 1
        at = jnp.bitwise_xor(owner, rel)
        rows = pl.ds(32 * kind, 32)
        ends = (
            (pieces_a[2 * c + y].at[x, :, rows, :], whole.at[kind, :, at, :, pl.ds(0, half)]),
            (pieces_b[2 * c + x].at[y, :, rows, :], whole.at[kind, :, at, :, pl.ds(half, half)]),
        )
        for i, (piece, place) in enumerate(ends):
            pair = (place, piece) if outward else (piece, place)
            copies.append(pltpu.make_async_copy(*pair, sems.at[kind, rel, i]))
    return copies


def seen(seg_row, rows_at, cols_at):
    row = seg_row.astype(jnp.float32)
    column = jnp.sum(jnp.where(rows_at == cols_at, row, 0.0), axis=1, keepdims=True)
    return (rows_at >= cols_at) & (column == row)


def packed_views(pack_ref):
    starts = (0, D, 2 * D, 2 * D + D // 2, 3 * D, 4 * D)
    return [pack_ref.at[:, pl.ds(a, b - a)] for a, b in zip(starts[:-1], starts[1:])]


def attention_forward_kernel(*refs):
    pieces_a, pieces_b = refs[0:4], refs[4:8]
    arrays, finals, buffers = refs[8:13], refs[13:17], refs[17:22]
    x_ref, seg_row, gain1_ref, gain2_ref, rope_ref = buffers
    pack_ref, hidden_ref, small_ref, normed2_ref, whole, sems, out_sems, load_sems = refs[22:]
    loads = [
        pltpu.make_async_copy(there, here, load_sems.at[i])
        for i, (there, here) in enumerate(zip(arrays, buffers))
    ]
    for load in loads:
        load.start()
    outs = [
        pltpu.make_async_copy(here, there, out_sems.at[i])
        for i, (here, there) in enumerate(zip(refs[22:26], finals))
    ]
    normed_ref, q_ref, k_ref, v_ref, att_ref = packed_views(pack_ref)
    owner = lax.axis_index(EX)
    half = D // 2
    for kind in range(3):
        for copy in weight_copies(pieces_a, pieces_b, whole, sems, owner, kind, False):
            copy.start()
    for load in loads:
        load.wait()
    inputs = x_ref[...].astype(jnp.float32)
    inverse = lax.rsqrt(jnp.mean(inputs * inputs, axis=1, keepdims=True) + epsilon)
    normed = (inputs * inverse * gain1_ref[...]).astype(jnp.bfloat16)
    normed_ref[...] = normed
    small_ref[:128, 8:9] = inverse
    cosine, signed = rope_ref[0], rope_ref[1]
    for kind in range(2):
        for copy in weight_copies(pieces_a, pieces_b, whole, sems, owner, kind, False):
            copy.wait()
    query = jnp.dot(normed, whole[0].reshape(D, D), preferred_element_type=jnp.float32)
    keyval = jnp.dot(normed, whole[1].reshape(D, D), preferred_element_type=jnp.float32)
    for s in range(8):
        cols = slice(128 * s, 128 * s + 128)
        q_ref[:, cols] = turn(query[:, cols], cosine, signed).astype(jnp.bfloat16)
    for s in range(4):
        cols = slice(128 * s, 128 * s + 128)
        k_ref[:, cols] = turn(keyval[:, cols], cosine, signed).astype(jnp.bfloat16)
    v_ref[...] = keyval[:, half:].astype(jnp.bfloat16)
    rows_at = lax.broadcasted_iota(jnp.int32, (128, 128), 0)
    cols_at = lax.broadcasted_iota(jnp.int32, (128, 128), 1)
    visible = seen(seg_row[...], rows_at, cols_at)
    visible2 = jnp.concatenate([visible, visible], axis=0)
    low = cols_at < 64
    for head in range(KV_HEADS):
        slab = slice(128 * (head // 2), 128 * (head // 2) + 128)
        q2 = halves_stacked(q_ref[:, 128 * head : 128 * head + 128], low)
        k2 = doubled(k_ref[:, slab], low, head % 2)
        v2 = doubled(v_ref[:, slab], low, head % 2)
        scores = lax.dot_general(
            q2, k2, (((1,), (1,)), ((), ())), preferred_element_type=jnp.float32
        )
        scores = jnp.where(visible2, scores * score_scale, -1e30)
        highest = jnp.max(scores, axis=1, keepdims=True)
        log_total = highest + jnp.log(jnp.sum(jnp.exp(scores - highest), axis=1, keepdims=True))
        probabilities = jnp.exp(scores - log_total).astype(jnp.bfloat16)
        small_ref[:, head : head + 1] = log_total
        mixed = jnp.dot(probabilities, v2, preferred_element_type=jnp.float32)
        att_ref[:, 128 * head : 128 * head + 128] = jnp.where(
            low, mixed[:128], mixed[128:]
        ).astype(jnp.bfloat16)
    for copy in weight_copies(pieces_a, pieces_b, whole, sems, owner, 2, False):
        copy.wait()
    outs[0].start()
    hidden = inputs + residual_scale * jnp.dot(
        att_ref[...], whole[2].reshape(D, D), preferred_element_type=jnp.float32
    )
    inverse2 = lax.rsqrt(jnp.mean(hidden * hidden, axis=1, keepdims=True) + epsilon)
    normed2 = (hidden * inverse2 * gain2_ref[...]).astype(jnp.bfloat16)
    hidden_ref[...] = hidden
    small_ref[:128, 9:10] = inverse2
    outs[1].start()
    outs[2].start()
    for z in range(4):
        normed2_ref[z, 0] = normed2[:, :half]
        normed2_ref[z, 1] = normed2[:, half:]
    outs[3].start()
    for out in outs:
        out.wait()


def attention_forward(pieces_a, pieces_b, *rest):
    hbm = pl.BlockSpec(memory_space=pltpu.HBM)
    f32, b16 = jnp.float32, jnp.bfloat16
    shapes = [
        ((128, 4 * D), b16),
        ((128, D), f32),
        ((256, 16), f32),
        ((4, 2, 128, D // 2), b16),
    ]
    return pl.pallas_call(
        attention_forward_kernel,
        in_specs=[hbm] * (8 + len(rest)),
        out_specs=[hbm] * 4,
        out_shape=[pltpu.HBM(s, t) for s, t in shapes],
        scratch_shapes=[pltpu.VMEM(array.shape, array.dtype) for array in rest]
        + [pltpu.VMEM(s, t) for s, t in shapes]
        + [
            pltpu.VMEM((3, 4, 8, 32, D), b16),
            pltpu.SemaphoreType.DMA((3, 8, 2)),
            pltpu.SemaphoreType.DMA((4,)),
            pltpu.SemaphoreType.DMA((len(rest),)),
        ],
        compiler_params=pltpu.CompilerParams(vmem_limit_bytes=40 * 1024 * 1024),
    )(*pieces_a, *pieces_b, *rest)


def attention_backward_kernel(*refs):
    pieces_a, pieces_b = refs[0:4], refs[4:8]
    arrays = refs[8:21]
    grads_a, grads_b = refs[21:25], refs[25:29]
    finals = refs[29:32]
    buffers = refs[32:45]
    (
        x_ref,
        seg_row,
        gain1_ref,
        gain2_ref,
        rope_ref,
        pack_ref,
        hidden_ref,
        small_ref,
        dout_ref,
        back_ref,
        dgate_ref,
        routes_ref,
        router_ref,
    ) = buffers
    input_grad_ref, gains_ref, router_grad_ref = refs[45:48]
    whole, grad, datt_scr, dq_scr, dkv_scr, sems, out_sems, load_sems, last_sems = refs[48:]
    loads = [
        pltpu.make_async_copy(there, here, load_sems.at[i])
        for i, (there, here) in enumerate(zip(arrays, buffers))
    ]
    lasts = [
        pltpu.make_async_copy(here, there, last_sems.at[i])
        for i, (here, there) in enumerate(zip(refs[45:48], finals))
    ]
    for load in loads:
        load.start()
    normed_ref, q_ref, k_ref, v_ref, att_ref = packed_views(pack_ref)
    owner = lax.axis_index(EX)
    half = D // 2
    for kind in (2, 0, 1):
        for copy in weight_copies(pieces_a, pieces_b, whole, sems, owner, kind, False):
            copy.start()
    for load in loads:
        load.wait()
    hidden, inverse2 = hidden_ref[...], small_ref[:128, 9:10]
    normed2 = (hidden * inverse2 * gain2_ref[...]).astype(jnp.bfloat16)
    names = lax.broadcasted_iota(jnp.int32, (EXPERTS, 128), 0)
    routes = routes_ref[...]
    named = routes[0:1] == names
    for i in range(1, TOPK):
        named = named | (routes[i : i + 1] == names)
    logits = lax.dot_general(
        router_ref[...], normed2, (((1,), (1,)), ((), ())), preferred_element_type=jnp.float32
    )
    highest = jnp.max(jnp.where(named, logits, -3e38), axis=0, keepdims=True)
    exponent = jnp.where(named, jnp.exp(jnp.where(named, logits - highest, 0.0)), 0.0)
    gates = exponent / jnp.sum(exponent, axis=0, keepdims=True)
    d_gates = dgate_ref[...]
    d_logits = (gates * (d_gates - jnp.sum(gates * d_gates, axis=0, keepdims=True))).astype(
        jnp.bfloat16
    )
    router_grad_ref[...] = jnp.dot(d_logits, normed2, preferred_element_type=jnp.float32)
    back = [
        sum(back_ref[z, i].astype(jnp.float32) for z in range(4)) for i in range(2)
    ]
    d_normed2 = jnp.concatenate(back, axis=1) + lax.dot_general(
        d_logits, router_ref[...], (((0,), (0,)), ((), ())), preferred_element_type=jnp.float32
    )
    gains_ref[1:2, :] = jnp.sum(d_normed2 * hidden * inverse2, axis=0, keepdims=True)
    weighted = d_normed2 * gain2_ref[...]
    d_hidden = (
        dout_ref[...].astype(jnp.float32)
        + inverse2 * weighted
        - hidden
        * (inverse2 * inverse2 * inverse2)
        * jnp.mean(weighted * hidden, axis=1, keepdims=True)
    )
    d_branch = (residual_scale * d_hidden).astype(jnp.bfloat16)
    tn = (((0,), (0,)), ((), ()))
    nt = (((1,), (1,)), ((), ()))
    for z in range(4):
        grad[2, z] = (
            lax.dot_general(
                att_ref[:, 256 * z : 256 * z + 256], d_branch, tn, preferred_element_type=jnp.float32
            )
            .astype(jnp.bfloat16)
            .reshape(8, 32, D)
        )
    for copy in weight_copies(grads_a, grads_b, grad, out_sems, owner, 2, True):
        copy.start()
    for copy in weight_copies(pieces_a, pieces_b, whole, sems, owner, 2, False):
        copy.wait()
    datt_scr[...] = lax.dot_general(
        d_branch, whole[2].reshape(D, D), nt, preferred_element_type=jnp.float32
    ).astype(jnp.bfloat16)
    cosine, signed = rope_ref[0], -rope_ref[1]
    rows_at = lax.broadcasted_iota(jnp.int32, (128, 128), 0)
    cols_at = lax.broadcasted_iota(jnp.int32, (128, 128), 1)
    visible = seen(seg_row[...], rows_at, cols_at)
    visible2 = jnp.concatenate([visible, visible], axis=0)
    low = cols_at < 64
    keep_k = keep_v = None
    for head in range(KV_HEADS):
        cols = slice(128 * head, 128 * head + 128)
        slab = slice(128 * (head // 2), 128 * (head // 2) + 128)
        q2 = halves_stacked(q_ref[:, cols], low)
        k2 = doubled(k_ref[:, slab], low, head % 2)
        v2 = doubled(v_ref[:, slab], low, head % 2)
        d_att = datt_scr[:, cols]
        da2 = halves_stacked(d_att, low)
        scores = lax.dot_general(q2, k2, nt, preferred_element_type=jnp.float32)
        scores = jnp.where(visible2, scores * score_scale, -1e30)
        probs = jnp.exp(scores - small_ref[:, head : head + 1])
        d_value = lax.dot_general(
            probs.astype(jnp.bfloat16), da2, tn, preferred_element_type=jnp.float32
        )
        d_probs = lax.dot_general(da2, v2, nt, preferred_element_type=jnp.float32)
        product = d_att.astype(jnp.float32) * att_ref[:, cols].astype(jnp.float32)
        delta = jnp.sum(halves_stacked(product, low), axis=1, keepdims=True)
        d_scores = (probs * (d_probs - delta) * score_scale).astype(jnp.bfloat16)
        d_q2 = jnp.dot(d_scores, k2, preferred_element_type=jnp.float32)
        d_query = jnp.where(low, d_q2[:128], d_q2[128:])
        dq_scr[:, cols] = turn(d_query, cosine, signed).astype(jnp.bfloat16)
        d_key = lax.dot_general(d_scores, q2, tn, preferred_element_type=jnp.float32)
        d_key = d_key + pltpu.roll(d_key, 64, 1)
        d_value = d_value + pltpu.roll(d_value, 64, 1)
        if head % 2 == 0:
            keep_k, keep_v = d_key, d_value
        else:
            dkv_scr[:, slab] = turn(jnp.where(low, keep_k, d_key), cosine, signed).astype(
                jnp.bfloat16
            )
            dkv_scr[:, half + slab.start : half + slab.stop] = jnp.where(
                low, keep_v, d_value
            ).astype(jnp.bfloat16)
    for kind, source in ((0, dq_scr), (1, dkv_scr)):
        for z in range(4):
            grad[kind, z] = (
                lax.dot_general(
                    normed_ref[:, 256 * z : 256 * z + 256],
                    source[...],
                    tn,
                    preferred_element_type=jnp.float32,
                )
                .astype(jnp.bfloat16)
                .reshape(8, 32, D)
            )
        for copy in weight_copies(grads_a, grads_b, grad, out_sems, owner, kind, True):
            copy.start()
    for kind in range(2):
        for copy in weight_copies(pieces_a, pieces_b, whole, sems, owner, kind, False):
            copy.wait()
    d_normed = lax.dot_general(
        dq_scr[...], whole[0].reshape(D, D), nt, preferred_element_type=jnp.float32
    ) + lax.dot_general(
        dkv_scr[...], whole[1].reshape(D, D), nt, preferred_element_type=jnp.float32
    )
    inputs, inverse = x_ref[...].astype(jnp.float32), small_ref[:128, 8:9]
    gains_ref[0:1, :] = jnp.sum(d_normed * inputs * inverse, axis=0, keepdims=True)
    weighted = d_normed * gain1_ref[...]
    input_grad_ref[...] = (
        d_hidden
        + inverse * weighted
        - inputs
        * (inverse * inverse * inverse)
        * jnp.mean(weighted * inputs, axis=1, keepdims=True)
    ).astype(jnp.bfloat16)
    for last in lasts:
        last.start()
    for kind in range(3):
        for copy in weight_copies(grads_a, grads_b, grad, out_sems, owner, kind, True):
            copy.wait()
    for last in lasts:
        last.wait()


def attention_backward(pieces_a, pieces_b, *rest):
    hbm = pl.BlockSpec(memory_space=pltpu.HBM)
    f32, b16 = jnp.float32, jnp.bfloat16
    far = pltpu.HBM((2, 4, 96, D // 2), b16)
    shapes = [((128, D), b16), ((2, D), f32), ((EXPERTS, D), f32)]
    outs = pl.pallas_call(
        attention_backward_kernel,
        in_specs=[hbm] * (8 + len(rest)),
        out_specs=[hbm] * 11,
        out_shape=[far] * 8 + [pltpu.HBM(*pair) for pair in shapes],
        scratch_shapes=[pltpu.VMEM(array.shape, array.dtype) for array in rest]
        + [pltpu.VMEM(*pair) for pair in shapes]
        + [
            pltpu.VMEM((3, 4, 8, 32, D), b16),
            pltpu.VMEM((3, 4, 8, 32, D), b16),
            pltpu.VMEM((128, D), b16),
            pltpu.VMEM((128, D), b16),
            pltpu.VMEM((128, D), b16),
            pltpu.SemaphoreType.DMA((3, 8, 2)),
            pltpu.SemaphoreType.DMA((3, 8, 2)),
            pltpu.SemaphoreType.DMA((len(rest),)),
            pltpu.SemaphoreType.DMA((3,)),
        ],
        compiler_params=pltpu.CompilerParams(vmem_limit_bytes=48 * 1024 * 1024),
    )(*pieces_a, *pieces_b, *rest)
    return outs[0:4], outs[4:8], outs[8], outs[9], outs[10]


def slice_kernel(*refs):
    weights, outs, buffers, sems = refs[0:2], refs[2:5], refs[5:8], refs[8]
    group = lax.axis_index(DP)
    loads, stores = [], []
    for s in range(3):
        at = jnp.bitwise_xor(group, s + 1)
        for i, rows in enumerate((pl.ds(0, 256), pl.ds(256, 128))):
            loads.append(
                pltpu.make_async_copy(weights[i].at[at], buffers[s].at[rows, :], sems.at[i, s])
            )
        stores.append(pltpu.make_async_copy(buffers[s], outs[s], sems.at[2, s]))
    for load in loads:
        load.start()
    for s in range(3):
        loads[2 * s].wait()
        loads[2 * s + 1].wait()
        stores[s].start()
    for store in stores:
        store.wait()


def sliced(up, down):
    hbm = pl.BlockSpec(memory_space=pltpu.HBM)
    return pl.pallas_call(
        slice_kernel,
        in_specs=[hbm] * 2,
        out_specs=[hbm] * 3,
        out_shape=[pltpu.HBM((384, D), up.dtype)] * 3,
        scratch_shapes=[pltpu.VMEM((384, D), up.dtype)] * 3 + [pltpu.SemaphoreType.DMA((3, 3))],
    )(up, down)


def finish_experts_kernel(*refs):
    pieces, up_out, down_out = refs[0:4], refs[4], refs[5]
    for s in range(4):
        at = jnp.bitwise_xor(lax.axis_index(DP), s)
        up_out[at] = pieces[s][0:256, :].astype(jnp.float32)
        down_out[at] = pieces[s][256:384, :].astype(jnp.float32)


def finish_experts(pieces):
    vmem = pl.BlockSpec(memory_space=pltpu.VMEM)
    return pl.pallas_call(
        finish_experts_kernel,
        in_specs=[vmem] * 4,
        out_specs=[vmem] * 2,
        out_shape=[
            jax.ShapeDtypeStruct((4, 256, 2 * F), jnp.float32),
            jax.ShapeDtypeStruct((4, 128, D), jnp.float32),
        ],
    )(*pieces)


def finish_weights_kernel(*refs):
    pieces_a, pieces_b, outs, router_out = refs[0:4], refs[4:8], refs[8:11], refs[11]
    half = D // 2
    owner = lax.axis_index(EX)
    for rel in range(8):
        c, x, y = rel & 1, (rel >> 1) & 1, (rel >> 2) & 1
        at = jnp.bitwise_xor(owner, rel)
        rows = pl.ds(pl.multiple_of(at * 32, 32), 32)
        for i, piece in enumerate((pieces_a[2 * c + y].at[x], pieces_b[2 * c + x].at[y])):
            cols = pl.ds(half * i, half)
            for kind in range(3):
                outs[kind][rows, cols] = piece[32 * kind : 32 * kind + 32, :].astype(jnp.float32)
            router_out[at, :, cols] = piece[96:97, :].astype(jnp.float32)


def finish_weights(pieces_a, pieces_b):
    vmem = pl.BlockSpec(memory_space=pltpu.VMEM)
    return pl.pallas_call(
        finish_weights_kernel,
        in_specs=[vmem] * 8,
        out_specs=[vmem] * 4,
        out_shape=[jax.ShapeDtypeStruct((256, D), jnp.float32)] * 3
        + [jax.ShapeDtypeStruct((8, 1, D), jnp.float32)],
    )(*pieces_a, *pieces_b)


CORE, ACROSS, ALONG = 1, 2, 4


def swap(array, bit):
    return lax.ppermute(array, EX, [(i, i ^ bit) for i in range(8)])


def trade(array, step):
    return lax.ppermute(array, DP, [(i, i ^ step) for i in range(4)])


def everyone(array, axes):
    return lax.all_to_all(array, axes, split_axis=0, concat_axis=0, tiled=True)


def to_group(array, axes, count):
    return everyone(jnp.broadcast_to(array[None], (count,) + array.shape), axes)


def gather_halves(copies):
    column = everyone(copies, DP)
    return gather_plane(column[:, 0], column[:, 1])


def gather_traded(halves):
    traded = [halves] + [trade(halves, s) for s in range(1, 4)]
    here = lax.axis_index(DP)

    def at(place, column):
        picked = traded[3 ^ place][column]
        for z in range(2, -1, -1):
            picked = jnp.where(here == z, traded[z ^ place][column], picked)
        return picked

    a0, b0 = (jnp.stack([at(place, column) for place in range(4)]) for column in range(2))
    return gather_plane(a0, b0)


def gather_plane(a0, b0):
    a = jnp.stack([a0, swap(a0, ACROSS)])
    b = jnp.stack([b0, swap(b0, ALONG)])
    a_far, b_far = swap(a, ALONG), swap(b, ACROSS)
    pieces_a = [a, a_far, swap(a, CORE), swap(a_far, CORE)]
    pieces_b = [b, b_far, swap(b, CORE), swap(b_far, CORE)]
    return pieces_a, pieces_b


def add(one, two):
    return (one.astype(jnp.float32) + two.astype(jnp.float32)).astype(jnp.bfloat16)


def scatter_halves(pieces_a, pieces_b):
    a_far = add(pieces_a[1], swap(pieces_a[3], CORE))
    b_far = add(pieces_b[1], swap(pieces_b[3], CORE))
    a_near = add(pieces_a[0], swap(pieces_a[2], CORE))
    b_near = add(pieces_b[0], swap(pieces_b[2], CORE))
    a = add(a_near, swap(a_far, ALONG))
    b = add(b_near, swap(b_far, ACROSS))
    a_end, b_end = swap(a[1], ACROSS), swap(b[1], ALONG)
    a_own, b_own = add(a[0], a_end), add(b[0], b_end)
    return a_own, b_own


def block_inner(
    layer_input,
    segment_ids,
    expert_routes,
    first_gain,
    w_query,
    w_keyvalue,
    w_output,
    second_gain,
    w_router,
    w_gate_up,
    w_down,
    out_cotangent,
):
    half = D // 2
    owner_at = lax.axis_index(EX)

    def own_part(weight):
        return lax.dynamic_slice_in_dim(weight, owner_at * 32, 32, 0)

    def split(rows):
        return jnp.stack([rows[:, :half], rows[:, half:]])

    pack = jnp.concatenate([own_part(w_query), own_part(w_keyvalue), own_part(w_output)], axis=0)
    weights_a, weights_b = gather_halves(jnp.broadcast_to(split(pack)[None], (4, 2, 96, half)))
    routes = expert_routes.T
    small = jnp.stack(
        [routes.astype(jnp.bfloat16).reshape(D), own_part(w_router).T.reshape(32 * EXPERTS)]
    )
    small = to_group(small, (EX, DP), 32)
    all_routes = small[:, 0].astype(jnp.int32).reshape(32, TOPK, 128)
    router = small[:, 1].reshape(8, 4, EXPERTS, 32).transpose(2, 1, 0, 3)
    router = router.reshape(EXPERTS, D)

    sent = sliced(w_gate_up, w_down)

    def in_hbm(pieces):
        return [pltpu.with_memory_space_constraint(p, pltpu.HBM) for p in pieces]

    weights = [w_gate_up, w_down]
    weights += in_hbm([trade(sent[s - 1], s) for s in range(1, 4)])
    cot_a, cot_b = gather_traded(split(out_cotangent))

    weights_a, weights_b = in_hbm(weights_a), in_hbm(weights_b)
    rope = jnp.asarray(np.stack(rope_constants(128)))
    shared = (segment_ids[None, :], first_gain[None, :], second_gain[None, :], rope)
    saved = attention_forward(weights_a, weights_b, layer_input, *shared)
    packed, hidden, scalars, normed2 = saved
    tok_a, tok_b = gather_halves(normed2)

    def flat(pieces):
        return [p.reshape(1024, half) for p in pieces]

    mix_a, mix_b, back_a, back_b, d_experts, d_gate = expert_call(
        flat(tok_a),
        flat(tok_b),
        flat(cot_a),
        flat(cot_b),
        weights,
        all_routes,
        router,
    )

    def deep(pieces):
        return [p.reshape(2, 4, 128, half) for p in pieces]

    back = everyone(jnp.stack(scatter_halves(deep(back_a), deep(back_b)), axis=1), DP)
    d_gates = everyone(d_gate, (EX, DP)).reshape(EXPERTS, 128)
    grads_a, grads_b, input_grad, d_gains, d_router = attention_backward(
        weights_a,
        weights_b,
        layer_input,
        *shared,
        packed,
        hidden,
        scalars,
        out_cotangent,
        back,
        d_gates,
        routes,
        router,
    )
    arrived = [d_experts[0]] + [trade(d_experts[s], s) for s in range(1, 4)]
    gate_up_grad, down_grad = finish_experts(arrived)
    mix_near = scatter_halves(deep(mix_a), deep(mix_b))
    group_at = lax.axis_index(DP)

    def part_for(step):
        at = jnp.bitwise_xor(group_at, step)
        pair = [lax.dynamic_index_in_dim(own, at, 0, keepdims=False) for own in mix_near]
        return jnp.stack(pair)

    mixed = part_for(0).astype(jnp.float32)
    for step in range(1, 4):
        mixed = mixed + trade(part_for(step), step).astype(jnp.float32)
    mixed = jnp.concatenate([mixed[0], mixed[1]], axis=1)
    layer_output = (hidden + residual_scale * mixed).astype(jnp.bfloat16)

    small = jnp.concatenate(
        [
            jnp.broadcast_to(d_gains.reshape(1, 2 * D), (32, 2 * D)),
            d_router.reshape(EXPERTS, 32, 32).transpose(1, 2, 0).reshape(32, D),
        ],
        axis=1,
    )
    small = jnp.sum(everyone(small, (DP, EX)), axis=0)
    first_gain_grad, second_gain_grad = small[:D], small[D : 2 * D]

    summed = jnp.stack(scatter_halves(grads_a, grads_b), axis=1)
    summed = everyone(summed, DP)
    summed = jnp.sum(summed.astype(jnp.float32), axis=0)
    summed = jnp.concatenate([summed, small[2 * D :].reshape(2, 1, half)], axis=1)
    summed = summed.astype(jnp.bfloat16)
    whole_a, whole_b = gather_plane(summed[0], summed[1])
    query_grad, keyvalue_grad, output_grad, router_grad = finish_weights(whole_a, whole_b)
    router_grad = router_grad.reshape(256, EXPERTS)
    return (
        layer_output,
        input_grad,
        first_gain_grad,
        query_grad,
        keyvalue_grad,
        output_grad,
        second_gain_grad,
        router_grad,
        gate_up_grad,
        down_grad,
    )


def block_device(*args):
    return block_inner(*args)


def solution(mesh):
    sizes = (mesh.shape[DP], mesh.shape[EX])
    return jax.shard_map(
        block_device if sizes == (4, 8) else general_device,
        mesh=mesh,
        in_specs=(
            P((DP, EX), None),
            P((DP, EX)),
            P((DP, EX), None),
            P(),
            P(DP, None),
            P(DP, None),
            P(DP, None),
            P(),
            P(DP, None),
            P(EX, DP, None),
            P(EX, DP, None),
            P((DP, EX), None),
        ),
        out_specs=(
            P((DP, EX), None),
            P((DP, EX), None),
            P(),
            P(DP, None),
            P(DP, None),
            P(DP, None),
            P(),
            P(DP, None),
            P(EX, DP, None),
            P(EX, DP, None),
        ),
        check_vma=False,
    )
```
